32 devices in a mesh: dp: 4 (over z), fsdp: 8 (over y, x, core).
Axes of the slice: x: 2, y: 2, z: 4, core: 2. Of those that a mesh axis runs over, the one named last changes fastest.
Arguments:
- hidden: bfloat16 [16384, 2048], P(('dp', 'fsdp')), may hold values from -6 to 6
- out_cotangent: bfloat16 [16384, 2048], P(('dp', 'fsdp')), may hold values from -6 to 6
- norm_gain: bfloat16 [2048], P(('dp', 'fsdp')), may hold values from 0.5 to 1.5
- in_weight: bfloat16 [2048, 8512], P(('dp', 'fsdp')), may hold values from -0.125 to 0.125
- conv_weight: bfloat16 [4352, 4], P('fsdp'), may hold values from -3 to 3
- conv_bias: bfloat16 [4352], P('fsdp'), may hold values from -1.796875 to 1.796875
- step_bias: bfloat16 [64], P('fsdp'), may hold values from -4 to -2
- decay_log: bfloat16 [64], P('fsdp'), may hold values from -7 to 0
- skip_gain: bfloat16 [64], P('fsdp'), may hold values from 0.5 to 1.5
- gate_gain: bfloat16 [4096], P(('dp', 'fsdp')), may hold values from 0.5 to 1.5
- out_weight: bfloat16 [4096, 2048], P(('dp', 'fsdp')), may hold values from -0.09375 to 0.09375
- stretch_len: int32 [64], P(('dp', 'fsdp')), may hold values from 0 to 256, as said below
- stretch_start: int32 [64], P(('dp', 'fsdp')), may hold values from 0 to 1, as said below
Outputs:
- block_out: bfloat16 [16384, 2048], P(('dp', 'fsdp'))
- hidden_grad: float32 [16384, 2048], P(('dp', 'fsdp'))
- norm_gain_grad: float32 [2048], P(('dp', 'fsdp'))
- in_weight_grad: float32 [2048, 8512], P(('dp', 'fsdp'))
- conv_weight_grad: float32 [4352, 4], P('fsdp')
- conv_bias_grad: float32 [4352], P('fsdp')
- step_bias_grad: float32 [64], P('fsdp')
- decay_log_grad: float32 [64], P('fsdp')
- skip_gain_grad: float32 [64], P('fsdp')
- gate_gain_grad: float32 [4096], P(('dp', 'fsdp'))
- out_weight_grad: float32 [4096, 2048], P(('dp', 'fsdp'))
The draws below stay inside these ranges and needn't reach their ends.
Inputs may be any that keep to these rules, and one draw needn't show every extreme that they name: `stretch_len`: the stretches fall into aligned groups of 16; in each group one sample begins in the group's first stretch or the one after and ends in the group's last 2 stretches, before the group's last stretch; a sample's stretches are full up to one partial stretch and then empty; a sample that takes only the group's first stretch is longer than half of it. `stretch_start`: 1 at the first stretch of every aligned group of 16 stretches, and at the start of the sample that follows a one-stretch sample.
All inputs are finite; a program needn't handle non-finite values.
Results may differ from the reference program's by a relative error of at most 0.011.
Values may be sent and summed in bfloat16 or wider, within the bound.
No kernel may reach another device: no remote copies, remote signals or barrier semaphores. Data moves between devices by JAX's collectives and lax.ppermute only.
A program may use at most 448 MiB of HBM per device.

```python
import jax
import jax.numpy as jnp
from jax import lax

D = 2048
H = 64
P_SIZE = 64
N = 128
TAPS = 4
STRETCH = 256
TOK_DEV = 512
DI = 4096
CONV = 4352
XPROJ = 8512
TOKENS = 16384
LONGEST = 4096
NCHUNKS = 64


def layout(key):
    per_device = TOK_DEV // STRETCH
    group = LONGEST // STRETCH
    groups = NCHUNKS // group
    leading = jax.random.randint(jax.random.fold_in(key, 5), (groups,), 0, 2)
    lead_len = STRETCH // 2 + 1 + jax.random.randint(jax.random.fold_in(key, 6), (groups,), 0, STRETCH - STRETCH // 2)
    lowest = (group - per_device - leading) * STRETCH + 1
    highest = (group - 1 - leading) * STRETCH
    raw_draw = jax.random.randint(jax.random.fold_in(key, 9), (groups,), 0, 1 << 20)
    span_len = lowest + raw_draw % (highest - lowest + 1)
    stretch_index = jnp.arange(group)[None, :]
    relative = stretch_index - leading[:, None]
    span_live = jnp.where(relative >= 0, jnp.clip(span_len[:, None] - relative * STRETCH, 0, STRETCH), 0)
    first_lead = (leading[:, None] == 1) & (stretch_index == 0)
    live_counts = jnp.where(first_lead, lead_len[:, None], span_live)
    starts_all = ((stretch_index == 0) | (stretch_index == leading[:, None])).astype(jnp.int32)
    return (starts_all.reshape(-1).astype(jnp.int32), live_counts.reshape(-1).astype(jnp.int32))


def draw_stretch_len(key, part):
    return layout(key)[1]


def draw_stretch_start(key, part):
    return layout(key)[0]


def levels(rng, dims, cuts, smallest, largest):
    def one(axis_at, shards_of):
        heights = jax.random.uniform(jax.random.fold_in(jax.random.fold_in(rng, 6), axis_at), (shards_of,), jnp.float32, smallest / len(cuts), largest / len(cuts))
        return jnp.repeat(jnp.exp(heights), dims[axis_at] // shards_of).reshape((-1,) + (1,) * (len(dims) - axis_at - 1))

    level = one(*cuts[0])
    for cut in cuts[1:]:
        level = level * one(*cut)
    return level


def noise(key, shape, width, limit, cuts=(), dtype=jnp.bfloat16):
    entries = width * jax.random.normal(key, shape, jnp.float32)
    if cuts:
        entries = entries * levels(key, shape, cuts, -0.22, 0.18)
    return jnp.clip(entries, -limit, limit).astype(dtype)


def setup_inputs(seed: int = 0) -> dict:
    seeds = jax.random.split(jax.random.key(seed), 14)
    return {
        "hidden": noise(seeds[0], (TOKENS, D), 1.0, 6.0, ((0, 32),)),
        "out_cotangent": noise(seeds[1], (TOKENS, D), 1.0, 6.0, ((0, 32),)),
        "norm_gain": jnp.clip(1.0 + 0.1 * jax.random.normal(seeds[2], (D,), jnp.float32), 0.5, 1.5).astype(jnp.bfloat16),
        "in_weight": noise(seeds[3], (D, XPROJ), D ** -0.5, 0.125, ((0, 32),)),
        "conv_weight": noise(seeds[4], (CONV, TAPS), TAPS ** -0.5, 3.0, ((0, 8),)),
        "conv_bias": noise(seeds[5], (CONV,), 0.3, 1.796875, ((0, 8),)),
        "step_bias": jnp.clip(-4.0 + 2.0 * jax.random.uniform(seeds[6], (H,), jnp.float32) ** levels(seeds[6], (H,), ((0, 8),), -0.2, 0.2), -4.0, -2.0).astype(jnp.bfloat16),
        "decay_log": jnp.clip(-7.0 + 7.0 * jax.random.uniform(seeds[7], (H,), jnp.float32) ** levels(seeds[7], (H,), ((0, 8),), -0.2, 0.2), -7.0, 0.0).astype(jnp.bfloat16),
        "skip_gain": jnp.clip(0.5 + 1.0 * jax.random.uniform(seeds[8], (H,), jnp.float32) ** levels(seeds[8], (H,), ((0, 8),), -0.2, 0.2), 0.5, 1.5).astype(jnp.bfloat16),
        "gate_gain": jnp.clip(1.0 + 0.1 * jax.random.normal(seeds[9], (DI,), jnp.float32), 0.5, 1.5).astype(jnp.bfloat16),
        "out_weight": noise(seeds[10], (DI, D), DI ** -0.5, 0.09375, ((0, 32),)),
        "stretch_len": draw_stretch_len(jax.random.fold_in(seeds[13], 71), 0),
        "stretch_start": draw_stretch_start(jax.random.fold_in(seeds[13], 71), 0),
    }


PRECISE = lax.Precision.HIGHEST
EPSILON = 1e-05

@jax.custom_vjp
def low(v):
    return lax.optimization_barrier(v.astype(jnp.bfloat16)).astype(jnp.float32)

@jax.custom_vjp
def low_back(v):
    return v

def low_keep(v):
    return (low(v), None)

def low_pass(kept, grad):
    return (grad,)

def back_keep(v):
    return (v, None)

def back_low(kept, grad):
    return (low(grad),)
low.defvjp(low_keep, low_pass)
low_back.defvjp(back_keep, back_low)

def rms_scale(values):
    return lax.rsqrt(lax.optimization_barrier(jnp.mean(values * values, axis=-1, keepdims=True)) + EPSILON)

def gated_norm(mixed, gate_part):
    gated = mixed * jax.nn.silu(gate_part)
    return gated * rms_scale(gated)

def convolve(conv_input, edge_rows, weights, conv_bias, row_start, offset):
    row_count = conv_input.shape[0]
    extended = jnp.concatenate([edge_rows, conv_input], axis=0)
    accumulated = conv_bias[None, :] + conv_input * weights[None, :, TAPS - 1]
    for lag_rows in range(1, TAPS):
        keep_mask = 1.0 - row_start * (offset < lag_rows)
        lower = TAPS - 1 - lag_rows
        accumulated = accumulated + extended[lower:lower + row_count] * keep_mask[:, None] * weights[None, :, lower]
    return jax.nn.silu(accumulated)

def stretch_terms(values, written, readout, step_size, rates):
    steps = values.shape[0]
    log_decay = jnp.cumsum(step_size * rates[None, :], axis=0)
    scores = jnp.dot(readout, written.T, precision=PRECISE)
    later_mask = (jnp.arange(steps)[:, None] >= jnp.arange(steps)[None, :])[None]
    log_gap = log_decay.T[:, :, None] - log_decay.T[:, None, :]
    decay_map = jnp.where(later_mask, jnp.exp(jnp.where(later_mask, log_gap, 0.0)), 0.0)
    mixing = decay_map * scores[None] * step_size.T[:, None, :]
    inner_out = jnp.einsum('hts,shp->thp', mixing, values, precision=PRECISE)
    tail_weight = jnp.exp(log_decay[-1][None, :] - log_decay) * step_size
    local_state = jnp.einsum('shp,sn->hpn', values * tail_weight[:, :, None], written, precision=PRECISE)
    return (inner_out, log_decay, local_state)

def ssd_scan(values, written, readout, step_size, rates, skip_gain, starts):
    nchunk = starts.shape[0]

    def advance(end_state, pieces):
        stretch_values, stretch_written, stretch_readout, stretch_steps, opening = pieces
        end_state = end_state * (1.0 - opening)
        inner_out, log_decay, local_state = stretch_terms(stretch_values, stretch_written, stretch_readout, stretch_steps, rates)
        carried = jnp.einsum('tn,hpn->thp', stretch_readout, end_state, precision=PRECISE)
        stretch_out = inner_out + jnp.exp(log_decay)[:, :, None] * carried + skip_gain[None, :, None] * stretch_values
        end_state = jnp.exp(log_decay[-1])[:, None, None] * end_state + local_state
        return (end_state, stretch_out)
    initial = jnp.zeros((H, P_SIZE, N), jnp.float32)
    pieces = (values.reshape(nchunk, STRETCH, H, P_SIZE), written.reshape(nchunk, STRETCH, N), readout.reshape(nchunk, STRETCH, N), step_size.reshape(nchunk, STRETCH, H), starts)
    _, outputs = lax.scan(jax.checkpoint(advance), initial, pieces)
    return outputs.reshape(-1, H, P_SIZE)

def block_forward(params, rows_in, starts, lengths):
    norm_gain, in_weight, conv_weight, conv_bias, step_bias, decay_log, skip_gain, gate_gain, out_weight = params
    row_count = rows_in.shape[0]
    offset = jnp.arange(row_count) % STRETCH
    row_start = jnp.repeat(starts, STRETCH)
    live_rows = (offset < jnp.repeat(lengths, STRETCH)).astype(jnp.float32)
    unit_rows = rows_in * rms_scale(rows_in)
    inputs = low(unit_rows * norm_gain[None, :])
    projected = low_back(jnp.dot(inputs, in_weight, precision=PRECISE))
    gate_part = projected[:, :DI]
    conv_input = projected[:, DI:DI + CONV]
    step_raw = projected[:, DI + CONV:]
    activated = convolve(conv_input, jnp.zeros((TAPS - 1, CONV), jnp.float32), conv_weight, conv_bias, row_start, offset)
    values = activated[:, :DI].reshape(row_count, H, P_SIZE)
    written = activated[:, DI:DI + N]
    readout = activated[:, DI + N:]
    step_size = jax.nn.softplus(step_raw + step_bias[None, :])
    rates = -jnp.exp(decay_log)
    mixed = ssd_scan(values, written, readout, step_size, rates, skip_gain, starts).reshape(row_count, DI)
    normed = gated_norm(mixed, gate_part)
    gated_low = low(normed * gate_gain[None, :])
    branch = jnp.dot(gated_low, out_weight, precision=PRECISE)
    return rows_in + live_rows[:, None] * branch

def reference(hidden, out_cotangent, norm_gain, in_weight, conv_weight, conv_bias, step_bias, decay_log, skip_gain, gate_gain, out_weight, stretch_len, stretch_start):
    params = tuple((p.astype(jnp.float32) for p in (norm_gain, in_weight, conv_weight, conv_bias, step_bias, decay_log, skip_gain, gate_gain, out_weight)))
    blocks = TOKENS // LONGEST
    per_block = LONGEST // STRETCH
    pieces = (hidden.astype(jnp.float32).reshape(blocks, LONGEST, D), out_cotangent.astype(jnp.float32).reshape(blocks, LONGEST, D), stretch_start.astype(jnp.float32).reshape(blocks, per_block), stretch_len.reshape(blocks, per_block))

    def visit(running, piece):
        rows_in, cotangent, starts, lengths = piece

        def forward(p_all, rows_all):
            return block_forward(p_all, rows_all, starts, lengths)
        result, pull = jax.vjp(forward, params, rows_in)
        param_grads, row_grads = pull(cotangent)
        running = jax.tree.map(lambda left, right: left + right, running, param_grads)
        return (running, (result.astype(jnp.bfloat16), row_grads))
    zeros_all = jax.tree.map(jnp.zeros_like, params)
    summed, (results, row_grads) = lax.scan(visit, zeros_all, pieces)
    return (results.reshape(TOKENS, D), row_grads.reshape(TOKENS, D), summed[0], summed[1], summed[2], summed[3], summed[4], summed[5], summed[6], summed[7], summed[8])
```

```python
import functools
import math

import jax
import jax.numpy as jnp
import numpy as np
from jax import lax
from jax.experimental import pallas as pl
from jax.experimental.pallas import tpu as pltpu
from jax.sharding import PartitionSpec as P

H = 64
P_SIZE = 64
N = 128
TAPS = 4
STRETCH = 256
DI = 4096
CONV = 4352
LANES = 128
HALO = 8

EPSILON = 1e-05
BF = jnp.bfloat16
F32 = jnp.float32
VMEM_BYTES = 58 * 1024 * 1024
NEGATIVE = -1e30
PACK = 32
ROWS = 32
HALF = 128


def mm(a, b):
    return lax.dot_general(a, b, (((1,), (0,)), ((), ())), preferred_element_type=F32)


def mm_nt(a, b):
    return lax.dot_general(a, b, (((1,), (1,)), ((), ())), preferred_element_type=F32)


def mm_tn(a, b):
    return lax.dot_general(a, b, (((0,), (0,)), ((), ())), preferred_element_type=F32)


def mm_exact(a, b):
    return lax.dot_general(
        a, b, (((1,), (0,)), ((), ())), precision=lax.Precision.HIGHEST, preferred_element_type=F32
    )


def mm_nt_exact(a, b):
    return lax.dot_general(
        a, b, (((1,), (1,)), ((), ())), precision=lax.Precision.HIGHEST, preferred_element_type=F32
    )


def sigmoid(v):
    return 1.0 / (1.0 + jnp.exp(-v))


def softplus(v):
    return jnp.maximum(v, 0.0) + jnp.log1p(jnp.exp(-jnp.abs(v)))


def half_mask(rows):
    return lax.broadcasted_iota(jnp.int32, (rows, LANES), 1) < P_SIZE


def convolved(ext, taps):
    out = taps[TAPS : TAPS + 1, :]
    for j in range(TAPS):
        low = HALO - (TAPS - 1) + j
        out = out + ext[low : low + STRETCH, :] * taps[j : j + 1, :]
    return out


def three_parts(table, heads_here):
    lane = lax.broadcasted_iota(jnp.int32, table.shape, 1)
    table = jnp.where(lane < heads_here, table, 0.0)
    high = table.astype(BF).astype(F32)
    rest = table - high
    middle = rest.astype(BF).astype(F32)
    low = rest - middle
    packed = high + pltpu.roll(middle, PACK, 1) + pltpu.roll(low, 2 * PACK, 1)
    return packed.astype(BF)


def spreader(heads_here, width):
    source = np.arange(LANES)
    head = np.where(source < 3 * PACK, source % PACK, heads_here)
    return jnp.asarray(head[:, None] == np.arange(heads_here * width)[None, :] // width, BF)


def split_sum(ones, table, heads_here):
    lane = lax.broadcasted_iota(jnp.int32, table.shape, 1)
    got = mm(ones.astype(F32).astype(BF), three_parts(table, heads_here))
    got = got + pltpu.roll(got, LANES - PACK, 1) + pltpu.roll(got, LANES - 2 * PACK, 1)
    return jnp.where(lane < heads_here, got, 0.0)


def lower_ones():
    rows = lax.broadcasted_iota(jnp.int32, (STRETCH, STRETCH), 0)
    cols = lax.broadcasted_iota(jnp.int32, (STRETCH, STRETCH), 1)
    return rows, cols


def forward_kernel(
    starts, hid, gain, w1, taps, heads, skip, to_pairs, to_lanes, u_out, xin_out, dtp_out, mixed_out, sin_out, state, ext,
    scores, mixing, columns, steps,
):
    c = pl.program_id(0)
    fresh = starts[c] > 0
    lanes_v = skip.shape[1]
    lanes_x = taps.shape[1]
    rows_in = hid[...]
    wide = rows_in.astype(F32)
    square = jnp.sum(wide * wide, axis=1, keepdims=True)
    rs = lax.rsqrt(square / rows_in.shape[1] + EPSILON)
    u = (wide * rs * gain[...]).astype(BF)
    u_out[...] = u
    projected = mm(u, w1[...])
    conv_input = projected[:, :lanes_x]
    dtp = projected[:, lanes_x:] + heads[0:1, :]
    xin_out[...] = conv_input
    dtp_out[...] = dtp
    halo = ext[pl.ds(STRETCH, HALO), :]
    ext[pl.ds(0, HALO), :] = jnp.where(fresh, 0.0, halo)
    ext[pl.ds(HALO, STRETCH), :] = conv_input
    pre = convolved(ext, taps)
    act = pre * sigmoid(pre)
    values = act[:, :lanes_v]
    written = act[:, lanes_v : lanes_v + N].astype(BF)
    readout = act[:, lanes_v + N :].astype(BF)
    step = softplus(dtp)
    rows, cols = lower_ones()
    causal = rows >= cols
    decay = split_sum(causal, step * heads[1:2, :], lanes_v // P_SIZE)
    decay_t = decay.T
    before = jnp.where(fresh, 0.0, state[...])
    sin_out[0] = before
    scores[...] = mm_nt(readout, written)
    columns[...] = mm(three_parts(decay, lanes_v // P_SIZE), to_lanes[...])
    steps[...] = mm(three_parts(step, lanes_v // P_SIZE), to_pairs[...])
    carried = mm(readout, before.astype(BF))
    written_t = act[:, lanes_v : lanes_v + N].T.astype(BF)
    left = half_mask(STRETCH)
    for pair in range(lanes_v // LANES):
        lo = pair * LANES
        v = values[:, lo : lo + LANES]
        step_pair = steps[:, lo : lo + LANES]
        decay_pair = jnp.where(
            left, columns[:, 2 * lo : 2 * lo + LANES], columns[:, 2 * lo + LANES : 2 * (lo + LANES)]
        )
        last_pair = decay_pair[STRETCH - 1 :, :]
        sv_wide = v * step_pair
        sv = sv_wide.astype(BF)
        out = jnp.exp(decay_pair) * carried[:, lo : lo + LANES] + skip[:, lo : lo + LANES] * v
        top, bottom = out[:HALF], out[HALF:]
        for j in range(2):
            h = 2 * pair + j
            for r in range(0, STRETCH, ROWS):
                column = columns[r : r + ROWS, h * HALF : (h + 1) * HALF]
                for t in range(0, HALF if r < HALF else STRETCH, HALF):
                    gap = column - decay_t[h : h + 1, t : t + HALF]
                    if t + HALF > r:
                        gap = jnp.where(block_mask(r, t), gap, NEGATIVE)
                    block = scores[r : r + ROWS, t : t + HALF] * jnp.exp(gap)
                    mixing[j, r : r + ROWS, t : t + HALF] = block.astype(BF)
            mine = left if j == 0 else jnp.logical_not(left)
            sv_mine = jnp.where(mine, sv, jnp.zeros_like(sv))
            top = top + mm(mixing[j, :HALF, :HALF], sv_mine[:HALF])
            bottom = bottom + mm(mixing[j, HALF:, :], sv_mine)
        mixed_out[:HALF, lo : lo + LANES] = top
        mixed_out[HALF:, lo : lo + LANES] = bottom
        tv = (sv_wide * jnp.exp(last_pair - decay_pair)).astype(BF)
        state[:, lo : lo + LANES] = jnp.exp(last_pair) * before[:, lo : lo + LANES] + mm(
            written_t, tv
        )


def block_mask(r, t):
    rows = lax.broadcasted_iota(jnp.int32, (ROWS, HALF), 0) + r
    cols = lax.broadcasted_iota(jnp.int32, (ROWS, HALF), 1) + t
    return rows >= cols


def block_mask_t(r, t):
    rows = lax.broadcasted_iota(jnp.int32, (ROWS, HALF), 0) + r
    cols = lax.broadcasted_iota(jnp.int32, (ROWS, HALF), 1) + t
    return rows <= cols


def column_rows(column):
    wide = jnp.broadcast_to(column, (STRETCH, LANES))
    return wide.T[0:8, :]


def gate_kernel(u, wg, ow, mixed, gain, branch_out, gate_out, squares_out):
    gate = mm(u[...], wg[...])
    gate_out[...] = gate
    gated = mixed[...] * gate * sigmoid(gate)
    branch_out[...] = mm((gated * gain[...]).astype(BF), ow[...]).astype(BF)
    squares_out[...] = column_rows(jnp.sum(gated * gated, axis=1, keepdims=True))


def pull_kernel(lengths, cot, ow, gate, mixed, gain, gg_out, along_out):
    c = pl.program_id(0)
    alive = lax.broadcasted_iota(jnp.int32, (STRETCH, 1), 0) < lengths[c]
    cotangent = cot[...]
    cotangent = jnp.where(alive, cotangent, jnp.zeros_like(cotangent))
    gg = mm_nt(cotangent, ow[...])
    gg_out[...] = gg
    gated = mixed[...] * gate[...] * sigmoid(gate[...])
    along_out[...] = column_rows(jnp.sum(gg * gain[...] * gated, axis=1, keepdims=True))


def gate_back_kernel(
    outer,
    lengths,
    hid,
    cot,
    gate,
    gg,
    mixed,
    stats,
    gain,
    dmix_out,
    dgate_out,
    ggg_out,
    *rest,
):
    c = pl.program_id(0)
    outs, (owg, iwg) = rest[:-2], rest[-2:]
    count = pl.num_programs(0)
    iwg_outs = outs[:outer]
    owg_outs = outs[outer:]
    r = stats[:, 0:1]
    m = stats[:, 1:2]
    v = gate[...]
    s = sigmoid(v)
    silu = v * s
    mix = mixed[...]
    normed = mix * silu * r
    back = gg[...]
    dgated = r * (back * gain[...] - normed * m)
    dmix_out[...] = dgated * silu
    dgate = dgated * mix * (s * (1.0 + v * (1.0 - s)))
    dgate_low = dgate.astype(BF)
    dgate_out[...] = dgate_low
    alive = lax.broadcasted_iota(jnp.int32, (STRETCH, 1), 0) < lengths[c]
    cotangent = cot[...]
    cotangent = jnp.where(alive, cotangent, jnp.zeros_like(cotangent))
    owg_part = mm_tn((normed * gain[...]).astype(BF), cotangent)
    iwg_part = mm_tn(hid[...], dgate_low)
    ggg_part = jnp.sum(back * normed, axis=0, keepdims=True)

    @pl.when(c == 0)
    def _():
        owg[...] = owg_part
        iwg[...] = iwg_part
        ggg_out[...] = ggg_part

    @pl.when(c > 0)
    def _():
        owg[...] += owg_part
        iwg[...] += iwg_part
        ggg_out[...] += ggg_part

    @pl.when(c == pl.num_programs(0) - 1)
    def _():
        for whole, parts in ((owg, owg_outs), (iwg, iwg_outs)):
            rows = whole.shape[0] // len(parts)
            for k, out in enumerate(parts):
                at = lax.rem(lengths[count] + k, len(parts)) * rows
                out[...] = whole[pl.ds(pl.multiple_of(at, 16), rows), :].astype(BF)


def backward_kernel(
    starts,
    xin,
    xprev,
    dtp_in,
    dmix,
    dgate,
    sin,
    w1,
    wg,
    taps,
    heads,
    skip,
    to_pairs,
    to_lanes,
    f_out,
    gpv_out,
    gps_out,
    conv_out,
    head_out,
    skip_out,
    dstate,
    ext,
    gext,
    gbuf,
    scores,
    dscores,
    dmixing,
    mixing,
    row_sums,
    col_sums,
    columns,
    steps,
):
    step_id = pl.program_id(0)
    count = pl.num_programs(0)
    c = count - 1 - step_id
    fresh = starts[c] > 0
    lanes_v = skip.shape[1]
    lanes_x = taps.shape[1]
    first = step_id == 0
    next_fresh = jnp.logical_or(first, starts[jnp.minimum(c + 1, count - 1)] > 0)

    ext[pl.ds(0, HALO), :] = jnp.where(fresh, 0.0, xprev[...])
    ext[pl.ds(HALO, STRETCH), :] = xin[...]
    pre = convolved(ext, taps)
    sig = sigmoid(pre)
    act = pre * sig
    values = act[:, :lanes_v]
    written_f = act[:, lanes_v : lanes_v + N]
    readout_f = act[:, lanes_v + N :]
    written = written_f.astype(BF)
    readout = readout_f.astype(BF)
    dtp = dtp_in[...]
    step = softplus(dtp)
    rate = heads[1:2, :]
    rows, cols = lower_ones()
    causal = rows >= cols
    anti = rows <= cols
    decay = split_sum(causal, step * rate, lanes_v // P_SIZE)
    decay_t = decay.T
    last = decay[STRETCH - 1 : STRETCH, :]
    grow_last = jnp.exp(last)
    before = sin[0]
    before_low = before.astype(BF)
    after = jnp.where(next_fresh, 0.0, dstate[...])
    after_low = after.astype(BF)
    scores[...] = mm_nt(written, readout)
    columns[...] = mm(three_parts(decay, lanes_v // P_SIZE), to_lanes[...])
    steps[...] = mm(three_parts(step, lanes_v // P_SIZE), to_pairs[...])
    carried = mm(readout, before_low)
    spread = mm(written, after_low)
    readout_t = readout_f.T.astype(BF)
    left = half_mask(STRETCH)
    left_row = half_mask(1)
    lane = lax.broadcasted_iota(jnp.int32, (STRETCH, LANES), 1)
    lane_row = lax.broadcasted_iota(jnp.int32, (1, LANES), 1)
    row_sums[...] = jnp.zeros_like(row_sums)
    lane_rows = lax.broadcasted_iota(jnp.int32, (ROWS, LANES), 1)
    within = jnp.zeros((STRETCH, LANES), F32)
    inner = jnp.zeros((STRETCH, LANES), F32)
    direct = jnp.zeros((STRETCH, LANES), F32)
    through = jnp.zeros((1, LANES), F32)
    dwritten = jnp.zeros((STRETCH, N), F32)
    dreadout = jnp.zeros((STRETCH, N), F32)
    for pair in range(lanes_v // LANES):
        lo = pair * LANES
        v = values[:, lo : lo + LANES]
        dy = dmix[:, lo : lo + LANES]
        step_pair = steps[:, lo : lo + LANES]
        decay_pair = jnp.where(
            left, columns[:, 2 * lo : 2 * lo + LANES], columns[:, 2 * lo + LANES : 2 * (lo + LANES)]
        )
        last_pair = decay_pair[STRETCH - 1 :, :]
        fall_pair = jnp.exp(last_pair - decay_pair)
        sv = v * step_pair
        sv_low = sv.astype(BF)
        dy_low = dy.astype(BF)
        q = fall_pair * spread[:, lo : lo + LANES]
        flow = sv * q
        grown = dy * jnp.exp(decay_pair)
        enter = grown * carried[:, lo : lo + LANES]
        top, bottom = q[:HALF], q[HALF:]
        for j in range(2):
            h = 2 * pair + j
            mine = left if j == 0 else jnp.logical_not(left)
            low_mine = jnp.where(mine, dy_low, jnp.zeros_like(dy_low))
            dmixing[j, :HALF, :] = mm_nt(sv_low[:HALF], low_mine)
            dmixing[j, HALF:, HALF:] = mm_nt(sv_low[HALF:], low_mine[HALF:])
            sums = [jnp.zeros((8, HALF), F32), jnp.zeros((8, HALF), F32)]
            for r in range(0, STRETCH, ROWS):
                column = columns[r : r + ROWS, h * HALF : (h + 1) * HALF]
                across = jnp.zeros((ROWS, HALF), F32)
                for t in range(0 if r < HALF else HALF, STRETCH, HALF):
                    gap = decay_t[h : h + 1, t : t + HALF] - column
                    if t < r + ROWS:
                        gap = jnp.where(block_mask_t(r, t), gap, NEGATIVE)
                    kernel = jnp.exp(gap)
                    block = scores[r : r + ROWS, t : t + HALF] * kernel
                    back = dmixing[j, r : r + ROWS, t : t + HALF]
                    mixing[j, r : r + ROWS, t : t + HALF] = block.astype(BF)
                    turned = kernel * back
                    if h:
                        turned = turned + dscores[r : r + ROWS, t : t + HALF]
                    dscores[r : r + ROWS, t : t + HALF] = turned
                    edges = block * back
                    across = across + edges
                    for k in range(0, ROWS, 8):
                        sums[t // HALF] = sums[t // HALF] + edges[k : k + 8]
                total = jnp.sum(across, axis=1, keepdims=True)
                old = col_sums[r : r + ROWS, :] if h else jnp.zeros((ROWS, LANES), F32)
                col_sums[r : r + ROWS, :] = jnp.where(lane_rows == h, total, old)
            row_sums[h : h + 1, :HALF] = jnp.sum(sums[0], axis=0, keepdims=True)
            row_sums[h : h + 1, HALF:] = jnp.sum(sums[1], axis=0, keepdims=True)
            top = top + mm(mixing[j, :HALF, :], low_mine)
            bottom = bottom + mm(mixing[j, HALF:, HALF:], low_mine[HALF:])
            zero = jnp.zeros_like(flow)
            within = jnp.where(
                lane == h, jnp.sum(jnp.where(mine, flow, zero), axis=1, keepdims=True), within
            )
            inner = jnp.where(
                lane == h, jnp.sum(jnp.where(mine, enter, zero), axis=1, keepdims=True), inner
            )
        q = jnp.concatenate([top, bottom], axis=0)
        vq = v * q
        cross = jnp.sum(
            before[:, lo : lo + LANES] * after[:, lo : lo + LANES], axis=0, keepdims=True
        )
        for j in range(2):
            h = 2 * pair + j
            mine = left if j == 0 else jnp.logical_not(left)
            mine_row = left_row if j == 0 else jnp.logical_not(left_row)
            direct = jnp.where(
                lane == h, jnp.sum(jnp.where(mine, vq, 0.0), axis=1, keepdims=True), direct
            )
            through = jnp.where(
                lane_row == h,
                jnp.sum(jnp.where(mine_row, cross, 0.0), axis=1, keepdims=True),
                through,
            )
        gbuf[:, lo : lo + LANES] = step_pair * q + skip[:, lo : lo + LANES] * dy
        skip_part = jnp.sum(dy * v, axis=0, keepdims=True)
        skip_out[0:1, lo : lo + LANES] = skip_part + jnp.where(
            first, 0.0, skip_out[0:1, lo : lo + LANES]
        )
        tv = (sv * fall_pair).astype(BF)
        grown_low = grown.astype(BF)
        dwritten = dwritten + mm_nt(tv, after_low[:, lo : lo + LANES])
        dreadout = dreadout + mm_nt_exact(grown, before[:, lo : lo + LANES])
        dstate[:, lo : lo + LANES] = jnp.exp(last_pair) * after[
            :, lo : lo + LANES
        ] + mm(readout_t, grown_low)
    low_top = dscores[:HALF, :].astype(BF)
    low_bottom = dscores[HALF:, HALF:].astype(BF)
    gbuf[:HALF, lanes_v : lanes_v + N] = dwritten[:HALF] + mm(low_top, readout)
    gbuf[HALF:, lanes_v : lanes_v + N] = dwritten[HALF:] + mm(low_bottom, readout[HALF:])
    turned_left = dscores[:HALF, :HALF].T.astype(BF)
    turned_right = dscores[:HALF, HALF:].T.astype(BF)
    turned_low = dscores[HALF:, HALF:].T.astype(BF)
    gbuf[:HALF, lanes_v + N :] = dreadout[:HALF] + mm(turned_left, written[:HALF])
    gbuf[HALF:, lanes_v + N :] = (
        dreadout[HALF:] + mm(turned_right, written[:HALF]) + mm(turned_low, written[HALF:])
    )

    suffix = row_sums[...].T - col_sums[...] + inner
    grad_a = (
        split_sum(anti, suffix, lanes_v // P_SIZE)
        + split_sum(rows > cols, within, lanes_v // P_SIZE)
        + grow_last * through
    )
    grad_step = direct + rate * grad_a
    grad_raw = grad_step * sigmoid(dtp)
    decay_part = jnp.sum(grad_a * step, axis=0, keepdims=True) * rate
    bias_part = jnp.sum(grad_raw, axis=0, keepdims=True)
    head_row = lax.broadcasted_iota(jnp.int32, (8, LANES), 0)
    head_part = jnp.where(head_row == 0, bias_part, jnp.where(head_row == 1, decay_part, 0.0))

    grad_pre = gbuf[...] * (sig * (1.0 + pre * (1.0 - sig)))
    gext[pl.ds(STRETCH, HALO), :] = jnp.where(next_fresh, 0.0, gext[pl.ds(0, HALO), :])
    gext[pl.ds(0, STRETCH), :] = grad_pre
    grad_in = grad_pre * taps[TAPS - 1 : TAPS, :]
    for j in range(TAPS - 1):
        up = TAPS - 1 - j
        grad_in = grad_in + gext[pl.ds(up, STRETCH), :] * taps[j : j + 1, :]
    conv_row = lax.broadcasted_iota(jnp.int32, (8, lanes_x), 0)
    conv_part = jnp.where(conv_row == TAPS, jnp.sum(grad_pre, axis=0, keepdims=True), 0.0)
    for j in range(TAPS):
        low = HALO - (TAPS - 1) + j
        conv_part = jnp.where(
            conv_row == j,
            jnp.sum(grad_pre * ext[pl.ds(low, STRETCH), :], axis=0, keepdims=True),
            conv_part,
        )
    conv_out[...] = conv_part + jnp.where(first, 0.0, conv_out[...])
    head_out[...] = head_part + jnp.where(first, 0.0, head_out[...])

    grad_in_low = grad_in.astype(BF)
    grad_raw_low = grad_raw.astype(BF)
    f = mm_nt(dgate[...], wg[...])
    f = f + mm_nt(grad_in_low, w1[:, :lanes_x])
    f = f + mm_nt(grad_raw_low, w1[:, lanes_x:])
    f_out[...] = f.astype(BF)
    gpv_out[...] = grad_in_low[:, :lanes_v]
    gps_out[:, : 2 * N] = grad_in_low[:, lanes_v:]
    gps_out[:, 2 * N :] = grad_raw_low


def full(shape):
    return pl.BlockSpec(shape, lambda c, *_: (0,) * len(shape))


def tokens(width):
    return pl.BlockSpec((STRETCH, width), lambda c, *_: (c, 0))


def cost(total, depth, lanes, passes):
    return pl.CostEstimate(
        flops=int(2 * total * depth * lanes * passes), bytes_accessed=0, transcendentals=0
    )


def params(name_limit=VMEM_BYTES):
    return pltpu.CompilerParams(
        dimension_semantics=("arbitrary",), vmem_limit_bytes=name_limit
    )


def spreaders(lanes_v):
    heads_here = lanes_v // P_SIZE
    return spreader(heads_here, P_SIZE), spreader(heads_here, LANES)


def run_forward(starts, hid, gain, w1, taps, heads, skip):
    count, depth = starts.shape[0], hid.shape[1]
    lanes_v, lanes_x = skip.shape[1], taps.shape[1]
    total = hid.shape[0]
    return pl.pallas_call(
        forward_kernel,
        grid_spec=pltpu.PrefetchScalarGridSpec(
            num_scalar_prefetch=1,
            grid=(count,),
            in_specs=[
                tokens(depth),
                full(gain.shape),
                full((depth, w1.shape[1])),
                full(taps.shape),
                full(heads.shape),
                full(skip.shape),
                full((LANES, lanes_v)),
                full((LANES, 2 * lanes_v)),
            ],
            out_specs=[
                tokens(depth),
                tokens(lanes_x),
                tokens(LANES),
                tokens(lanes_v),
                pl.BlockSpec((1, N, lanes_v), lambda c, *_: (c, 0, 0)),
            ],
            scratch_shapes=[
                pltpu.VMEM((N, lanes_v), F32),
                pltpu.VMEM((STRETCH + HALO, lanes_x), F32),
                pltpu.VMEM((STRETCH, STRETCH), F32),
                pltpu.VMEM((2, STRETCH, STRETCH), BF),
                pltpu.VMEM((STRETCH, 2 * lanes_v), F32),
                pltpu.VMEM((STRETCH, lanes_v), F32),
            ],
        ),
        out_shape=[
            jax.ShapeDtypeStruct((total, depth), BF),
            jax.ShapeDtypeStruct((total, lanes_x), F32),
            jax.ShapeDtypeStruct((total, LANES), F32),
            jax.ShapeDtypeStruct((total, lanes_v), F32),
            jax.ShapeDtypeStruct((count, N, lanes_v), F32),
        ],
        compiler_params=params(),
        cost_estimate=cost(total, depth, lanes_v, 6),
    )(starts, hid, gain, w1, taps, heads, skip, *spreaders(lanes_v))


def run_gate(u, wg, ow, mixed, gain):
    depth = u.shape[1]
    total, lanes_v = mixed.shape
    return pl.pallas_call(
        gate_kernel,
        grid=(total // STRETCH,),
        in_specs=[
            tokens(depth),
            full((depth, lanes_v)),
            full((lanes_v, depth)),
            tokens(lanes_v),
            full(gain.shape),
        ],
        out_specs=[
            tokens(depth),
            tokens(lanes_v),
            pl.BlockSpec((8, STRETCH), lambda c, *_: (0, c)),
        ],
        out_shape=[
            jax.ShapeDtypeStruct((total, depth), BF),
            jax.ShapeDtypeStruct((total, lanes_v), F32),
            jax.ShapeDtypeStruct((8, total), F32),
        ],
        compiler_params=params(),
        cost_estimate=cost(total, depth, lanes_v, 1),
    )(u, wg, ow, mixed, gain)


def run_pull(lengths, cot, ow, gate, mixed, gain):
    count, depth = lengths.shape[0], cot.shape[1]
    total, lanes_v = mixed.shape
    return pl.pallas_call(
        pull_kernel,
        grid_spec=pltpu.PrefetchScalarGridSpec(
            num_scalar_prefetch=1,
            grid=(count,),
            in_specs=[
                tokens(depth),
                full((lanes_v, depth)),
                tokens(lanes_v),
                tokens(lanes_v),
                full(gain.shape),
            ],
            out_specs=[tokens(lanes_v), pl.BlockSpec((8, STRETCH), lambda c, *_: (0, c))],
        ),
        out_shape=[
            jax.ShapeDtypeStruct((total, lanes_v), F32),
            jax.ShapeDtypeStruct((8, total), F32),
        ],
        compiler_params=params(),
        cost_estimate=cost(total, depth, lanes_v, 0.01),
    )(lengths, cot, ow, gate, mixed, gain)


def run_gate_back(lengths, place, outer, strided, hid, cot, gate, gg, mixed, stats, gain):
    count, depth = lengths.shape[0], hid.shape[1]
    total, lanes_v = mixed.shape
    lengths = jnp.concatenate([lengths, place[None]])
    blocks = [(depth // outer, lanes_v)] * outer
    blocks += [(lanes_v // outer, depth)] * outer if strided else [(lanes_v, depth)]
    return pl.pallas_call(
        functools.partial(gate_back_kernel, outer),
        grid_spec=pltpu.PrefetchScalarGridSpec(
            num_scalar_prefetch=1,
            grid=(count,),
            in_specs=[
                tokens(depth),
                tokens(depth),
                tokens(lanes_v),
                tokens(lanes_v),
                tokens(lanes_v),
                tokens(LANES),
                full(gain.shape),
            ],
            out_specs=[
                tokens(lanes_v),
                tokens(lanes_v),
                full((1, lanes_v)),
                *[full(shape) for shape in blocks],
            ],
            scratch_shapes=[
                pltpu.VMEM((lanes_v, depth), F32),
                pltpu.VMEM((depth, lanes_v), F32),
            ],
        ),
        out_shape=[
            jax.ShapeDtypeStruct((total, lanes_v), F32),
            jax.ShapeDtypeStruct((total, lanes_v), BF),
            jax.ShapeDtypeStruct((1, lanes_v), F32),
            *[jax.ShapeDtypeStruct(shape, BF) for shape in blocks],
        ],
        compiler_params=params(),
        cost_estimate=cost(total, depth, lanes_v, 0.01),
    )(lengths, hid, cot, gate, gg, mixed, stats, gain)


def run_backward(starts, depth, xin, dtp, dmix, dgate, sin, w1, wg, taps, heads, skip):
    count = starts.shape[0]
    lanes_v, lanes_x = skip.shape[1], taps.shape[1]
    total = xin.shape[0]
    per = STRETCH // HALO
    shape1 = (depth, w1.shape[1])

    def back(width):
        return pl.BlockSpec((STRETCH, width), lambda i, *_: (count - 1 - i, 0))

    return pl.pallas_call(
        backward_kernel,
        grid_spec=pltpu.PrefetchScalarGridSpec(
            num_scalar_prefetch=1,
            grid=(count,),
            in_specs=[
                back(lanes_x),
                pl.BlockSpec(
                    (HALO, lanes_x), lambda i, *_: (jnp.maximum((count - 1 - i) * per - 1, 0), 0)
                ),
                back(LANES),
                back(lanes_v),
                back(lanes_v),
                pl.BlockSpec((1, N, lanes_v), lambda i, *_: (count - 1 - i, 0, 0)),
                full(shape1),
                full((depth, lanes_v)),
                full(taps.shape),
                full(heads.shape),
                full(skip.shape),
                full((LANES, lanes_v)),
                full((LANES, 2 * lanes_v)),
            ],
            out_specs=[
                back(depth),
                back(lanes_v),
                back(2 * N + LANES),
                full((8, lanes_x)),
                full((8, LANES)),
                full((1, lanes_v)),
            ],
            scratch_shapes=[
                pltpu.VMEM((N, lanes_v), F32),
                pltpu.VMEM((STRETCH + HALO, lanes_x), F32),
                pltpu.VMEM((STRETCH + HALO, lanes_x), F32),
                pltpu.VMEM((STRETCH, lanes_x), F32),
                pltpu.VMEM((STRETCH, STRETCH), F32),
                pltpu.VMEM((STRETCH, STRETCH), F32),
                pltpu.VMEM((2, STRETCH, STRETCH), F32),
                pltpu.VMEM((2, STRETCH, STRETCH), BF),
                pltpu.VMEM((LANES, STRETCH), F32),
                pltpu.VMEM((STRETCH, LANES), F32),
                pltpu.VMEM((STRETCH, 2 * lanes_v), F32),
                pltpu.VMEM((STRETCH, lanes_v), F32),
            ],
        ),
        out_shape=[
            jax.ShapeDtypeStruct((total, depth), BF),
            jax.ShapeDtypeStruct((total, lanes_v), BF),
            jax.ShapeDtypeStruct((total, 2 * N + LANES), BF),
            jax.ShapeDtypeStruct((8, lanes_x), F32),
            jax.ShapeDtypeStruct((8, LANES), F32),
            jax.ShapeDtypeStruct((1, lanes_v), F32),
        ],
        compiler_params=params(),
        cost_estimate=cost(total, depth, lanes_v, 0.01),
    )(starts, xin, xin, dtp, dmix, dgate, sin, w1, wg, taps, heads, skip, *spreaders(lanes_v))


def relay_blocks(part, axis, beside=()):
    count, place = lax.axis_size(axis), lax.axis_index(axis)
    got = []
    right, left = part, part
    for k in range(1, count):
        if k >= 2 and k - 2 < len(beside):
            right, left, beside[k - 2] = lax.optimization_barrier((right, left, beside[k - 2]))
        right = lax.ppermute(right, axis, [(i, i + 1) for i in range(count - 1)])
        left = lax.ppermute(left, axis, [(i + 1, i) for i in range(count - 1)])
        got.append((right, jnp.where(place >= k, place - k, count)))
        got.append((left, jnp.where(place + k < count, place + k, count)))
    return got


def rotation(block, axis, k):
    count = lax.axis_size(axis)
    return lax.ppermute(block, axis, [(i, (i + k) % count) for i in range(count)])


def direct_blocks(part, axis):
    count, place = lax.axis_size(axis), lax.axis_index(axis)
    return [(rotation(part, axis, k), lax.rem(place + count - k, count)) for k in range(1, count)]


def exchanged_sum(blocks, axis):
    total = blocks[0].astype(F32)
    for k in range(1, len(blocks)):
        total = total + rotation(blocks[k], axis, k).astype(F32)
    return total


def assembled(part, got, axis, after=None):
    count, place = lax.axis_size(axis), lax.axis_index(axis)
    rows = part.shape[0]
    start = (0,) * (part.ndim - 1)
    blocks = [part] + [block for block, _ in got]
    places = [place] + [at for _, at in got]
    if after is not None:
        blocks, _ = lax.optimization_barrier((blocks, after))
    whole = jnp.zeros(((count + 1) * rows, *part.shape[1:]), part.dtype)
    for block, at in zip(blocks, places):
        whole = lax.dynamic_update_slice(whole, block, (at * rows, *start))
    return whole


def rows_kernel(outer_h, gate, values, shared, weight, gain, grad_out, norm_out):
    inner, rows, lanes_v = gate.shape
    width = lanes_v // outer_h
    per = lanes_v // P_SIZE // outer_h
    total = jnp.zeros((rows, 1), F32)

    def put(low, part):
        grad_out[:, low : low + part.shape[1]] = part
        old = weight[:, low : low + part.shape[1]].astype(F32)
        return jnp.sum(old * part, axis=1, keepdims=True)

    for base, got in ((0, gate), (DI, values)):
        for f in range(inner):
            for z in range(outer_h):
                part = got[f, :, z * width : (z + 1) * width].astype(F32)
                total = total + put(base + (z * inner + f) * width, part)
    common = jnp.zeros((rows, 2 * N), F32)
    steps = jnp.zeros((rows, H), F32)
    source = lax.broadcasted_iota(jnp.int32, (LANES, H), 0)
    target = lax.broadcasted_iota(jnp.int32, (LANES, H), 1)
    for f in range(inner):
        common = common + shared[f, :, : 2 * N].astype(F32)
        spot = ((source // per) * inner + f) * per + source % per
        chosen = jnp.logical_and(spot == target, source < per * outer_h)
        steps = steps + mm(shared[f, :, 2 * N :], chosen.astype(F32).astype(BF))
    total = total + put(2 * DI, common) + put(2 * DI + 2 * N, steps)
    norm_out[...] = jnp.broadcast_to(total / gain[...], norm_out.shape)


def run_rows(outer_h, gate, values, shared, weight, gain):
    rows, width = weight.shape
    return pl.pallas_call(
        functools.partial(rows_kernel, outer_h),
        out_shape=[
            jax.ShapeDtypeStruct((rows, width), F32),
            jax.ShapeDtypeStruct((rows, LANES), F32),
        ],
        compiler_params=pltpu.CompilerParams(vmem_limit_bytes=VMEM_BYTES),
    )(gate, values, shared, weight, gain)


def body(
    hidden,
    out_cotangent,
    norm_gain,
    in_weight,
    conv_weight,
    conv_bias,
    step_bias,
    decay_log,
    skip_gain,
    gate_gain,
    out_weight,
    stretch_len,
    stretch_start,
):
    outer, inner = lax.axis_size("dp"), lax.axis_size("fsdp")
    place = lax.axis_index("fsdp")
    local_heads = H // inner
    lanes_v = local_heads * P_SIZE
    lanes_x = lanes_v + 2 * N
    rows_w = in_weight.shape[0]
    rows_o = out_weight.shape[0]
    depth = hidden.shape[1]
    strided = rows_o % P_SIZE == 0
    outer_h = outer if strided else 1

    def by_place(whole, axis, unit):
        shape = whole.shape
        cut = (*shape[:axis], outer_h, inner, local_heads // outer_h * unit, *shape[axis + 1 :])
        parts = jnp.moveaxis(whole.reshape(cut), axis + 1, 0)
        return parts.reshape(inner, *shape[:axis], local_heads * unit, *shape[axis + 1 :])

    def from_places(parts, axis, unit):
        shape = parts.shape[1:]
        cut = (inner, *shape[:axis], outer_h, local_heads // outer_h * unit, *shape[axis + 1 :])
        whole = jnp.moveaxis(parts.reshape(cut), 0, axis + 1)
        return whole.reshape(*shape[:axis], H * unit, *shape[axis + 1 :])

    def own(whole, axis, unit):
        return lax.dynamic_index_in_dim(by_place(whole, axis, unit), place, 0, False)

    wide = CONV - 2 * N
    to_values = by_place(in_weight[:, DI : DI + wide], 1, P_SIZE)
    to_shared = jnp.broadcast_to(
        in_weight[None, :, DI + wide : DI + CONV], (inner, rows_w, 2 * N)
    )
    to_steps = by_place(in_weight[:, DI + CONV :], 1, 1)
    to_steps = jnp.pad(to_steps, ((0, 0), (0, 0), (0, LANES - local_heads)))
    sent = jnp.concatenate([to_values, to_shared, to_steps], axis=2)
    w1 = lax.all_to_all(sent, "fsdp", 0, 0, tiled=True).reshape(inner * rows_w, lanes_x + LANES)
    to_gate = by_place(in_weight[:, :DI], 1, P_SIZE)
    wg = lax.all_to_all(to_gate, "fsdp", 0, 0, tiled=True).reshape(inner * rows_w, lanes_v)
    hid = lax.all_gather(hidden, "fsdp", axis=0, tiled=True)

    small = (
        norm_gain,
        gate_gain,
        conv_weight,
        conv_bias,
        step_bias,
        decay_log,
        skip_gain,
        stretch_len.astype(BF),
        stretch_start.astype(BF),
    )
    sizes = [math.prod(a.shape) for a in small]
    packed = jnp.concatenate([a.reshape(-1) for a in small]).astype(F32)
    spread = lax.all_gather(packed[None, None, :], "fsdp", axis=0, tiled=True)[:, 0]
    gains = lax.all_gather(spread[None, :, : sizes[0] + sizes[1]], "dp", axis=0, tiled=True)
    beside = [spread, gains]
    w1_got = relay_blocks(w1, "dp", beside)
    spread, gains = beside
    if strided:
        ow_got = relay_blocks(out_weight, "dp")
        w1, ow_got, wg = lax.optimization_barrier((w1, ow_got, wg))
    w1 = assembled(w1, w1_got, "dp")
    late = max(len(w1_got) - 4, 0)
    wg, _ = lax.optimization_barrier((wg, w1_got[late : late + 2]))
    wg_got = direct_blocks(wg, "dp")
    ends = [sum(sizes[: i + 1]) for i in range(len(sizes))]
    pieces = [spread[:, end - size : end] for end, size in zip(ends, sizes)]
    norm_full = gains[:, :, : sizes[0]].reshape(-1)
    gate_full = gains[:, :, sizes[0] :].reshape(-1)
    conv_full = pieces[2].reshape(CONV, TAPS)
    bias_full = pieces[3].reshape(CONV)
    per_head = [own(a.reshape(H), 0, 1) for a in pieces[4:7]]
    lengths = pieces[7].reshape(-1).astype(jnp.int32)
    starts = pieces[8].reshape(-1).astype(jnp.int32)

    gain_own = own(gate_full, 0, P_SIZE)[None, :]
    taps_all = jnp.concatenate([conv_full.T, bias_full[None, :]], axis=0)
    taps = jnp.concatenate([own(taps_all[:, :wide], 1, P_SIZE), taps_all[:, wide:]], axis=1)
    taps = jnp.pad(taps, ((0, 8 - (TAPS + 1)), (0, 0)))
    heads = jnp.stack([per_head[0], -jnp.exp(per_head[1])])
    heads = jnp.pad(heads, ((0, 6), (0, LANES - local_heads)))
    skip = jnp.repeat(per_head[2], P_SIZE)[None, :]

    u, xin, dtp, mixed, sin = run_forward(starts, hid, norm_full[None, :], w1, taps, heads, skip)

    wg = assembled(wg, wg_got, "dp", mixed)
    if strided:
        ow = assembled(out_weight, ow_got, "dp")
    else:
        ow = own(lax.all_gather(out_weight, ("dp", "fsdp"), axis=0, tiled=True), 0, P_SIZE)
    cot, _ = lax.optimization_barrier((out_cotangent, w1))
    cot = lax.all_gather(cot, "fsdp", axis=0, tiled=True)

    branch, gate, squares = run_gate(u, wg, ow, mixed, gain_own)
    gg, along = run_pull(lengths, cot, ow, gate, mixed, gain_own)
    stats = lax.psum(jnp.concatenate([squares[0:1], along[0:1]], axis=0), "fsdp")
    r = lax.rsqrt(stats[0] / DI + EPSILON)
    m = r * stats[1] / DI
    table = jnp.pad(jnp.stack([r, m], axis=1), ((0, 0), (0, LANES - 2)))
    branch = lax.psum_scatter(branch, "fsdp", scatter_dimension=0, tiled=True)

    dmix, dgate, ggg, *blocks = run_gate_back(
        lengths, lax.axis_index("dp"), outer, strided, u, cot, gate, gg, mixed, table, gain_own
    )
    iwg_gate = exchanged_sum(blocks[:outer], "dp").astype(BF)
    if strided:
        out_weight_grad = exchanged_sum(blocks[outer:], "dp")
    else:
        rows = lax.dynamic_update_slice_in_dim(
            jnp.zeros((DI, depth), BF), blocks[outer], place * lanes_v, 0
        )
        out_weight_grad = lax.psum_scatter(rows, ("dp", "fsdp"), scatter_dimension=0, tiled=True)
        out_weight_grad = out_weight_grad.astype(F32)

    def to_rows(mine):
        mine = mine.reshape(inner, rows_w, mine.shape[1])
        return lax.all_to_all(mine, "fsdp", 0, 0, tiled=True)


    f, gpv, gps, conv_sums, head_sums, skip_sums = run_backward(
        starts, depth, xin, dtp, dmix, dgate, sin, w1, wg, taps, heads, skip
    )
    f, branch, out_weight_grad, iwg_gate = lax.optimization_barrier(
        (f, branch, out_weight_grad, iwg_gate)
    )
    f = lax.psum_scatter(f, "fsdp", scatter_dimension=0, tiled=True).astype(F32)
    def by_rows(grad):
        rows = depth // outer
        place_z = lax.axis_index("dp")
        blocks = [
            lax.dynamic_slice_in_dim(grad, lax.rem(place_z + k, outer) * rows, rows, 0)
            for k in range(outer)
        ]
        return exchanged_sum(blocks, "dp").astype(BF)

    iwg_values = by_rows(mm_tn(u, gpv).astype(BF))
    iwg_shared = by_rows(mm_tn(u, gps).astype(BF))
    gate_rows, value_rows, shared_rows = (to_rows(a) for a in (iwg_gate, iwg_values, iwg_shared))
    in_weight_grad, norm_rows = run_rows(
        outer_h, gate_rows, value_rows, shared_rows, in_weight, norm_gain.astype(F32)[:, None]
    )
    norm_gain_grad = norm_rows[:, 0]

    total = hidden.shape[0]
    r_own = lax.dynamic_slice_in_dim(r, place * total, total, 0)
    len_here = jnp.repeat(stretch_len, STRETCH)
    alive = (jnp.arange(total) % STRETCH < len_here).astype(F32)
    rows_float = hidden.astype(F32)
    rs_own = lax.rsqrt(jnp.mean(rows_float * rows_float, axis=1, keepdims=True) + EPSILON)
    block_out = (rows_float + (alive * r_own)[:, None] * branch.astype(F32)).astype(BF)
    unit = rows_float * rs_own
    scaled = f * norm_full[None, :]
    hidden_grad = out_cotangent.astype(F32) + rs_own * (
        scaled - unit * jnp.mean(scaled * unit, axis=1, keepdims=True)
    )

    skip_part = jnp.sum(skip_sums.reshape(local_heads, P_SIZE), axis=1)
    parts = (
        conv_sums[: TAPS + 1, :lanes_v].reshape(-1),
        conv_sums[: TAPS + 1, lanes_v:].reshape(-1),
        head_sums[0:2, :local_heads].reshape(-1),
        skip_part,
        ggg.reshape(-1),
    )
    counts = [a.shape[0] for a in parts]
    bundle = lax.psum(jnp.concatenate(parts), "dp")
    bundle = lax.all_gather(bundle, "fsdp", axis=0, tiled=False)
    stops = [sum(counts[: i + 1]) for i in range(len(counts))]
    cuts = [bundle[:, stop - size : stop] for stop, size in zip(stops, counts)]
    conv_values = from_places(cuts[0].reshape(inner, TAPS + 1, lanes_v), 1, P_SIZE)
    conv_shared = jnp.sum(cuts[1].reshape(inner, TAPS + 1, 2 * N), axis=0)
    conv_all = jnp.concatenate([conv_values, conv_shared], axis=1)
    conv_mine = lax.dynamic_slice_in_dim(
        conv_all, place * conv_weight.shape[0], conv_weight.shape[0], 1
    )
    conv_weight_grad = conv_mine[:TAPS].T
    conv_bias_grad = conv_mine[TAPS]

    def heads_mine(parts_h, size):
        whole = from_places(parts_h, 0, 1)
        return lax.dynamic_slice_in_dim(whole, place * size, size, 0)

    pair_sums = cuts[2].reshape(inner, 2, local_heads)
    step_bias_grad = heads_mine(pair_sums[:, 0], step_bias.shape[0])
    decay_log_grad = heads_mine(pair_sums[:, 1], decay_log.shape[0])
    skip_gain_grad = heads_mine(cuts[3], skip_gain.shape[0])
    gate_all = from_places(cuts[4], 0, P_SIZE)
    flat = lax.axis_index("dp") * inner + place
    gate_gain_grad = lax.dynamic_slice_in_dim(
        gate_all, flat * gate_gain.shape[0], gate_gain.shape[0], 0
    )
    return (
        block_out,
        hidden_grad,
        norm_gain_grad,
        in_weight_grad,
        conv_weight_grad,
        conv_bias_grad,
        step_bias_grad,
        decay_log_grad,
        skip_gain_grad,
        gate_gain_grad,
        out_weight_grad,
    )


def solution(mesh):
    both = P(("dp", "fsdp"))
    rows = P(("dp", "fsdp"), None)
    one = P("fsdp")
    return jax.shard_map(
        body,
        mesh=mesh,
        in_specs=(rows, rows, both, rows, P("fsdp", None), one, one, one, one, both, rows, both, both),
        out_specs=(rows, rows, both, rows, P("fsdp", None), one, one, one, one, both, rows),
        check_vma=False,
    )
```

```python
import functools
import math

import jax
import jax.numpy as jnp
import numpy as np
from jax import lax
from jax.experimental import pallas as pl
from jax.experimental.pallas import tpu as pltpu
from jax.sharding import PartitionSpec as P

H = 64
P_SIZE = 64
N = 128
TAPS = 4
STRETCH = 256
DI = 4096
CONV = 4352
LANES = 128
HALO = 8

EPSILON = 1e-05
BF = jnp.bfloat16
F32 = jnp.float32
VMEM_BYTES = 58 * 1024 * 1024
NEGATIVE = -1e30
PACK = 32
ROWS = 32
HALF = 128


def mm(a, b):
    return lax.dot_general(a, b, (((1,), (0,)), ((), ())), preferred_element_type=F32)


def mm_nt(a, b):
    return lax.dot_general(a, b, (((1,), (1,)), ((), ())), preferred_element_type=F32)


def mm_tn(a, b):
    return lax.dot_general(a, b, (((0,), (0,)), ((), ())), preferred_element_type=F32)


def mm_exact(a, b):
    return lax.dot_general(
        a, b, (((1,), (0,)), ((), ())), precision=lax.Precision.HIGHEST, preferred_element_type=F32
    )


def mm_nt_exact(a, b):
    return lax.dot_general(
        a, b, (((1,), (1,)), ((), ())), precision=lax.Precision.HIGHEST, preferred_element_type=F32
    )


def sigmoid(v):
    return 1.0 / (1.0 + jnp.exp(-v))


def softplus(v):
    return jnp.maximum(v, 0.0) + jnp.log1p(jnp.exp(-jnp.abs(v)))


def half_mask(rows):
    return lax.broadcasted_iota(jnp.int32, (rows, LANES), 1) < P_SIZE


def convolved(ext, taps):
    out = taps[TAPS : TAPS + 1, :]
    for j in range(TAPS):
        low = HALO - (TAPS - 1) + j
        out = out + ext[low : low + STRETCH, :] * taps[j : j + 1, :]
    return out


def three_parts(table, heads_here):
    lane = lax.broadcasted_iota(jnp.int32, table.shape, 1)
    table = jnp.where(lane < heads_here, table, 0.0)
    high = table.astype(BF).astype(F32)
    rest = table - high
    middle = rest.astype(BF).astype(F32)
    low = rest - middle
    packed = high + pltpu.roll(middle, PACK, 1) + pltpu.roll(low, 2 * PACK, 1)
    return packed.astype(BF)


def spreader(heads_here, width):
    source = np.arange(LANES)
    head = np.where(source < 3 * PACK, source % PACK, heads_here)
    return jnp.asarray(head[:, None] == np.arange(heads_here * width)[None, :] // width, BF)


def split_sum(ones, table, heads_here):
    lane = lax.broadcasted_iota(jnp.int32, table.shape, 1)
    got = mm(ones.astype(F32).astype(BF), three_parts(table, heads_here))
    got = got + pltpu.roll(got, LANES - PACK, 1) + pltpu.roll(got, LANES - 2 * PACK, 1)
    return jnp.where(lane < heads_here, got, 0.0)


def lower_ones():
    rows = lax.broadcasted_iota(jnp.int32, (STRETCH, STRETCH), 0)
    cols = lax.broadcasted_iota(jnp.int32, (STRETCH, STRETCH), 1)
    return rows, cols


def forward_kernel(
    starts, hid, gain, wv, ws, taps, heads, skip, to_pairs, to_lanes, u_out, xin_out, dtp_out, mixed_out, sin_out, state, ext,
    scores, mixing, columns, steps,
):
    c = pl.program_id(0)
    fresh = starts[c] > 0
    lanes_v = skip.shape[1]
    rows_in = hid[...]
    wide = rows_in.astype(F32)
    square = jnp.sum(wide * wide, axis=1, keepdims=True)
    rs = lax.rsqrt(square / rows_in.shape[1] + EPSILON)
    u = (wide * rs * gain[...]).astype(BF)
    u_out[...] = u
    halo = ext[pl.ds(STRETCH, HALO), :]
    ext[pl.ds(0, HALO), :] = jnp.where(fresh, 0.0, halo)
    from_values = mm(u, wv[...])
    from_shared = mm(u, ws[...])
    dtp = from_shared[:, 2 * N :] + heads[0:1, :]
    xin_out[:, :lanes_v] = from_values
    xin_out[:, lanes_v:] = from_shared[:, : 2 * N]
    dtp_out[...] = dtp
    ext[pl.ds(HALO, STRETCH), :lanes_v] = from_values
    ext[pl.ds(HALO, STRETCH), lanes_v:] = from_shared[:, : 2 * N]
    pre = convolved(ext, taps)
    act = pre * sigmoid(pre)
    values = act[:, :lanes_v]
    written = act[:, lanes_v : lanes_v + N].astype(BF)
    readout = act[:, lanes_v + N :].astype(BF)
    step = softplus(dtp)
    rows, cols = lower_ones()
    causal = rows >= cols
    decay = split_sum(causal, step * heads[1:2, :], lanes_v // P_SIZE)
    decay_t = decay.T
    before = jnp.where(fresh, 0.0, state[...])
    sin_out[0] = before
    scores[...] = mm_nt(readout, written)
    columns[...] = mm(three_parts(decay, lanes_v // P_SIZE), to_lanes[...])
    steps[...] = mm(three_parts(step, lanes_v // P_SIZE), to_pairs[...])
    carried = mm_exact(act[:, lanes_v + N :], before)
    written_t = act[:, lanes_v : lanes_v + N].T.astype(BF)
    left = half_mask(STRETCH)
    for pair in range(lanes_v // LANES):
        lo = pair * LANES
        v = values[:, lo : lo + LANES]
        step_pair = steps[:, lo : lo + LANES]
        decay_pair = jnp.where(
            left, columns[:, 2 * lo : 2 * lo + LANES], columns[:, 2 * lo + LANES : 2 * (lo + LANES)]
        )
        last_pair = decay_pair[STRETCH - 1 :, :]
        sv_wide = v * step_pair
        sv = sv_wide.astype(BF)
        out = jnp.exp(decay_pair) * carried[:, lo : lo + LANES] + skip[:, lo : lo + LANES] * v
        top, bottom = out[:HALF], out[HALF:]
        for j in range(2):
            h = 2 * pair + j
            for r in range(0, STRETCH, ROWS):
                column = columns[r : r + ROWS, h * HALF : (h + 1) * HALF]
                for t in range(0, HALF if r < HALF else STRETCH, HALF):
                    gap = column - decay_t[h : h + 1, t : t + HALF]
                    if t + HALF > r:
                        gap = jnp.where(block_mask(r, t), gap, NEGATIVE)
                    block = scores[r : r + ROWS, t : t + HALF] * jnp.exp(gap)
                    mixing[j, r : r + ROWS, t : t + HALF] = block.astype(BF)
            mine = left if j == 0 else jnp.logical_not(left)
            sv_mine = jnp.where(mine, sv, jnp.zeros_like(sv))
            top = top + mm(mixing[j, :HALF, :HALF], sv_mine[:HALF])
            bottom = bottom + mm(mixing[j, HALF:, :], sv_mine)
        mixed_out[:HALF, lo : lo + LANES] = top
        mixed_out[HALF:, lo : lo + LANES] = bottom
        tv = (sv_wide * jnp.exp(last_pair - decay_pair)).astype(BF)
        state[:, lo : lo + LANES] = jnp.exp(last_pair) * before[:, lo : lo + LANES] + mm(
            written_t, tv
        )


def block_mask(r, t):
    rows = lax.broadcasted_iota(jnp.int32, (ROWS, HALF), 0) + r
    cols = lax.broadcasted_iota(jnp.int32, (ROWS, HALF), 1) + t
    return rows >= cols


def block_mask_t(r, t):
    rows = lax.broadcasted_iota(jnp.int32, (ROWS, HALF), 0) + r
    cols = lax.broadcasted_iota(jnp.int32, (ROWS, HALF), 1) + t
    return rows <= cols


def column_rows(column):
    wide = jnp.broadcast_to(column, (STRETCH, LANES))
    return wide.T[0:8, :]


def gate_kernel(u, wg, ow, mixed, gain, branch_out, gate_out, squares_out):
    gate = mm(u[...], wg[...])
    gate_out[...] = gate
    gated = mixed[...] * gate * sigmoid(gate)
    branch_out[...] = mm((gated * gain[...]).astype(BF), ow[...]).astype(BF)
    squares_out[...] = column_rows(jnp.sum(gated * gated, axis=1, keepdims=True))


def pull_kernel(lengths, cot, ow, gate, mixed, gain, gg_out, along_out):
    c = pl.program_id(0)
    alive = lax.broadcasted_iota(jnp.int32, (STRETCH, 1), 0) < lengths[c]
    cotangent = cot[...]
    cotangent = jnp.where(alive, cotangent, jnp.zeros_like(cotangent))
    gg = mm_nt(cotangent, ow[...])
    gg_out[...] = gg
    gated = mixed[...] * gate[...] * sigmoid(gate[...])
    along_out[...] = column_rows(jnp.sum(gg * gain[...] * gated, axis=1, keepdims=True))


def gate_back_kernel(
    outer,
    lengths,
    hid,
    cot,
    gate,
    gg,
    mixed,
    stats,
    gain,
    dmix_out,
    dgate_out,
    ggg_out,
    *rest,
):
    c = pl.program_id(0)
    outs, (owg, iwg) = rest[:-2], rest[-2:]
    count = pl.num_programs(0)
    iwg_outs = outs[:outer]
    owg_outs = outs[outer:]
    r = stats[:, 0:1]
    m = stats[:, 1:2]
    v = gate[...]
    s = sigmoid(v)
    silu = v * s
    mix = mixed[...]
    normed = mix * silu * r
    back = gg[...]
    dgated = r * (back * gain[...] - normed * m)
    dmix_out[...] = dgated * silu
    dgate = dgated * mix * (s * (1.0 + v * (1.0 - s)))
    dgate_low = dgate.astype(BF)
    dgate_out[...] = dgate_low
    alive = lax.broadcasted_iota(jnp.int32, (STRETCH, 1), 0) < lengths[c]
    cotangent = cot[...]
    cotangent = jnp.where(alive, cotangent, jnp.zeros_like(cotangent))
    owg_part = mm_tn((normed * gain[...]).astype(BF), cotangent)
    iwg_part = mm_tn(hid[...], dgate_low)
    ggg_part = jnp.sum(back * normed, axis=0, keepdims=True)

    @pl.when(c == 0)
    def _():
        owg[...] = owg_part
        iwg[...] = iwg_part
        ggg_out[...] = ggg_part

    @pl.when(c > 0)
    def _():
        owg[...] += owg_part
        iwg[...] += iwg_part
        ggg_out[...] += ggg_part

    @pl.when(c == pl.num_programs(0) - 1)
    def _():
        for whole, parts in ((owg, owg_outs), (iwg, iwg_outs)):
            rows = whole.shape[0] // len(parts)
            for k, out in enumerate(parts):
                at = lax.rem(lengths[count] + k, len(parts)) * rows
                out[...] = whole[pl.ds(pl.multiple_of(at, 16), rows), :].astype(BF)


def backward_kernel(
    starts,
    xin,
    xprev,
    dtp_in,
    dmix,
    dgate,
    sin,
    wv,
    ws,
    wg,
    taps,
    heads,
    skip,
    to_pairs,
    to_lanes,
    f_out,
    gpv_out,
    gps_out,
    conv_out,
    head_out,
    skip_out,
    dstate,
    ext,
    gext,
    gbuf,
    scores,
    dscores,
    dmixing,
    mixing,
    row_sums,
    col_sums,
    columns,
    steps,
):
    step_id = pl.program_id(0)
    count = pl.num_programs(0)
    c = count - 1 - step_id
    fresh = starts[c] > 0
    lanes_v = skip.shape[1]
    lanes_x = taps.shape[1]
    first = step_id == 0
    next_fresh = jnp.logical_or(first, starts[jnp.minimum(c + 1, count - 1)] > 0)

    ext[pl.ds(0, HALO), :] = jnp.where(fresh, 0.0, xprev[...])
    ext[pl.ds(HALO, STRETCH), :] = xin[...]
    pre = convolved(ext, taps)
    sig = sigmoid(pre)
    act = pre * sig
    values = act[:, :lanes_v]
    written_f = act[:, lanes_v : lanes_v + N]
    readout_f = act[:, lanes_v + N :]
    written = written_f.astype(BF)
    readout = readout_f.astype(BF)
    dtp = dtp_in[...]
    step = softplus(dtp)
    rate = heads[1:2, :]
    rows, cols = lower_ones()
    causal = rows >= cols
    anti = rows <= cols
    decay = split_sum(causal, step * rate, lanes_v // P_SIZE)
    decay_t = decay.T
    last = decay[STRETCH - 1 : STRETCH, :]
    grow_last = jnp.exp(last)
    before = sin[0]
    before_low = before.astype(BF)
    after = jnp.where(next_fresh, 0.0, dstate[...])
    after_low = after.astype(BF)
    scores[...] = mm_nt(written, readout)
    columns[...] = mm(three_parts(decay, lanes_v // P_SIZE), to_lanes[...])
    steps[...] = mm(three_parts(step, lanes_v // P_SIZE), to_pairs[...])
    carried = mm(readout, before_low)
    spread = mm(written, after_low)
    readout_t = readout_f.T.astype(BF)
    left = half_mask(STRETCH)
    left_row = half_mask(1)
    lane = lax.broadcasted_iota(jnp.int32, (STRETCH, LANES), 1)
    lane_row = lax.broadcasted_iota(jnp.int32, (1, LANES), 1)
    row_sums[...] = jnp.zeros_like(row_sums)
    lane_rows = lax.broadcasted_iota(jnp.int32, (ROWS, LANES), 1)
    within = jnp.zeros((STRETCH, LANES), F32)
    inner = jnp.zeros((STRETCH, LANES), F32)
    direct = jnp.zeros((STRETCH, LANES), F32)
    through = jnp.zeros((1, LANES), F32)
    dwritten = jnp.zeros((STRETCH, N), F32)
    dreadout = jnp.zeros((STRETCH, N), F32)
    for pair in range(lanes_v // LANES):
        lo = pair * LANES
        v = values[:, lo : lo + LANES]
        dy = dmix[:, lo : lo + LANES]
        step_pair = steps[:, lo : lo + LANES]
        decay_pair = jnp.where(
            left, columns[:, 2 * lo : 2 * lo + LANES], columns[:, 2 * lo + LANES : 2 * (lo + LANES)]
        )
        last_pair = decay_pair[STRETCH - 1 :, :]
        fall_pair = jnp.exp(last_pair - decay_pair)
        sv = v * step_pair
        sv_low = sv.astype(BF)
        dy_low = dy.astype(BF)
        q = fall_pair * spread[:, lo : lo + LANES]
        flow = sv * q
        grown = dy * jnp.exp(decay_pair)
        enter = grown * carried[:, lo : lo + LANES]
        top, bottom = q[:HALF], q[HALF:]
        for j in range(2):
            h = 2 * pair + j
            mine = left if j == 0 else jnp.logical_not(left)
            low_mine = jnp.where(mine, dy_low, jnp.zeros_like(dy_low))
            dmixing[j, :HALF, :] = mm_nt(sv_low[:HALF], low_mine)
            dmixing[j, HALF:, HALF:] = mm_nt(sv_low[HALF:], low_mine[HALF:])
            sums = [jnp.zeros((8, HALF), F32), jnp.zeros((8, HALF), F32)]
            for r in range(0, STRETCH, ROWS):
                column = columns[r : r + ROWS, h * HALF : (h + 1) * HALF]
                across = jnp.zeros((ROWS, HALF), F32)
                for t in range(0 if r < HALF else HALF, STRETCH, HALF):
                    gap = decay_t[h : h + 1, t : t + HALF] - column
                    if t < r + ROWS:
                        gap = jnp.where(block_mask_t(r, t), gap, NEGATIVE)
                    kernel = jnp.exp(gap)
                    block = scores[r : r + ROWS, t : t + HALF] * kernel
                    back = dmixing[j, r : r + ROWS, t : t + HALF]
                    mixing[j, r : r + ROWS, t : t + HALF] = block.astype(BF)
                    turned = kernel * back
                    if h:
                        turned = turned + dscores[r : r + ROWS, t : t + HALF]
                    dscores[r : r + ROWS, t : t + HALF] = turned
                    edges = block * back
                    across = across + edges
                    for k in range(0, ROWS, 8):
                        sums[t // HALF] = sums[t // HALF] + edges[k : k + 8]
                total = jnp.sum(across, axis=1, keepdims=True)
                old = col_sums[r : r + ROWS, :] if h else jnp.zeros((ROWS, LANES), F32)
                col_sums[r : r + ROWS, :] = jnp.where(lane_rows == h, total, old)
            row_sums[h : h + 1, :HALF] = jnp.sum(sums[0], axis=0, keepdims=True)
            row_sums[h : h + 1, HALF:] = jnp.sum(sums[1], axis=0, keepdims=True)
            top = top + mm(mixing[j, :HALF, :], low_mine)
            bottom = bottom + mm(mixing[j, HALF:, HALF:], low_mine[HALF:])
            zero = jnp.zeros_like(flow)
            within = jnp.where(
                lane == h, jnp.sum(jnp.where(mine, flow, zero), axis=1, keepdims=True), within
            )
            inner = jnp.where(
                lane == h, jnp.sum(jnp.where(mine, enter, zero), axis=1, keepdims=True), inner
            )
        q = jnp.concatenate([top, bottom], axis=0)
        vq = v * q
        cross = jnp.sum(
            before[:, lo : lo + LANES] * after[:, lo : lo + LANES], axis=0, keepdims=True
        )
        for j in range(2):
            h = 2 * pair + j
            mine = left if j == 0 else jnp.logical_not(left)
            mine_row = left_row if j == 0 else jnp.logical_not(left_row)
            direct = jnp.where(
                lane == h, jnp.sum(jnp.where(mine, vq, 0.0), axis=1, keepdims=True), direct
            )
            through = jnp.where(
                lane_row == h,
                jnp.sum(jnp.where(mine_row, cross, 0.0), axis=1, keepdims=True),
                through,
            )
        gbuf[:, lo : lo + LANES] = step_pair * q + skip[:, lo : lo + LANES] * dy
        skip_part = jnp.sum(dy * v, axis=0, keepdims=True)
        skip_out[0:1, lo : lo + LANES] = skip_part + jnp.where(
            first, 0.0, skip_out[0:1, lo : lo + LANES]
        )
        tv = (sv * fall_pair).astype(BF)
        grown_low = grown.astype(BF)
        dwritten = dwritten + mm_nt(tv, after_low[:, lo : lo + LANES])
        dreadout = dreadout + mm_nt_exact(grown, before[:, lo : lo + LANES])
        dstate[:, lo : lo + LANES] = jnp.exp(last_pair) * after[
            :, lo : lo + LANES
        ] + mm(readout_t, grown_low)
    low_top = dscores[:HALF, :].astype(BF)
    low_bottom = dscores[HALF:, HALF:].astype(BF)
    gbuf[:HALF, lanes_v : lanes_v + N] = dwritten[:HALF] + mm(low_top, readout)
    gbuf[HALF:, lanes_v : lanes_v + N] = dwritten[HALF:] + mm(low_bottom, readout[HALF:])
    turned_left = dscores[:HALF, :HALF].T.astype(BF)
    turned_right = dscores[:HALF, HALF:].T.astype(BF)
    turned_low = dscores[HALF:, HALF:].T.astype(BF)
    gbuf[:HALF, lanes_v + N :] = dreadout[:HALF] + mm(turned_left, written[:HALF])
    gbuf[HALF:, lanes_v + N :] = (
        dreadout[HALF:] + mm(turned_right, written[:HALF]) + mm(turned_low, written[HALF:])
    )

    suffix = row_sums[...].T - col_sums[...] + inner
    grad_a = (
        split_sum(anti, suffix, lanes_v // P_SIZE)
        + split_sum(rows > cols, within, lanes_v // P_SIZE)
        + grow_last * through
    )
    grad_step = direct + rate * grad_a
    grad_raw = grad_step * sigmoid(dtp)
    decay_part = jnp.sum(grad_a * step, axis=0, keepdims=True) * rate
    bias_part = jnp.sum(grad_raw, axis=0, keepdims=True)
    head_row = lax.broadcasted_iota(jnp.int32, (8, LANES), 0)
    head_part = jnp.where(head_row == 0, bias_part, jnp.where(head_row == 1, decay_part, 0.0))

    grad_pre = gbuf[...] * (sig * (1.0 + pre * (1.0 - sig)))
    gext[pl.ds(STRETCH, HALO), :] = jnp.where(next_fresh, 0.0, gext[pl.ds(0, HALO), :])
    gext[pl.ds(0, STRETCH), :] = grad_pre
    grad_in = grad_pre * taps[TAPS - 1 : TAPS, :]
    for j in range(TAPS - 1):
        up = TAPS - 1 - j
        grad_in = grad_in + gext[pl.ds(up, STRETCH), :] * taps[j : j + 1, :]
    conv_row = lax.broadcasted_iota(jnp.int32, (8, lanes_x), 0)
    conv_part = jnp.where(conv_row == TAPS, jnp.sum(grad_pre, axis=0, keepdims=True), 0.0)
    for j in range(TAPS):
        low = HALO - (TAPS - 1) + j
        conv_part = jnp.where(
            conv_row == j,
            jnp.sum(grad_pre * ext[pl.ds(low, STRETCH), :], axis=0, keepdims=True),
            conv_part,
        )
    conv_out[...] = conv_part + jnp.where(first, 0.0, conv_out[...])
    head_out[...] = head_part + jnp.where(first, 0.0, head_out[...])

    grad_in_low = grad_in.astype(BF)
    grad_raw_low = grad_raw.astype(BF)
    f = mm_nt(dgate[...], wg[...])
    f = f + mm_nt(grad_in_low[:, :lanes_v], wv[...])
    f = f + mm_nt(grad_in_low[:, lanes_v:], ws[:, : 2 * N])
    f = f + mm_nt(grad_raw_low, ws[:, 2 * N :])
    f_out[...] = f.astype(BF)
    gpv_out[...] = grad_in_low[:, :lanes_v]
    gps_out[:, : 2 * N] = grad_in_low[:, lanes_v:]
    gps_out[:, 2 * N :] = grad_raw_low


def full(shape):
    return pl.BlockSpec(shape, lambda c, *_: (0,) * len(shape))


def tokens(width):
    return pl.BlockSpec((STRETCH, width), lambda c, *_: (c, 0))


def cost(total, depth, lanes, passes):
    return pl.CostEstimate(
        flops=int(2 * total * depth * lanes * passes), bytes_accessed=0, transcendentals=0
    )


def params(name_limit=VMEM_BYTES):
    return pltpu.CompilerParams(
        dimension_semantics=("arbitrary",), vmem_limit_bytes=name_limit
    )


def spreaders(lanes_v):
    heads_here = lanes_v // P_SIZE
    return spreader(heads_here, P_SIZE), spreader(heads_here, LANES)


def run_forward(starts, hid, gain, wv, ws, taps, heads, skip):
    count, depth = starts.shape[0], hid.shape[1]
    lanes_v, lanes_x = skip.shape[1], taps.shape[1]
    total = hid.shape[0]
    return pl.pallas_call(
        forward_kernel,
        grid_spec=pltpu.PrefetchScalarGridSpec(
            num_scalar_prefetch=1,
            grid=(count,),
            in_specs=[
                tokens(depth),
                full(gain.shape),
                full((depth, wv.shape[1])),
                full((depth, ws.shape[1])),
                full(taps.shape),
                full(heads.shape),
                full(skip.shape),
                full((LANES, lanes_v)),
                full((LANES, 2 * lanes_v)),
            ],
            out_specs=[
                tokens(depth),
                tokens(lanes_x),
                tokens(LANES),
                tokens(lanes_v),
                pl.BlockSpec((1, N, lanes_v), lambda c, *_: (c, 0, 0)),
            ],
            scratch_shapes=[
                pltpu.VMEM((N, lanes_v), F32),
                pltpu.VMEM((STRETCH + HALO, lanes_x), F32),
                pltpu.VMEM((STRETCH, STRETCH), F32),
                pltpu.VMEM((2, STRETCH, STRETCH), BF),
                pltpu.VMEM((STRETCH, 2 * lanes_v), F32),
                pltpu.VMEM((STRETCH, lanes_v), F32),
            ],
        ),
        out_shape=[
            jax.ShapeDtypeStruct((total, depth), BF),
            jax.ShapeDtypeStruct((total, lanes_x), F32),
            jax.ShapeDtypeStruct((total, LANES), F32),
            jax.ShapeDtypeStruct((total, lanes_v), F32),
            jax.ShapeDtypeStruct((count, N, lanes_v), F32),
        ],
        compiler_params=params(),
        cost_estimate=cost(total, depth, lanes_v, 6),
    )(starts, hid, gain, wv, ws, taps, heads, skip, *spreaders(lanes_v))


def run_gate(u, wg, ow, mixed, gain):
    depth = u.shape[1]
    total, lanes_v = mixed.shape
    return pl.pallas_call(
        gate_kernel,
        grid=(total // STRETCH,),
        in_specs=[
            tokens(depth),
            full((depth, lanes_v)),
            full((lanes_v, depth)),
            tokens(lanes_v),
            full(gain.shape),
        ],
        out_specs=[
            tokens(depth),
            tokens(lanes_v),
            pl.BlockSpec((8, STRETCH), lambda c, *_: (0, c)),
        ],
        out_shape=[
            jax.ShapeDtypeStruct((total, depth), BF),
            jax.ShapeDtypeStruct((total, lanes_v), F32),
            jax.ShapeDtypeStruct((8, total), F32),
        ],
        compiler_params=params(),
        cost_estimate=cost(total, depth, lanes_v, 1),
    )(u, wg, ow, mixed, gain)


def run_pull(lengths, cot, ow, gate, mixed, gain):
    count, depth = lengths.shape[0], cot.shape[1]
    total, lanes_v = mixed.shape
    return pl.pallas_call(
        pull_kernel,
        grid_spec=pltpu.PrefetchScalarGridSpec(
            num_scalar_prefetch=1,
            grid=(count,),
            in_specs=[
                tokens(depth),
                full((lanes_v, depth)),
                tokens(lanes_v),
                tokens(lanes_v),
                full(gain.shape),
            ],
            out_specs=[tokens(lanes_v), pl.BlockSpec((8, STRETCH), lambda c, *_: (0, c))],
        ),
        out_shape=[
            jax.ShapeDtypeStruct((total, lanes_v), F32),
            jax.ShapeDtypeStruct((8, total), F32),
        ],
        compiler_params=params(),
        cost_estimate=cost(total, depth, lanes_v, 0.01),
    )(lengths, cot, ow, gate, mixed, gain)


def run_gate_back(lengths, place, outer, strided, hid, cot, gate, gg, mixed, stats, gain):
    count, depth = lengths.shape[0], hid.shape[1]
    total, lanes_v = mixed.shape
    lengths = jnp.concatenate([lengths, place[None]])
    blocks = [(depth // outer, lanes_v)] * outer
    blocks += [(lanes_v // outer, depth)] * outer if strided else [(lanes_v, depth)]
    return pl.pallas_call(
        functools.partial(gate_back_kernel, outer),
        grid_spec=pltpu.PrefetchScalarGridSpec(
            num_scalar_prefetch=1,
            grid=(count,),
            in_specs=[
                tokens(depth),
                tokens(depth),
                tokens(lanes_v),
                tokens(lanes_v),
                tokens(lanes_v),
                tokens(LANES),
                full(gain.shape),
            ],
            out_specs=[
                tokens(lanes_v),
                tokens(lanes_v),
                full((1, lanes_v)),
                *[full(shape) for shape in blocks],
            ],
            scratch_shapes=[
                pltpu.VMEM((lanes_v, depth), F32),
                pltpu.VMEM((depth, lanes_v), F32),
            ],
        ),
        out_shape=[
            jax.ShapeDtypeStruct((total, lanes_v), F32),
            jax.ShapeDtypeStruct((total, lanes_v), BF),
            jax.ShapeDtypeStruct((1, lanes_v), F32),
            *[jax.ShapeDtypeStruct(shape, BF) for shape in blocks],
        ],
        compiler_params=params(),
        cost_estimate=cost(total, depth, lanes_v, 0.01),
    )(lengths, hid, cot, gate, gg, mixed, stats, gain)


def run_backward(starts, depth, xin, dtp, dmix, dgate, sin, wv, ws, wg, taps, heads, skip):
    count = starts.shape[0]
    lanes_v, lanes_x = skip.shape[1], taps.shape[1]
    total = xin.shape[0]
    per = STRETCH // HALO

    def back(width):
        return pl.BlockSpec((STRETCH, width), lambda i, *_: (count - 1 - i, 0))

    return pl.pallas_call(
        backward_kernel,
        grid_spec=pltpu.PrefetchScalarGridSpec(
            num_scalar_prefetch=1,
            grid=(count,),
            in_specs=[
                back(lanes_x),
                pl.BlockSpec(
                    (HALO, lanes_x), lambda i, *_: (jnp.maximum((count - 1 - i) * per - 1, 0), 0)
                ),
                back(LANES),
                back(lanes_v),
                back(lanes_v),
                pl.BlockSpec((1, N, lanes_v), lambda i, *_: (count - 1 - i, 0, 0)),
                full((depth, wv.shape[1])),
                full((depth, ws.shape[1])),
                full((depth, lanes_v)),
                full(taps.shape),
                full(heads.shape),
                full(skip.shape),
                full((LANES, lanes_v)),
                full((LANES, 2 * lanes_v)),
            ],
            out_specs=[
                back(depth),
                back(lanes_v),
                back(2 * N + LANES),
                full((8, lanes_x)),
                full((8, LANES)),
                full((1, lanes_v)),
            ],
            scratch_shapes=[
                pltpu.VMEM((N, lanes_v), F32),
                pltpu.VMEM((STRETCH + HALO, lanes_x), F32),
                pltpu.VMEM((STRETCH + HALO, lanes_x), F32),
                pltpu.VMEM((STRETCH, lanes_x), F32),
                pltpu.VMEM((STRETCH, STRETCH), F32),
                pltpu.VMEM((STRETCH, STRETCH), F32),
                pltpu.VMEM((2, STRETCH, STRETCH), F32),
                pltpu.VMEM((2, STRETCH, STRETCH), BF),
                pltpu.VMEM((LANES, STRETCH), F32),
                pltpu.VMEM((STRETCH, LANES), F32),
                pltpu.VMEM((STRETCH, 2 * lanes_v), F32),
                pltpu.VMEM((STRETCH, lanes_v), F32),
            ],
        ),
        out_shape=[
            jax.ShapeDtypeStruct((total, depth), BF),
            jax.ShapeDtypeStruct((total, lanes_v), BF),
            jax.ShapeDtypeStruct((total, 2 * N + LANES), BF),
            jax.ShapeDtypeStruct((8, lanes_x), F32),
            jax.ShapeDtypeStruct((8, LANES), F32),
            jax.ShapeDtypeStruct((1, lanes_v), F32),
        ],
        compiler_params=params(),
        cost_estimate=cost(total, depth, lanes_v, 0.01),
    )(starts, xin, xin, dtp, dmix, dgate, sin, wv, ws, wg, taps, heads, skip, *spreaders(lanes_v))


def relay_blocks(part, axis):
    count, place = lax.axis_size(axis), lax.axis_index(axis)
    got = []
    right, left = part, part
    for k in range(1, count):
        right = lax.ppermute(right, axis, [(i, i + 1) for i in range(count - 1)])
        left = lax.ppermute(left, axis, [(i + 1, i) for i in range(count - 1)])
        got.append((right, jnp.where(place >= k, place - k, count)))
        got.append((left, jnp.where(place + k < count, place + k, count)))
    return got


def rotation(block, axis, k):
    count = lax.axis_size(axis)
    return lax.ppermute(block, axis, [(i, (i + k) % count) for i in range(count)])


def direct_blocks(part, axis):
    count, place = lax.axis_size(axis), lax.axis_index(axis)
    return [(rotation(part, axis, k), lax.rem(place + count - k, count)) for k in range(1, count)]


def exchanged_sum(blocks, axis):
    total = blocks[0].astype(F32)
    for k in range(1, len(blocks)):
        total = total + rotation(blocks[k], axis, k).astype(F32)
    return total


def assembled(part, got, axis, after=None):
    count, place = lax.axis_size(axis), lax.axis_index(axis)
    rows = part.shape[0]
    start = (0,) * (part.ndim - 1)
    blocks = [part] + [block for block, _ in got]
    places = [place] + [at for _, at in got]
    if after is not None:
        blocks, _ = lax.optimization_barrier((blocks, after))
    whole = jnp.zeros(((count + 1) * rows, *part.shape[1:]), part.dtype)
    for block, at in zip(blocks, places):
        whole = lax.dynamic_update_slice(whole, block, (at * rows, *start))
    return whole


def rows_kernel(outer_h, gate, values, shared, weight, gain, grad_out, norm_out):
    inner, rows, lanes_v = gate.shape
    width = lanes_v // outer_h
    per = lanes_v // P_SIZE // outer_h
    total = jnp.zeros((rows, 1), F32)

    def put(low, part):
        grad_out[:, low : low + part.shape[1]] = part
        old = weight[:, low : low + part.shape[1]].astype(F32)
        return jnp.sum(old * part, axis=1, keepdims=True)

    for base, got in ((0, gate), (DI, values)):
        for f in range(inner):
            for z in range(outer_h):
                part = got[f, :, z * width : (z + 1) * width].astype(F32)
                total = total + put(base + (z * inner + f) * width, part)
    common = jnp.zeros((rows, 2 * N), F32)
    steps = jnp.zeros((rows, H), F32)
    source = lax.broadcasted_iota(jnp.int32, (LANES, H), 0)
    target = lax.broadcasted_iota(jnp.int32, (LANES, H), 1)
    for f in range(inner):
        common = common + shared[f, :, : 2 * N].astype(F32)
        spot = ((source // per) * inner + f) * per + source % per
        chosen = jnp.logical_and(spot == target, source < per * outer_h)
        steps = steps + mm(shared[f, :, 2 * N :], chosen.astype(F32).astype(BF))
    total = total + put(2 * DI, common) + put(2 * DI + 2 * N, steps)
    norm_out[...] = jnp.broadcast_to(total / gain[...], norm_out.shape)


def run_rows(outer_h, gate, values, shared, weight, gain):
    rows, width = weight.shape
    return pl.pallas_call(
        functools.partial(rows_kernel, outer_h),
        out_shape=[
            jax.ShapeDtypeStruct((rows, width), F32),
            jax.ShapeDtypeStruct((rows, LANES), F32),
        ],
        compiler_params=pltpu.CompilerParams(vmem_limit_bytes=VMEM_BYTES),
    )(gate, values, shared, weight, gain)


def body(
    hidden,
    out_cotangent,
    norm_gain,
    in_weight,
    conv_weight,
    conv_bias,
    step_bias,
    decay_log,
    skip_gain,
    gate_gain,
    out_weight,
    stretch_len,
    stretch_start,
):
    outer, inner = lax.axis_size("dp"), lax.axis_size("fsdp")
    place = lax.axis_index("fsdp")
    local_heads = H // inner
    lanes_v = local_heads * P_SIZE
    lanes_x = lanes_v + 2 * N
    rows_w = in_weight.shape[0]
    rows_o = out_weight.shape[0]
    depth = hidden.shape[1]
    strided = rows_o % P_SIZE == 0
    outer_h = outer if strided else 1

    def by_place(whole, axis, unit):
        shape = whole.shape
        cut = (*shape[:axis], outer_h, inner, local_heads // outer_h * unit, *shape[axis + 1 :])
        parts = jnp.moveaxis(whole.reshape(cut), axis + 1, 0)
        return parts.reshape(inner, *shape[:axis], local_heads * unit, *shape[axis + 1 :])

    def from_places(parts, axis, unit):
        shape = parts.shape[1:]
        cut = (inner, *shape[:axis], outer_h, local_heads // outer_h * unit, *shape[axis + 1 :])
        whole = jnp.moveaxis(parts.reshape(cut), 0, axis + 1)
        return whole.reshape(*shape[:axis], H * unit, *shape[axis + 1 :])

    def own(whole, axis, unit):
        return lax.dynamic_index_in_dim(by_place(whole, axis, unit), place, 0, False)

    wide = CONV - 2 * N
    hid = lax.all_gather(hidden, "fsdp", axis=0, tiled=True)

    shared_width = 2 * N + H
    gains = (norm_gain, gate_gain)
    small = (
        conv_weight,
        conv_bias,
        step_bias,
        decay_log,
        skip_gain,
        stretch_len.astype(BF),
        stretch_start.astype(BF),
    )

    def in_rows(arrays):
        flat = jnp.concatenate([a.reshape(-1) for a in arrays])
        rows = -(-flat.shape[0] // shared_width)
        return jnp.pad(flat, (0, rows * shared_width - flat.shape[0])).reshape(rows, shared_width)

    gain_rows, small_rows = in_rows(gains), in_rows(small)
    block = jnp.concatenate([in_weight[:, DI + wide :], gain_rows, small_rows], axis=0)
    height = -(-block.shape[0] // 16) * 16
    block = jnp.pad(block, ((0, height - block.shape[0]), (0, 0)))
    along = assembled(block, direct_blocks(block, "dp"), "dp")[: outer * height]
    along = jnp.broadcast_to(along[None], (inner, *along.shape))
    common = lax.all_to_all(along, "fsdp", 0, 0, tiled=True)
    common = common.reshape(inner, outer, height, shared_width)

    wv = lax.all_to_all(by_place(in_weight[:, DI : DI + wide], 1, P_SIZE), "fsdp", 0, 0, tiled=True)
    wv = wv.reshape(inner * rows_w, lanes_v)
    wg = lax.all_to_all(by_place(in_weight[:, :DI], 1, P_SIZE), "fsdp", 0, 0, tiled=True)
    wg = wg.reshape(inner * rows_w, lanes_v)
    cot, _ = lax.optimization_barrier((out_cotangent, wv))
    cot = lax.all_gather(cot, "fsdp", axis=0, tiled=True)
    wv_got = relay_blocks(wv, "dp")
    late = max(len(wv_got) - 4, 0)
    wg, ow, _ = lax.optimization_barrier((wg, out_weight, wv_got[late : late + 2]))
    wg_got = direct_blocks(wg, "dp")
    if strided:
        ow_got = direct_blocks(ow, "dp")
    wv = assembled(wv, wv_got, "dp")

    rows_all = jnp.swapaxes(common[:, :, :rows_w], 0, 1).reshape(depth, shared_width)
    head_of = np.arange(H).reshape(outer_h, inner, local_heads // outer_h)
    order = jnp.asarray(np.swapaxes(head_of, 0, 1).reshape(inner, local_heads))
    mine = lax.dynamic_index_in_dim(order, place, 0, False)
    pick = (jnp.arange(H)[:, None] == mine[None, :]).astype(BF)
    pick = jnp.pad(pick, ((0, 0), (0, LANES - local_heads)))
    ws = jnp.concatenate([rows_all[:, : 2 * N], mm(rows_all[:, 2 * N :], pick).astype(BF)], axis=1)

    def out_of_rows(rows, arrays):
        flat = rows.reshape(*rows.shape[:-2], -1).astype(F32)
        parts, low = [], 0
        for a in arrays:
            size = math.prod(a.shape)
            parts.append(flat[..., low : low + size])
            low += size
        return parts

    at = rows_w + gain_rows.shape[0]
    norm_part, gate_part = out_of_rows(common[:, :, rows_w:at], gains)
    norm_full = jnp.swapaxes(norm_part, 0, 1).reshape(-1)
    gate_full = jnp.swapaxes(gate_part, 0, 1).reshape(-1)
    same = lax.dynamic_index_in_dim(common, lax.axis_index("dp"), 1, False)
    pieces = out_of_rows(same[:, at : at + small_rows.shape[0]], small)
    conv_full = pieces[0].reshape(CONV, TAPS)
    bias_full = pieces[1].reshape(CONV)
    per_head = [own(a.reshape(H), 0, 1) for a in pieces[2:5]]
    lengths = pieces[5].reshape(-1).astype(jnp.int32)
    starts = pieces[6].reshape(-1).astype(jnp.int32)

    gain_own = own(gate_full, 0, P_SIZE)[None, :]
    taps_all = jnp.concatenate([conv_full.T, bias_full[None, :]], axis=0)
    taps = jnp.concatenate([own(taps_all[:, :wide], 1, P_SIZE), taps_all[:, wide:]], axis=1)
    taps = jnp.pad(taps, ((0, 8 - (TAPS + 1)), (0, 0)))
    heads = jnp.stack([per_head[0], -jnp.exp(per_head[1])])
    heads = jnp.pad(heads, ((0, 6), (0, LANES - local_heads)))
    skip = jnp.repeat(per_head[2], P_SIZE)[None, :]

    u, xin, dtp, mixed, sin = run_forward(
        starts, hid, norm_full[None, :], wv, ws, taps, heads, skip
    )
    wg = assembled(wg, wg_got, "dp", mixed)
    if strided:
        ow = assembled(ow, ow_got, "dp", mixed)
    else:
        ow = own(lax.all_gather(out_weight, ("dp", "fsdp"), axis=0, tiled=True), 0, P_SIZE)

    branch, gate, squares = run_gate(u, wg, ow, mixed, gain_own)
    gg, along = run_pull(lengths, cot, ow, gate, mixed, gain_own)
    stats = lax.psum(jnp.concatenate([squares[0:1], along[0:1]], axis=0), "fsdp")
    r = lax.rsqrt(stats[0] / DI + EPSILON)
    m = r * stats[1] / DI
    table = jnp.pad(jnp.stack([r, m], axis=1), ((0, 0), (0, LANES - 2)))
    branch = lax.psum_scatter(branch, "fsdp", scatter_dimension=0, tiled=True)

    dmix, dgate, ggg, *blocks = run_gate_back(
        lengths, lax.axis_index("dp"), outer, strided, u, cot, gate, gg, mixed, table, gain_own
    )
    iwg_gate = exchanged_sum(blocks[:outer], "dp").astype(BF)
    if strided:
        out_weight_grad = exchanged_sum(blocks[outer:], "dp")
    else:
        rows = lax.dynamic_update_slice_in_dim(
            jnp.zeros((DI, depth), BF), blocks[outer], place * lanes_v, 0
        )
        out_weight_grad = lax.psum_scatter(rows, ("dp", "fsdp"), scatter_dimension=0, tiled=True)
        out_weight_grad = out_weight_grad.astype(F32)

    def to_rows(mine):
        mine = mine.reshape(inner, rows_w, mine.shape[1])
        return lax.all_to_all(mine, "fsdp", 0, 0, tiled=True)


    f, gpv, gps, conv_sums, head_sums, skip_sums = run_backward(
        starts, depth, xin, dtp, dmix, dgate, sin, wv, ws, wg, taps, heads, skip
    )
    skip_part = jnp.sum(skip_sums.reshape(local_heads, P_SIZE), axis=1)
    parts = (
        conv_sums[: TAPS + 1, :lanes_v].reshape(-1),
        conv_sums[: TAPS + 1, lanes_v:].reshape(-1),
        head_sums[0:2, :local_heads].reshape(-1),
        skip_part,
        ggg.reshape(-1),
    )
    counts = [a.shape[0] for a in parts]
    bundle = jnp.concatenate(parts)
    bundle = jnp.pad(bundle, (0, -bundle.shape[0] % (8 * LANES))).reshape(-1, LANES)
    f, branch, out_weight_grad, iwg_gate, bundle = lax.optimization_barrier(
        (f, branch, out_weight_grad, iwg_gate, bundle)
    )
    f = lax.psum_scatter(f, "fsdp", scatter_dimension=0, tiled=True)
    def by_rows(grad):
        rows = depth // outer
        place_z = lax.axis_index("dp")
        blocks = [
            lax.dynamic_slice_in_dim(grad, lax.rem(place_z + k, outer) * rows, rows, 0)
            for k in range(outer)
        ]
        return blocks[:1] + [rotation(blocks[k], "dp", k) for k in range(1, outer)]

    def row_sum(got):
        return sum(a.astype(F32) for a in got).astype(BF)

    iwg_values = by_rows(mm_tn(u, gpv).astype(BF))
    gate_rows = to_rows(iwg_gate)
    if outer > 1:
        gps, gate_rows, iwg_values[1] = lax.optimization_barrier((gps, gate_rows, iwg_values[1]))
    iwg_shared = by_rows(mm_tn(u, gps).astype(BF))
    value_rows, shared_rows = to_rows(row_sum(iwg_values)), to_rows(row_sum(iwg_shared))
    in_weight_grad, norm_rows = run_rows(
        outer_h, gate_rows, value_rows, shared_rows, in_weight, norm_gain.astype(F32)[:, None]
    )
    norm_gain_grad = norm_rows[:, 0]

    total = hidden.shape[0]
    r_own = lax.dynamic_slice_in_dim(r, place * total, total, 0)
    len_here = jnp.repeat(stretch_len, STRETCH)
    alive = (jnp.arange(total) % STRETCH < len_here).astype(F32)
    rows_float = hidden.astype(F32)
    rs_own = lax.rsqrt(jnp.mean(rows_float * rows_float, axis=1, keepdims=True) + EPSILON)
    block_out = (rows_float + (alive * r_own)[:, None] * branch.astype(F32)).astype(BF)
    unit = rows_float * rs_own
    scaled = f.astype(F32) * norm_full[None, :]
    hidden_grad = out_cotangent.astype(F32) + rs_own * (
        scaled - unit * jnp.mean(scaled * unit, axis=1, keepdims=True)
    )

    bundle = exchanged_sum([bundle] * outer, "dp")
    bundle = jnp.broadcast_to(bundle[None], (inner, *bundle.shape))
    bundle = lax.all_to_all(bundle, "fsdp", 0, 0, tiled=True).reshape(inner, -1)
    stops = [sum(counts[: i + 1]) for i in range(len(counts))]
    cuts = [bundle[:, stop - size : stop] for stop, size in zip(stops, counts)]
    conv_values = from_places(cuts[0].reshape(inner, TAPS + 1, lanes_v), 1, P_SIZE)
    conv_shared = jnp.sum(cuts[1].reshape(inner, TAPS + 1, 2 * N), axis=0)
    conv_all = jnp.concatenate([conv_values, conv_shared], axis=1)
    conv_mine = lax.dynamic_slice_in_dim(
        conv_all, place * conv_weight.shape[0], conv_weight.shape[0], 1
    )
    conv_weight_grad = conv_mine[:TAPS].T
    conv_bias_grad = conv_mine[TAPS]

    def heads_mine(parts_h, size):
        whole = from_places(parts_h, 0, 1)
        return lax.dynamic_slice_in_dim(whole, place * size, size, 0)

    pair_sums = cuts[2].reshape(inner, 2, local_heads)
    step_bias_grad = heads_mine(pair_sums[:, 0], step_bias.shape[0])
    decay_log_grad = heads_mine(pair_sums[:, 1], decay_log.shape[0])
    skip_gain_grad = heads_mine(cuts[3], skip_gain.shape[0])
    gate_all = from_places(cuts[4], 0, P_SIZE)
    flat = lax.axis_index("dp") * inner + place
    gate_gain_grad = lax.dynamic_slice_in_dim(
        gate_all, flat * gate_gain.shape[0], gate_gain.shape[0], 0
    )
    return (
        block_out,
        hidden_grad,
        norm_gain_grad,
        in_weight_grad,
        conv_weight_grad,
        conv_bias_grad,
        step_bias_grad,
        decay_log_grad,
        skip_gain_grad,
        gate_gain_grad,
        out_weight_grad,
    )


def solution(mesh):
    both = P(("dp", "fsdp"))
    rows = P(("dp", "fsdp"), None)
    one = P("fsdp")
    return jax.shard_map(
        body,
        mesh=mesh,
        in_specs=(rows, rows, both, rows, P("fsdp", None), one, one, one, one, both, rows, both, both),
        out_specs=(rows, rows, both, rows, P("fsdp", None), one, one, one, one, both, rows),
        check_vma=False,
    )
```

```python
import functools
import math

import jax
import jax.numpy as jnp
import numpy as np
from jax import lax
from jax.experimental import pallas as pl
from jax.experimental.pallas import tpu as pltpu
from jax.sharding import PartitionSpec as P

H = 64
P_SIZE = 64
N = 128
TAPS = 4
STRETCH = 256
DI = 4096
CONV = 4352
LANES = 128
HALO = 8

EPSILON = 1e-05
BF = jnp.bfloat16
F32 = jnp.float32
VMEM_BYTES = 58 * 1024 * 1024
NEGATIVE = -1e30
PACK = 32
WIDE = 2 * STRETCH
ROWS = 32
HALF = 128


def mm(a, b):
    return lax.dot_general(a, b, (((1,), (0,)), ((), ())), preferred_element_type=F32)


def mm_nt(a, b):
    return lax.dot_general(a, b, (((1,), (1,)), ((), ())), preferred_element_type=F32)


def mm_tn(a, b):
    return lax.dot_general(a, b, (((0,), (0,)), ((), ())), preferred_element_type=F32)


def mm_exact(a, b):
    return lax.dot_general(
        a, b, (((1,), (0,)), ((), ())), precision=lax.Precision.HIGHEST, preferred_element_type=F32
    )


def mm_nt_exact(a, b):
    return lax.dot_general(
        a, b, (((1,), (1,)), ((), ())), precision=lax.Precision.HIGHEST, preferred_element_type=F32
    )


def sigmoid(v):
    return 1.0 / (1.0 + jnp.exp(-v))


def softplus(v):
    return jnp.maximum(v, 0.0) + jnp.log1p(jnp.exp(-jnp.abs(v)))


def half_mask(rows):
    return lax.broadcasted_iota(jnp.int32, (rows, LANES), 1) < P_SIZE


def convolved(ext, taps):
    out = taps[TAPS : TAPS + 1, :]
    for j in range(TAPS):
        low = HALO - (TAPS - 1) + j
        out = out + ext[low : low + STRETCH, :] * taps[j : j + 1, :]
    return out


def three_parts(table, heads_here):
    lane = lax.broadcasted_iota(jnp.int32, table.shape, 1)
    table = jnp.where(lane < heads_here, table, 0.0)
    high = table.astype(BF).astype(F32)
    rest = table - high
    middle = rest.astype(BF).astype(F32)
    low = rest - middle
    packed = high + pltpu.roll(middle, PACK, 1) + pltpu.roll(low, 2 * PACK, 1)
    return packed.astype(BF)


def spreader(heads_here, width):
    source = np.arange(LANES)
    head = np.where(source < 3 * PACK, source % PACK, heads_here)
    return jnp.asarray(head[:, None] == np.arange(heads_here * width)[None, :] // width, BF)


def split_sum(ones, table, heads_here):
    lane = lax.broadcasted_iota(jnp.int32, table.shape, 1)
    got = mm(ones.astype(F32).astype(BF), three_parts(table, heads_here))
    got = got + pltpu.roll(got, LANES - PACK, 1) + pltpu.roll(got, LANES - 2 * PACK, 1)
    return jnp.where(lane < heads_here, got, 0.0)


def lower_ones():
    rows = lax.broadcasted_iota(jnp.int32, (STRETCH, STRETCH), 0)
    cols = lax.broadcasted_iota(jnp.int32, (STRETCH, STRETCH), 1)
    return rows, cols


def forward_kernel(
    starts, hid, gain, wv, ws, taps, heads, skip, to_pairs, to_lanes, u_out, xin_out, dtp_out, mixed_out, sin_out, state, ext,
    scores, mixing, columns, steps,
):
    c = pl.program_id(0)
    fresh = starts[c] > 0
    lanes_v = skip.shape[1]
    rows_in = hid[...]
    wide = rows_in.astype(F32)
    square = jnp.sum(wide * wide, axis=1, keepdims=True)
    rs = lax.rsqrt(square / rows_in.shape[1] + EPSILON)
    u = (wide * rs * gain[...]).astype(BF)
    u_out[...] = u
    halo = ext[pl.ds(STRETCH, HALO), :]
    ext[pl.ds(0, HALO), :] = jnp.where(fresh, 0.0, halo)
    from_values = mm(u, wv[...])
    from_shared = mm(u, ws[...])
    dtp = from_shared[:, 2 * N :] + heads[0:1, :]
    xin_out[:, :lanes_v] = from_values
    xin_out[:, lanes_v:] = from_shared[:, : 2 * N]
    dtp_out[...] = dtp
    ext[pl.ds(HALO, STRETCH), :lanes_v] = from_values
    ext[pl.ds(HALO, STRETCH), lanes_v:] = from_shared[:, : 2 * N]
    pre = convolved(ext, taps)
    act = pre * sigmoid(pre)
    values = act[:, :lanes_v]
    written = act[:, lanes_v : lanes_v + N].astype(BF)
    readout = act[:, lanes_v + N :].astype(BF)
    step = softplus(dtp)
    rows, cols = lower_ones()
    causal = rows >= cols
    decay = split_sum(causal, step * heads[1:2, :], lanes_v // P_SIZE)
    decay_t = decay.T
    before = jnp.where(fresh, 0.0, state[...])
    sin_out[0] = before
    scores[...] = mm_nt(readout, written)
    columns[...] = mm(three_parts(decay, lanes_v // P_SIZE), to_lanes[...])
    steps[...] = mm(three_parts(step, lanes_v // P_SIZE), to_pairs[...])
    read_rest = (act[:, lanes_v + N :] - readout.astype(F32)).astype(BF)
    before_high = before.astype(BF)
    before_rest = (before - before_high.astype(F32)).astype(BF)
    carried = mm(
        jnp.concatenate([readout, read_rest], axis=1),
        jnp.concatenate([before_high, before_high], axis=0),
    ) + mm(readout, before_rest)
    written_t = act[:, lanes_v : lanes_v + N].T.astype(BF)
    left = half_mask(STRETCH)
    for pair in range(lanes_v // LANES):
        lo = pair * LANES
        v = values[:, lo : lo + LANES]
        step_pair = steps[:, lo : lo + LANES]
        decay_pair = jnp.where(
            left, columns[:, 2 * lo : 2 * lo + LANES], columns[:, 2 * lo + LANES : 2 * (lo + LANES)]
        )
        last_pair = decay_pair[STRETCH - 1 :, :]
        sv_wide = v * step_pair
        sv = sv_wide.astype(BF)
        out = jnp.exp(decay_pair) * carried[:, lo : lo + LANES] + skip[:, lo : lo + LANES] * v
        top, bottom = out[:HALF], out[HALF:]
        for j in range(2):
            h = 2 * pair + j
            for r in range(0, STRETCH, ROWS):
                column = columns[r : r + ROWS, h * HALF : (h + 1) * HALF]
                for t in range(0, HALF if r < HALF else STRETCH, HALF):
                    gap = column - decay_t[h : h + 1, t : t + HALF]
                    if t + HALF > r:
                        gap = jnp.where(block_mask(r, t), gap, NEGATIVE)
                    block = scores[r : r + ROWS, t : t + HALF] * jnp.exp(gap)
                    mixing[j, r : r + ROWS, t : t + HALF] = block.astype(BF)
            mine = left if j == 0 else jnp.logical_not(left)
            sv_mine = jnp.where(mine, sv, jnp.zeros_like(sv))
            top = top + mm(mixing[j, :HALF, :HALF], sv_mine[:HALF])
            bottom = bottom + mm(mixing[j, HALF:, :], sv_mine)
        mixed_out[:HALF, lo : lo + LANES] = top
        mixed_out[HALF:, lo : lo + LANES] = bottom
        tv = (sv_wide * jnp.exp(last_pair - decay_pair)).astype(BF)
        state[:, lo : lo + LANES] = jnp.exp(last_pair) * before[:, lo : lo + LANES] + mm(
            written_t, tv
        )


def block_mask(r, t):
    rows = lax.broadcasted_iota(jnp.int32, (ROWS, HALF), 0) + r
    cols = lax.broadcasted_iota(jnp.int32, (ROWS, HALF), 1) + t
    return rows >= cols


def block_mask_t(r, t):
    rows = lax.broadcasted_iota(jnp.int32, (ROWS, HALF), 0) + r
    cols = lax.broadcasted_iota(jnp.int32, (ROWS, HALF), 1) + t
    return rows <= cols


def live_rows(block, lengths, c):
    row = lax.broadcasted_iota(jnp.int32, (WIDE, 1), 0)
    limit = jnp.where(row < STRETCH, lengths[2 * c], STRETCH + lengths[2 * c + 1])
    return jnp.where(row < limit, block, jnp.zeros_like(block))


def column_rows(column):
    wide = jnp.broadcast_to(column, (column.shape[0], LANES))
    return wide.T[0:8, :]


def gate_kernel(u, wg, ow, mixed, gain, branch_out, gate_out, squares_out):
    gate = mm(u[...], wg[...])
    gate_out[...] = gate
    gated = mixed[...] * gate * sigmoid(gate)
    branch_out[...] = mm((gated * gain[...]).astype(BF), ow[...]).astype(BF)
    squares_out[...] = column_rows(jnp.sum(gated * gated, axis=1, keepdims=True))


def pull_kernel(lengths, cot, ow, gate, mixed, gain, gg_out, along_out):
    c = pl.program_id(0)
    cotangent = live_rows(cot[...], lengths, c)
    gg = mm_nt(cotangent, ow[...])
    gg_out[...] = gg
    gated = mixed[...] * gate[...] * sigmoid(gate[...])
    along_out[...] = column_rows(jnp.sum(gg * gain[...] * gated, axis=1, keepdims=True))


def gate_back_kernel(
    outer,
    lengths,
    hid,
    cot,
    gate,
    gg,
    mixed,
    stats,
    gain,
    dmix_out,
    dgate_out,
    ggg_out,
    *rest,
):
    c = pl.program_id(0)
    outs, (owg, iwg) = rest[:-2], rest[-2:]
    count = pl.num_programs(0)
    r = stats[:, 0:1]
    m = stats[:, 1:2]
    v = gate[...]
    s = sigmoid(v)
    silu = v * s
    mix = mixed[...]
    normed = mix * silu * r
    back = gg[...]
    dgated = r * (back * gain[...] - normed * m)
    dmix_out[...] = dgated * silu
    dgate = dgated * mix * (s * (1.0 + v * (1.0 - s)))
    dgate_low = dgate.astype(BF)
    dgate_out[...] = dgate_low
    cotangent = live_rows(cot[...], lengths, c)
    owg_part = mm_tn((normed * gain[...]).astype(BF), cotangent)
    iwg_part = mm_tn(hid[...], dgate_low)
    ggg_part = jnp.sum(back * normed, axis=0, keepdims=True)

    @pl.when(c == 0)
    def _():
        owg[...] = owg_part
        iwg[...] = iwg_part
        ggg_out[...] = ggg_part

    @pl.when(c > 0)
    def _():
        owg[...] += owg_part
        iwg[...] += iwg_part
        ggg_out[...] += ggg_part

    @pl.when(c == pl.num_programs(0) - 1)
    def _():
        rows, cols = iwg.shape[0] // outer, iwg.shape[1]
        for k in range(outer):
            spot = lax.rem(lengths[2 * count] + k, outer)
            low = pl.multiple_of(spot * rows, 16)
            outs[k][:rows, :] = iwg[pl.ds(low, rows), :].astype(BF)
            if len(outs) == outer:
                high = owg.shape[0] // outer
                low = pl.multiple_of(spot * high, 16)
                for q in range(owg.shape[1] // cols):
                    part = owg[pl.ds(low, high), q * cols : (q + 1) * cols]
                    outs[k][rows + q * high : rows + (q + 1) * high, :] = part.astype(BF)
        if len(outs) > outer:
            outs[outer][...] = owg[...].astype(BF)


def backward_kernel(
    starts,
    xin,
    xprev,
    dtp_in,
    dmix,
    dgate,
    sin,
    wv,
    ws,
    wg,
    taps,
    heads,
    skip,
    to_pairs,
    to_lanes,
    f_out,
    gpv_out,
    gps_out,
    conv_out,
    head_out,
    skip_out,
    dstate,
    ext,
    gext,
    gbuf,
    scores,
    dscores,
    dmixing,
    mixing,
    row_sums,
    col_sums,
    columns,
    steps,
):
    step_id = pl.program_id(0)
    count = pl.num_programs(0)
    c = count - 1 - step_id
    fresh = starts[c] > 0
    lanes_v = skip.shape[1]
    lanes_x = taps.shape[1]
    first = step_id == 0
    next_fresh = jnp.logical_or(first, starts[jnp.minimum(c + 1, count - 1)] > 0)

    ext[pl.ds(0, HALO), :] = jnp.where(fresh, 0.0, xprev[...])
    ext[pl.ds(HALO, STRETCH), :] = xin[...]
    pre = convolved(ext, taps)
    sig = sigmoid(pre)
    act = pre * sig
    values = act[:, :lanes_v]
    written_f = act[:, lanes_v : lanes_v + N]
    readout_f = act[:, lanes_v + N :]
    written = written_f.astype(BF)
    readout = readout_f.astype(BF)
    dtp = dtp_in[...]
    step = softplus(dtp)
    rate = heads[1:2, :]
    rows, cols = lower_ones()
    causal = rows >= cols
    anti = rows <= cols
    decay = split_sum(causal, step * rate, lanes_v // P_SIZE)
    decay_t = decay.T
    last = decay[STRETCH - 1 : STRETCH, :]
    grow_last = jnp.exp(last)
    before = sin[0]
    before_low = before.astype(BF)
    after = jnp.where(next_fresh, 0.0, dstate[...])
    after_low = after.astype(BF)
    scores[...] = mm_nt(written, readout)
    columns[...] = mm(three_parts(decay, lanes_v // P_SIZE), to_lanes[...])
    steps[...] = mm(three_parts(step, lanes_v // P_SIZE), to_pairs[...])
    carried = mm(readout, before_low)
    spread = mm(written, after_low)
    readout_t = readout_f.T.astype(BF)
    left = half_mask(STRETCH)
    left_row = half_mask(1)
    lane = lax.broadcasted_iota(jnp.int32, (STRETCH, LANES), 1)
    lane_row = lax.broadcasted_iota(jnp.int32, (1, LANES), 1)
    row_sums[...] = jnp.zeros_like(row_sums)
    lane_rows = lax.broadcasted_iota(jnp.int32, (ROWS, LANES), 1)
    within = jnp.zeros((STRETCH, LANES), F32)
    inner = jnp.zeros((STRETCH, LANES), F32)
    direct = jnp.zeros((STRETCH, LANES), F32)
    through = jnp.zeros((1, LANES), F32)
    dwritten = jnp.zeros((STRETCH, N), F32)
    dreadout = jnp.zeros((STRETCH, N), F32)
    for pair in range(lanes_v // LANES):
        lo = pair * LANES
        v = values[:, lo : lo + LANES]
        dy = dmix[:, lo : lo + LANES]
        step_pair = steps[:, lo : lo + LANES]
        decay_pair = jnp.where(
            left, columns[:, 2 * lo : 2 * lo + LANES], columns[:, 2 * lo + LANES : 2 * (lo + LANES)]
        )
        last_pair = decay_pair[STRETCH - 1 :, :]
        fall_pair = jnp.exp(last_pair - decay_pair)
        sv = v * step_pair
        sv_low = sv.astype(BF)
        dy_low = dy.astype(BF)
        q = fall_pair * spread[:, lo : lo + LANES]
        flow = sv * q
        grown = dy * jnp.exp(decay_pair)
        enter = grown * carried[:, lo : lo + LANES]
        top, bottom = q[:HALF], q[HALF:]
        for j in range(2):
            h = 2 * pair + j
            mine = left if j == 0 else jnp.logical_not(left)
            low_mine = jnp.where(mine, dy_low, jnp.zeros_like(dy_low))
            dmixing[j, :HALF, :] = mm_nt(sv_low[:HALF], low_mine)
            dmixing[j, HALF:, HALF:] = mm_nt(sv_low[HALF:], low_mine[HALF:])
            sums = [jnp.zeros((8, HALF), F32), jnp.zeros((8, HALF), F32)]
            for r in range(0, STRETCH, ROWS):
                column = columns[r : r + ROWS, h * HALF : (h + 1) * HALF]
                across = jnp.zeros((ROWS, HALF), F32)
                for t in range(0 if r < HALF else HALF, STRETCH, HALF):
                    gap = decay_t[h : h + 1, t : t + HALF] - column
                    if t < r + ROWS:
                        gap = jnp.where(block_mask_t(r, t), gap, NEGATIVE)
                    kernel = jnp.exp(gap)
                    block = scores[r : r + ROWS, t : t + HALF] * kernel
                    back = dmixing[j, r : r + ROWS, t : t + HALF]
                    mixing[j, r : r + ROWS, t : t + HALF] = block.astype(BF)
                    turned = kernel * back
                    if h:
                        turned = turned + dscores[r : r + ROWS, t : t + HALF]
                    dscores[r : r + ROWS, t : t + HALF] = turned
                    edges = block * back
                    across = across + edges
                    for k in range(0, ROWS, 8):
                        sums[t // HALF] = sums[t // HALF] + edges[k : k + 8]
                total = jnp.sum(across, axis=1, keepdims=True)
                old = col_sums[r : r + ROWS, :] if h else jnp.zeros((ROWS, LANES), F32)
                col_sums[r : r + ROWS, :] = jnp.where(lane_rows == h, total, old)
            row_sums[h : h + 1, :HALF] = jnp.sum(sums[0], axis=0, keepdims=True)
            row_sums[h : h + 1, HALF:] = jnp.sum(sums[1], axis=0, keepdims=True)
            top = top + mm(mixing[j, :HALF, :], low_mine)
            bottom = bottom + mm(mixing[j, HALF:, HALF:], low_mine[HALF:])
            zero = jnp.zeros_like(flow)
            within = jnp.where(
                lane == h, jnp.sum(jnp.where(mine, flow, zero), axis=1, keepdims=True), within
            )
            inner = jnp.where(
                lane == h, jnp.sum(jnp.where(mine, enter, zero), axis=1, keepdims=True), inner
            )
        q = jnp.concatenate([top, bottom], axis=0)
        vq = v * q
        cross = jnp.sum(
            before[:, lo : lo + LANES] * after[:, lo : lo + LANES], axis=0, keepdims=True
        )
        for j in range(2):
            h = 2 * pair + j
            mine = left if j == 0 else jnp.logical_not(left)
            mine_row = left_row if j == 0 else jnp.logical_not(left_row)
            direct = jnp.where(
                lane == h, jnp.sum(jnp.where(mine, vq, 0.0), axis=1, keepdims=True), direct
            )
            through = jnp.where(
                lane_row == h,
                jnp.sum(jnp.where(mine_row, cross, 0.0), axis=1, keepdims=True),
                through,
            )
        gbuf[:, lo : lo + LANES] = step_pair * q + skip[:, lo : lo + LANES] * dy
        skip_part = jnp.sum(dy * v, axis=0, keepdims=True)
        skip_out[0:1, lo : lo + LANES] = skip_part + jnp.where(
            first, 0.0, skip_out[0:1, lo : lo + LANES]
        )
        tv = (sv * fall_pair).astype(BF)
        grown_low = grown.astype(BF)
        dwritten = dwritten + mm_nt(tv, after_low[:, lo : lo + LANES])
        dreadout = dreadout + mm_nt_exact(grown, before[:, lo : lo + LANES])
        dstate[:, lo : lo + LANES] = jnp.exp(last_pair) * after[
            :, lo : lo + LANES
        ] + mm(readout_t, grown_low)
    low_top = dscores[:HALF, :].astype(BF)
    low_bottom = dscores[HALF:, HALF:].astype(BF)
    gbuf[:HALF, lanes_v : lanes_v + N] = dwritten[:HALF] + mm(low_top, readout)
    gbuf[HALF:, lanes_v : lanes_v + N] = dwritten[HALF:] + mm(low_bottom, readout[HALF:])
    turned_left = dscores[:HALF, :HALF].T.astype(BF)
    turned_right = dscores[:HALF, HALF:].T.astype(BF)
    turned_low = dscores[HALF:, HALF:].T.astype(BF)
    gbuf[:HALF, lanes_v + N :] = dreadout[:HALF] + mm(turned_left, written[:HALF])
    gbuf[HALF:, lanes_v + N :] = (
        dreadout[HALF:] + mm(turned_right, written[:HALF]) + mm(turned_low, written[HALF:])
    )

    suffix = row_sums[...].T - col_sums[...] + inner
    grad_a = (
        split_sum(anti, suffix, lanes_v // P_SIZE)
        + split_sum(rows > cols, within, lanes_v // P_SIZE)
        + grow_last * through
    )
    grad_step = direct + rate * grad_a
    grad_raw = grad_step * sigmoid(dtp)
    decay_part = jnp.sum(grad_a * step, axis=0, keepdims=True) * rate
    bias_part = jnp.sum(grad_raw, axis=0, keepdims=True)
    head_row = lax.broadcasted_iota(jnp.int32, (8, LANES), 0)
    head_part = jnp.where(head_row == 0, bias_part, jnp.where(head_row == 1, decay_part, 0.0))

    grad_pre = gbuf[...] * (sig * (1.0 + pre * (1.0 - sig)))
    gext[pl.ds(STRETCH, HALO), :] = jnp.where(next_fresh, 0.0, gext[pl.ds(0, HALO), :])
    gext[pl.ds(0, STRETCH), :] = grad_pre
    grad_in = grad_pre * taps[TAPS - 1 : TAPS, :]
    for j in range(TAPS - 1):
        up = TAPS - 1 - j
        grad_in = grad_in + gext[pl.ds(up, STRETCH), :] * taps[j : j + 1, :]
    conv_row = lax.broadcasted_iota(jnp.int32, (8, lanes_x), 0)
    conv_part = jnp.where(conv_row == TAPS, jnp.sum(grad_pre, axis=0, keepdims=True), 0.0)
    for j in range(TAPS):
        low = HALO - (TAPS - 1) + j
        conv_part = jnp.where(
            conv_row == j,
            jnp.sum(grad_pre * ext[pl.ds(low, STRETCH), :], axis=0, keepdims=True),
            conv_part,
        )
    conv_out[...] = conv_part + jnp.where(first, 0.0, conv_out[...])
    head_out[...] = head_part + jnp.where(first, 0.0, head_out[...])

    grad_in_low = grad_in.astype(BF)
    grad_raw_low = grad_raw.astype(BF)
    f = mm_nt(dgate[...], wg[...])
    f = f + mm_nt(grad_in_low[:, :lanes_v], wv[...])
    f = f + mm_nt(grad_in_low[:, lanes_v:], ws[:, : 2 * N])
    f = f + mm_nt(grad_raw_low, ws[:, 2 * N :])
    f_out[...] = f.astype(BF)
    gpv_out[...] = grad_in_low[:, :lanes_v]
    gps_out[:, : 2 * N] = grad_in_low[:, lanes_v:]
    gps_out[:, 2 * N :] = grad_raw_low


def full(shape):
    return pl.BlockSpec(shape, lambda c, *_: (0,) * len(shape))


def blocks_of(width):
    return pl.BlockSpec((WIDE, width), lambda c, *_: (c, 0))


def tokens(width):
    return pl.BlockSpec((STRETCH, width), lambda c, *_: (c, 0))


def cost(total, depth, lanes, passes):
    return pl.CostEstimate(
        flops=int(2 * total * depth * lanes * passes), bytes_accessed=0, transcendentals=0
    )


def params(name_limit=VMEM_BYTES):
    return pltpu.CompilerParams(
        dimension_semantics=("arbitrary",), vmem_limit_bytes=name_limit
    )


def spreaders(lanes_v):
    heads_here = lanes_v // P_SIZE
    return spreader(heads_here, P_SIZE), spreader(heads_here, LANES)


def run_forward(starts, hid, gain, wv, ws, taps, heads, skip):
    count, depth = starts.shape[0], hid.shape[1]
    lanes_v, lanes_x = skip.shape[1], taps.shape[1]
    total = hid.shape[0]
    return pl.pallas_call(
        forward_kernel,
        grid_spec=pltpu.PrefetchScalarGridSpec(
            num_scalar_prefetch=1,
            grid=(count,),
            in_specs=[
                tokens(depth),
                full(gain.shape),
                full((depth, wv.shape[1])),
                full((depth, ws.shape[1])),
                full(taps.shape),
                full(heads.shape),
                full(skip.shape),
                full((LANES, lanes_v)),
                full((LANES, 2 * lanes_v)),
            ],
            out_specs=[
                tokens(depth),
                tokens(lanes_x),
                tokens(LANES),
                tokens(lanes_v),
                pl.BlockSpec((1, N, lanes_v), lambda c, *_: (c, 0, 0)),
            ],
            scratch_shapes=[
                pltpu.VMEM((N, lanes_v), F32),
                pltpu.VMEM((STRETCH + HALO, lanes_x), F32),
                pltpu.VMEM((STRETCH, STRETCH), F32),
                pltpu.VMEM((2, STRETCH, STRETCH), BF),
                pltpu.VMEM((STRETCH, 2 * lanes_v), F32),
                pltpu.VMEM((STRETCH, lanes_v), F32),
            ],
        ),
        out_shape=[
            jax.ShapeDtypeStruct((total, depth), BF),
            jax.ShapeDtypeStruct((total, lanes_x), F32),
            jax.ShapeDtypeStruct((total, LANES), F32),
            jax.ShapeDtypeStruct((total, lanes_v), F32),
            jax.ShapeDtypeStruct((count, N, lanes_v), F32),
        ],
        compiler_params=params(),
        cost_estimate=cost(total, depth, lanes_v, 6),
    )(starts, hid, gain, wv, ws, taps, heads, skip, *spreaders(lanes_v))


def run_gate(u, wg, ow, mixed, gain):
    depth = u.shape[1]
    total, lanes_v = mixed.shape
    return pl.pallas_call(
        gate_kernel,
        grid=(total // WIDE,),
        in_specs=[
            blocks_of(depth),
            full((depth, lanes_v)),
            full((lanes_v, depth)),
            blocks_of(lanes_v),
            full(gain.shape),
        ],
        out_specs=[
            blocks_of(depth),
            blocks_of(lanes_v),
            pl.BlockSpec((8, WIDE), lambda c, *_: (0, c)),
        ],
        out_shape=[
            jax.ShapeDtypeStruct((total, depth), BF),
            jax.ShapeDtypeStruct((total, lanes_v), F32),
            jax.ShapeDtypeStruct((8, total), F32),
        ],
        compiler_params=params(),
        cost_estimate=cost(total, depth, lanes_v, 1),
    )(u, wg, ow, mixed, gain)


def run_pull(lengths, cot, ow, gate, mixed, gain):
    count, depth = lengths.shape[0], cot.shape[1]
    total, lanes_v = mixed.shape
    return pl.pallas_call(
        pull_kernel,
        grid_spec=pltpu.PrefetchScalarGridSpec(
            num_scalar_prefetch=1,
            grid=(count // 2,),
            in_specs=[
                blocks_of(depth),
                full((lanes_v, depth)),
                blocks_of(lanes_v),
                blocks_of(lanes_v),
                full(gain.shape),
            ],
            out_specs=[blocks_of(lanes_v), pl.BlockSpec((8, WIDE), lambda c, *_: (0, c))],
        ),
        out_shape=[
            jax.ShapeDtypeStruct((total, lanes_v), F32),
            jax.ShapeDtypeStruct((8, total), F32),
        ],
        compiler_params=params(),
        cost_estimate=cost(total, depth, lanes_v, 0.01),
    )(lengths, cot, ow, gate, mixed, gain)


def run_gate_back(lengths, place, outer, strided, hid, cot, gate, gg, mixed, stats, gain):
    count, depth = lengths.shape[0], hid.shape[1]
    total, lanes_v = mixed.shape
    lengths = jnp.concatenate([lengths, place[None]])
    if strided:
        blocks = [(2 * depth // outer, lanes_v)] * outer
    else:
        blocks = [(depth // outer, lanes_v)] * outer + [(lanes_v, depth)]
    return pl.pallas_call(
        functools.partial(gate_back_kernel, outer),
        grid_spec=pltpu.PrefetchScalarGridSpec(
            num_scalar_prefetch=1,
            grid=(count // 2,),
            in_specs=[
                blocks_of(depth),
                blocks_of(depth),
                blocks_of(lanes_v),
                blocks_of(lanes_v),
                blocks_of(lanes_v),
                blocks_of(LANES),
                full(gain.shape),
            ],
            out_specs=[
                blocks_of(lanes_v),
                blocks_of(lanes_v),
                full((1, lanes_v)),
                *[full(shape) for shape in blocks],
            ],
            scratch_shapes=[
                pltpu.VMEM((lanes_v, depth), F32),
                pltpu.VMEM((depth, lanes_v), F32),
            ],
        ),
        out_shape=[
            jax.ShapeDtypeStruct((total, lanes_v), F32),
            jax.ShapeDtypeStruct((total, lanes_v), BF),
            jax.ShapeDtypeStruct((1, lanes_v), F32),
            *[jax.ShapeDtypeStruct(shape, BF) for shape in blocks],
        ],
        compiler_params=params(),
        cost_estimate=cost(total, depth, lanes_v, 0.01),
    )(lengths, hid, cot, gate, gg, mixed, stats, gain)


def run_backward(starts, depth, xin, dtp, dmix, dgate, sin, wv, ws, wg, taps, heads, skip):
    count = starts.shape[0]
    lanes_v, lanes_x = skip.shape[1], taps.shape[1]
    total = xin.shape[0]
    per = STRETCH // HALO

    def back(width):
        return pl.BlockSpec((STRETCH, width), lambda i, *_: (count - 1 - i, 0))

    return pl.pallas_call(
        backward_kernel,
        grid_spec=pltpu.PrefetchScalarGridSpec(
            num_scalar_prefetch=1,
            grid=(count,),
            in_specs=[
                back(lanes_x),
                pl.BlockSpec(
                    (HALO, lanes_x), lambda i, *_: (jnp.maximum((count - 1 - i) * per - 1, 0), 0)
                ),
                back(LANES),
                back(lanes_v),
                back(lanes_v),
                pl.BlockSpec((1, N, lanes_v), lambda i, *_: (count - 1 - i, 0, 0)),
                full((depth, wv.shape[1])),
                full((depth, ws.shape[1])),
                full((depth, lanes_v)),
                full(taps.shape),
                full(heads.shape),
                full(skip.shape),
                full((LANES, lanes_v)),
                full((LANES, 2 * lanes_v)),
            ],
            out_specs=[
                back(depth),
                back(lanes_v),
                back(2 * N + LANES),
                full((8, lanes_x)),
                full((8, LANES)),
                full((1, lanes_v)),
            ],
            scratch_shapes=[
                pltpu.VMEM((N, lanes_v), F32),
                pltpu.VMEM((STRETCH + HALO, lanes_x), F32),
                pltpu.VMEM((STRETCH + HALO, lanes_x), F32),
                pltpu.VMEM((STRETCH, lanes_x), F32),
                pltpu.VMEM((STRETCH, STRETCH), F32),
                pltpu.VMEM((STRETCH, STRETCH), F32),
                pltpu.VMEM((2, STRETCH, STRETCH), F32),
                pltpu.VMEM((2, STRETCH, STRETCH), BF),
                pltpu.VMEM((LANES, STRETCH), F32),
                pltpu.VMEM((STRETCH, LANES), F32),
                pltpu.VMEM((STRETCH, 2 * lanes_v), F32),
                pltpu.VMEM((STRETCH, lanes_v), F32),
            ],
        ),
        out_shape=[
            jax.ShapeDtypeStruct((total, depth), BF),
            jax.ShapeDtypeStruct((total, lanes_v), BF),
            jax.ShapeDtypeStruct((total, 2 * N + LANES), BF),
            jax.ShapeDtypeStruct((8, lanes_x), F32),
            jax.ShapeDtypeStruct((8, LANES), F32),
            jax.ShapeDtypeStruct((1, lanes_v), F32),
        ],
        compiler_params=params(),
        cost_estimate=cost(total, depth, lanes_v, 0.01),
    )(starts, xin, xin, dtp, dmix, dgate, sin, wv, ws, wg, taps, heads, skip, *spreaders(lanes_v))


def relay_blocks(part, axis):
    count, place = lax.axis_size(axis), lax.axis_index(axis)
    got = []
    right, left = part, part
    for k in range(1, count):
        right = lax.ppermute(right, axis, [(i, i + 1) for i in range(count - 1)])
        left = lax.ppermute(left, axis, [(i + 1, i) for i in range(count - 1)])
        got.append((right, jnp.where(place >= k, place - k, count)))
        got.append((left, jnp.where(place + k < count, place + k, count)))
    return got


def rotation(block, axis, k):
    count = lax.axis_size(axis)
    return lax.ppermute(block, axis, [(i, (i + k) % count) for i in range(count)])


def direct_blocks(part, axis):
    count, place = lax.axis_size(axis), lax.axis_index(axis)
    return [(rotation(part, axis, k), lax.rem(place + count - k, count)) for k in range(1, count)]


def exchanged_sum(blocks, axis):
    total = blocks[0].astype(F32)
    for k in range(1, len(blocks)):
        total = total + rotation(blocks[k], axis, k).astype(F32)
    return total


def assembled(part, got, axis, after=None):
    count, place = lax.axis_size(axis), lax.axis_index(axis)
    rows = part.shape[0]
    start = (0,) * (part.ndim - 1)
    blocks = [part] + [block for block, _ in got]
    places = [place] + [at for _, at in got]
    if after is not None:
        blocks, _ = lax.optimization_barrier((blocks, after))
    whole = jnp.zeros(((count + 1) * rows, *part.shape[1:]), part.dtype)
    for block, at in zip(blocks, places):
        whole = lax.dynamic_update_slice(whole, block, (at * rows, *start))
    return whole


def stacked(rows, width):
    return jnp.concatenate([rows[:, q : q + width] for q in range(0, rows.shape[1], width)], axis=0)


def rows_kernel(outer_h, gate, values, shared, weight, gain, grad_out, norm_out):
    inner, rows, lanes_v = gate.shape
    width = lanes_v // outer_h
    per = lanes_v // P_SIZE // outer_h
    total = jnp.zeros((rows, 1), F32)

    def put(low, part):
        grad_out[:, low : low + part.shape[1]] = part
        old = weight[:, low : low + part.shape[1]].astype(F32)
        return jnp.sum(old * part, axis=1, keepdims=True)

    for base, got in ((0, gate), (DI, values)):
        for f in range(inner):
            for z in range(outer_h):
                part = got[f, :, z * width : (z + 1) * width].astype(F32)
                total = total + put(base + (z * inner + f) * width, part)
    common = jnp.zeros((rows, 2 * N), F32)
    steps = jnp.zeros((rows, H), F32)
    source = lax.broadcasted_iota(jnp.int32, (LANES, H), 0)
    target = lax.broadcasted_iota(jnp.int32, (LANES, H), 1)
    for f in range(inner):
        common = common + shared[f, :, : 2 * N].astype(F32)
        spot = ((source // per) * inner + f) * per + source % per
        chosen = jnp.logical_and(spot == target, source < per * outer_h)
        steps = steps + mm(shared[f, :, 2 * N :], chosen.astype(F32).astype(BF))
    total = total + put(2 * DI, common) + put(2 * DI + 2 * N, steps)
    norm_out[...] = jnp.broadcast_to(total / gain[...], norm_out.shape)


def run_rows(outer_h, gate, values, shared, weight, gain):
    rows, width = weight.shape
    return pl.pallas_call(
        functools.partial(rows_kernel, outer_h),
        out_shape=[
            jax.ShapeDtypeStruct((rows, width), F32),
            jax.ShapeDtypeStruct((rows, LANES), F32),
        ],
        compiler_params=pltpu.CompilerParams(vmem_limit_bytes=VMEM_BYTES),
    )(gate, values, shared, weight, gain)


def body(
    hidden,
    out_cotangent,
    norm_gain,
    in_weight,
    conv_weight,
    conv_bias,
    step_bias,
    decay_log,
    skip_gain,
    gate_gain,
    out_weight,
    stretch_len,
    stretch_start,
):
    outer, inner = lax.axis_size("dp"), lax.axis_size("fsdp")
    place = lax.axis_index("fsdp")
    local_heads = H // inner
    lanes_v = local_heads * P_SIZE
    lanes_x = lanes_v + 2 * N
    rows_w = in_weight.shape[0]
    rows_o = out_weight.shape[0]
    depth = hidden.shape[1]
    strided = rows_o % P_SIZE == 0
    outer_h = outer if strided else 1

    def by_place(whole, axis, unit):
        shape = whole.shape
        cut = (*shape[:axis], outer_h, inner, local_heads // outer_h * unit, *shape[axis + 1 :])
        parts = jnp.moveaxis(whole.reshape(cut), axis + 1, 0)
        return parts.reshape(inner, *shape[:axis], local_heads * unit, *shape[axis + 1 :])

    def from_places(parts, axis, unit):
        shape = parts.shape[1:]
        cut = (inner, *shape[:axis], outer_h, local_heads // outer_h * unit, *shape[axis + 1 :])
        whole = jnp.moveaxis(parts.reshape(cut), 0, axis + 1)
        return whole.reshape(*shape[:axis], H * unit, *shape[axis + 1 :])

    def own(whole, axis, unit):
        return lax.dynamic_index_in_dim(by_place(whole, axis, unit), place, 0, False)

    wide = CONV - 2 * N
    hid = lax.all_gather(hidden, "fsdp", axis=0, tiled=True)

    shared_width = 2 * N + H
    gains = (norm_gain, gate_gain)
    small = (
        conv_weight,
        conv_bias,
        step_bias,
        decay_log,
        skip_gain,
        stretch_len.astype(BF),
        stretch_start.astype(BF),
    )

    def in_rows(arrays):
        flat = jnp.concatenate([a.reshape(-1) for a in arrays])
        rows = -(-flat.shape[0] // shared_width)
        return jnp.pad(flat, (0, rows * shared_width - flat.shape[0])).reshape(rows, shared_width)

    gain_rows, small_rows = in_rows(gains), in_rows(small)
    block = jnp.concatenate([in_weight[:, DI + wide :], gain_rows, small_rows], axis=0)
    height = -(-block.shape[0] // 16) * 16
    block = jnp.pad(block, ((0, height - block.shape[0]), (0, 0)))
    along = assembled(block, direct_blocks(block, "dp"), "dp")[: outer * height]
    along = jnp.broadcast_to(along[None], (inner, *along.shape))
    common = lax.all_to_all(along, "fsdp", 0, 0, tiled=True)
    common = common.reshape(inner, outer, height, shared_width)

    wv = lax.all_to_all(by_place(in_weight[:, DI : DI + wide], 1, P_SIZE), "fsdp", 0, 0, tiled=True)
    wv = wv.reshape(inner * rows_w, lanes_v)
    wg = lax.all_to_all(by_place(in_weight[:, :DI], 1, P_SIZE), "fsdp", 0, 0, tiled=True)
    wg = wg.reshape(inner * rows_w, lanes_v)
    cot, _ = lax.optimization_barrier((out_cotangent, wv))
    cot = lax.all_gather(cot, "fsdp", axis=0, tiled=True)
    wv_got = relay_blocks(wv, "dp")
    late = max(len(wv_got) - 4, 0)
    if strided:
        later = jnp.concatenate([wg, stacked(out_weight, lanes_v)], axis=0)
    else:
        later = wg
    later, _ = lax.optimization_barrier((later, wv_got[late : late + 2]))
    later_got = direct_blocks(later, "dp")
    wv = assembled(wv, wv_got, "dp")

    rows_all = jnp.swapaxes(common[:, :, :rows_w], 0, 1).reshape(depth, shared_width)
    head_of = np.arange(H).reshape(outer_h, inner, local_heads // outer_h)
    order = jnp.asarray(np.swapaxes(head_of, 0, 1).reshape(inner, local_heads))
    mine = lax.dynamic_index_in_dim(order, place, 0, False)
    pick = (jnp.arange(H)[:, None] == mine[None, :]).astype(BF)
    pick = jnp.pad(pick, ((0, 0), (0, LANES - local_heads)))
    ws = jnp.concatenate([rows_all[:, : 2 * N], mm(rows_all[:, 2 * N :], pick).astype(BF)], axis=1)

    def out_of_rows(rows, arrays):
        flat = rows.reshape(*rows.shape[:-2], -1).astype(F32)
        parts, low = [], 0
        for a in arrays:
            size = math.prod(a.shape)
            parts.append(flat[..., low : low + size])
            low += size
        return parts

    at = rows_w + gain_rows.shape[0]
    norm_part, gate_part = out_of_rows(common[:, :, rows_w:at], gains)
    norm_full = jnp.swapaxes(norm_part, 0, 1).reshape(-1)
    gate_full = jnp.swapaxes(gate_part, 0, 1).reshape(-1)
    same = lax.dynamic_index_in_dim(common, lax.axis_index("dp"), 1, False)
    pieces = out_of_rows(same[:, at : at + small_rows.shape[0]], small)
    conv_full = pieces[0].reshape(CONV, TAPS)
    bias_full = pieces[1].reshape(CONV)
    per_head = [own(a.reshape(H), 0, 1) for a in pieces[2:5]]
    lengths = pieces[5].reshape(-1).astype(jnp.int32)
    starts = pieces[6].reshape(-1).astype(jnp.int32)

    gain_own = own(gate_full, 0, P_SIZE)[None, :]
    taps_all = jnp.concatenate([conv_full.T, bias_full[None, :]], axis=0)
    taps = jnp.concatenate([own(taps_all[:, :wide], 1, P_SIZE), taps_all[:, wide:]], axis=1)
    taps = jnp.pad(taps, ((0, 8 - (TAPS + 1)), (0, 0)))
    heads = jnp.stack([per_head[0], -jnp.exp(per_head[1])])
    heads = jnp.pad(heads, ((0, 6), (0, LANES - local_heads)))
    skip = jnp.repeat(per_head[2], P_SIZE)[None, :]

    u, xin, dtp, mixed, sin = run_forward(
        starts, hid, norm_full[None, :], wv, ws, taps, heads, skip
    )
    later = assembled(later, later_got, "dp", mixed)
    if strided:
        both = later.reshape(outer + 1, -1, lanes_v)[:outer]
        wg = both[:, : inner * rows_w].reshape(depth, lanes_v)
        ow = jnp.swapaxes(both[:, inner * rows_w :].reshape(outer, -1, rows_o, lanes_v), 1, 2)
        ow = ow.reshape(outer * rows_o, depth)
    else:
        wg = later
        ow = own(lax.all_gather(out_weight, ("dp", "fsdp"), axis=0, tiled=True), 0, P_SIZE)

    branch, gate, squares = run_gate(u, wg, ow, mixed, gain_own)
    gg, along = run_pull(lengths, cot, ow, gate, mixed, gain_own)
    stats = lax.psum(jnp.concatenate([squares[0:1], along[0:1]], axis=0), "fsdp")
    r = lax.rsqrt(stats[0] / DI + EPSILON)
    m = r * stats[1] / DI
    table = jnp.pad(jnp.stack([r, m], axis=1), ((0, 0), (0, LANES - 2)))
    branch = lax.psum_scatter(branch, "fsdp", scatter_dimension=0, tiled=True)

    dmix, dgate, ggg, *blocks = run_gate_back(
        lengths, lax.axis_index("dp"), outer, strided, u, cot, gate, gg, mixed, table, gain_own
    )
    weight_sum = exchanged_sum(blocks[:outer], "dp")
    iwg_gate = weight_sum[: depth // outer].astype(BF)
    if strided:
        out_weight_grad = weight_sum[depth // outer :].reshape(-1, rows_o, lanes_v)
        out_weight_grad = jnp.swapaxes(out_weight_grad, 0, 1).reshape(rows_o, depth)
    else:
        rows = lax.dynamic_update_slice_in_dim(
            jnp.zeros((DI, depth), BF), blocks[outer], place * lanes_v, 0
        )
        out_weight_grad = lax.psum_scatter(rows, ("dp", "fsdp"), scatter_dimension=0, tiled=True)
        out_weight_grad = out_weight_grad.astype(F32)

    def to_rows(mine):
        mine = mine.reshape(inner, rows_w, mine.shape[1])
        return lax.all_to_all(mine, "fsdp", 0, 0, tiled=True)


    f, gpv, gps, conv_sums, head_sums, skip_sums = run_backward(
        starts, depth, xin, dtp, dmix, dgate, sin, wv, ws, wg, taps, heads, skip
    )
    skip_part = jnp.sum(skip_sums.reshape(local_heads, P_SIZE), axis=1)
    parts = (
        conv_sums[: TAPS + 1, :lanes_v].reshape(-1),
        conv_sums[: TAPS + 1, lanes_v:].reshape(-1),
        head_sums[0:2, :local_heads].reshape(-1),
        skip_part,
        ggg.reshape(-1),
    )
    counts = [a.shape[0] for a in parts]
    bundle = jnp.concatenate(parts)
    bundle = jnp.pad(bundle, (0, -bundle.shape[0] % (8 * LANES))).reshape(-1, LANES)
    f, branch, out_weight_grad, iwg_gate, bundle = lax.optimization_barrier(
        (f, branch, out_weight_grad, iwg_gate, bundle)
    )
    f = lax.psum_scatter(f, "fsdp", scatter_dimension=0, tiled=True)
    def by_rows(grad):
        rows = depth // outer
        place_z = lax.axis_index("dp")
        blocks = [
            lax.dynamic_slice_in_dim(grad, lax.rem(place_z + k, outer) * rows, rows, 0)
            for k in range(outer)
        ]
        return blocks[:1] + [rotation(blocks[k], "dp", k) for k in range(1, outer)]

    def row_sum(got):
        return sum(a.astype(F32) for a in got).astype(BF)

    iwg_values = by_rows(mm_tn(u, gpv).astype(BF))
    gate_rows = to_rows(iwg_gate)
    if outer > 1:
        gps, gate_rows, iwg_values[1] = lax.optimization_barrier((gps, gate_rows, iwg_values[1]))
    iwg_shared = by_rows(mm_tn(u, gps).astype(BF))
    value_rows, shared_rows = to_rows(row_sum(iwg_values)), to_rows(row_sum(iwg_shared))
    in_weight_grad, norm_rows = run_rows(
        outer_h, gate_rows, value_rows, shared_rows, in_weight, norm_gain.astype(F32)[:, None]
    )
    norm_gain_grad = norm_rows[:, 0]

    total = hidden.shape[0]
    r_own = lax.dynamic_slice_in_dim(r, place * total, total, 0)
    len_here = jnp.repeat(stretch_len, STRETCH)
    alive = (jnp.arange(total) % STRETCH < len_here).astype(F32)
    rows_float = hidden.astype(F32)
    rs_own = lax.rsqrt(jnp.mean(rows_float * rows_float, axis=1, keepdims=True) + EPSILON)
    block_out = (rows_float + (alive * r_own)[:, None] * branch.astype(F32)).astype(BF)
    unit = rows_float * rs_own
    scaled = f.astype(F32) * norm_full[None, :]
    hidden_grad = out_cotangent.astype(F32) + rs_own * (
        scaled - unit * jnp.mean(scaled * unit, axis=1, keepdims=True)
    )

    bundle = exchanged_sum([bundle] * outer, "dp")
    bundle = jnp.broadcast_to(bundle[None], (inner, *bundle.shape))
    bundle = lax.all_to_all(bundle, "fsdp", 0, 0, tiled=True).reshape(inner, -1)
    stops = [sum(counts[: i + 1]) for i in range(len(counts))]
    cuts = [bundle[:, stop - size : stop] for stop, size in zip(stops, counts)]
    conv_values = from_places(cuts[0].reshape(inner, TAPS + 1, lanes_v), 1, P_SIZE)
    conv_shared = jnp.sum(cuts[1].reshape(inner, TAPS + 1, 2 * N), axis=0)
    conv_all = jnp.concatenate([conv_values, conv_shared], axis=1)
    conv_mine = lax.dynamic_slice_in_dim(
        conv_all, place * conv_weight.shape[0], conv_weight.shape[0], 1
    )
    conv_weight_grad = conv_mine[:TAPS].T
    conv_bias_grad = conv_mine[TAPS]

    def heads_mine(parts_h, size):
        whole = from_places(parts_h, 0, 1)
        return lax.dynamic_slice_in_dim(whole, place * size, size, 0)

    pair_sums = cuts[2].reshape(inner, 2, local_heads)
    step_bias_grad = heads_mine(pair_sums[:, 0], step_bias.shape[0])
    decay_log_grad = heads_mine(pair_sums[:, 1], decay_log.shape[0])
    skip_gain_grad = heads_mine(cuts[3], skip_gain.shape[0])
    gate_all = from_places(cuts[4], 0, P_SIZE)
    flat = lax.axis_index("dp") * inner + place
    gate_gain_grad = lax.dynamic_slice_in_dim(
        gate_all, flat * gate_gain.shape[0], gate_gain.shape[0], 0
    )
    return (
        block_out,
        hidden_grad,
        norm_gain_grad,
        in_weight_grad,
        conv_weight_grad,
        conv_bias_grad,
        step_bias_grad,
        decay_log_grad,
        skip_gain_grad,
        gate_gain_grad,
        out_weight_grad,
    )


def solution(mesh):
    both = P(("dp", "fsdp"))
    rows = P(("dp", "fsdp"), None)
    one = P("fsdp")
    return jax.shard_map(
        body,
        mesh=mesh,
        in_specs=(rows, rows, both, rows, P("fsdp", None), one, one, one, one, both, rows, both, both),
        out_specs=(rows, rows, both, rows, P("fsdp", None), one, one, one, one, both, rows),
        check_vma=False,
    )
```

```python
import functools
import math

import jax
import jax.numpy as jnp
import numpy as np
from jax import lax
from jax.experimental import pallas as pl
from jax.experimental.pallas import tpu as pltpu
from jax.sharding import PartitionSpec as P

H = 64
P_SIZE = 64
N = 128
TAPS = 4
STRETCH = 256
DI = 4096
CONV = 4352
LANES = 128
HALO = 8

EPSILON = 1e-05
BF = jnp.bfloat16
F32 = jnp.float32
VMEM_BYTES = 58 * 1024 * 1024
NEGATIVE = -1e30
PACK = 32
WIDE = 2 * STRETCH
ROWS = 32
HALF = 128


def mm(a, b):
    return lax.dot_general(a, b, (((1,), (0,)), ((), ())), preferred_element_type=F32)


def mm_nt(a, b):
    return lax.dot_general(a, b, (((1,), (1,)), ((), ())), preferred_element_type=F32)


def mm_tn(a, b):
    return lax.dot_general(a, b, (((0,), (0,)), ((), ())), preferred_element_type=F32)


def mm_exact(a, b):
    return lax.dot_general(
        a, b, (((1,), (0,)), ((), ())), precision=lax.Precision.HIGHEST, preferred_element_type=F32
    )


def mm_nt_exact(a, b):
    return lax.dot_general(
        a, b, (((1,), (1,)), ((), ())), precision=lax.Precision.HIGHEST, preferred_element_type=F32
    )


def sigmoid(v):
    return 1.0 / (1.0 + jnp.exp(-v))


def softplus(v):
    return jnp.maximum(v, 0.0) + jnp.log1p(jnp.exp(-jnp.abs(v)))


def half_mask(rows):
    return lax.broadcasted_iota(jnp.int32, (rows, LANES), 1) < P_SIZE


def convolved(ext, taps):
    out = taps[TAPS : TAPS + 1, :]
    for j in range(TAPS):
        low = HALO - (TAPS - 1) + j
        out = out + ext[low : low + STRETCH, :] * taps[j : j + 1, :]
    return out


def three_parts(table, heads_here):
    lane = lax.broadcasted_iota(jnp.int32, table.shape, 1)
    table = jnp.where(lane < heads_here, table, 0.0)
    high = table.astype(BF).astype(F32)
    rest = table - high
    middle = rest.astype(BF).astype(F32)
    low = rest - middle
    packed = high + pltpu.roll(middle, PACK, 1) + pltpu.roll(low, 2 * PACK, 1)
    return packed.astype(BF)


def spreader(heads_here, width):
    source = np.arange(LANES)
    head = np.where(source < 3 * PACK, source % PACK, heads_here)
    return jnp.asarray(head[:, None] == np.arange(heads_here * width)[None, :] // width, BF)


def split_sum(ones, table, heads_here):
    lane = lax.broadcasted_iota(jnp.int32, table.shape, 1)
    got = mm(ones.astype(F32).astype(BF), three_parts(table, heads_here))
    got = got + pltpu.roll(got, LANES - PACK, 1) + pltpu.roll(got, LANES - 2 * PACK, 1)
    return jnp.where(lane < heads_here, got, 0.0)


def lower_ones():
    rows = lax.broadcasted_iota(jnp.int32, (STRETCH, STRETCH), 0)
    cols = lax.broadcasted_iota(jnp.int32, (STRETCH, STRETCH), 1)
    return rows, cols


def forward_kernel(
    starts, hid, gain, wv, ws, taps, heads, skip, to_pairs, to_lanes, u_out, xin_out, dtp_out, mixed_out, sin_out, state, ext,
    scores, mixing, columns, steps,
):
    step_id = pl.program_id(0)
    lanes_v = skip.shape[1]
    rows_in = hid[...]
    wide = rows_in.astype(F32)
    square = jnp.sum(wide * wide, axis=1, keepdims=True)
    rs = lax.rsqrt(square / rows_in.shape[1] + EPSILON)
    u = (wide * rs * gain[...]).astype(BF)
    u_out[...] = u
    from_values = mm(u, wv[...])
    from_shared = mm(u, ws[...])
    xin_out[:, :lanes_v] = from_values
    xin_out[:, lanes_v:] = from_shared[:, : 2 * N]
    dtp_out[...] = from_shared[:, 2 * N :] + heads[0:1, :]
    for half in range(2):
        part = pl.ds(half * STRETCH, STRETCH)
        forward_stretch(
            starts[2 * step_id + half] > 0,
            half,
            taps,
            heads,
            skip,
            to_pairs,
            to_lanes,
            xin_out.at[part, :],
            dtp_out.at[part, :],
            mixed_out.at[part, :],
            sin_out,
            state,
            ext,
            scores,
            mixing,
            columns,
            steps,
        )


def forward_stretch(
    fresh,
    half,
    taps,
    heads,
    skip,
    to_pairs,
    to_lanes,
    xin,
    dtp_in,
    mixed_out,
    sin_out,
    state,
    ext,
    scores,
    mixing,
    columns,
    steps,
):
    lanes_v = skip.shape[1]
    halo = ext[pl.ds(STRETCH, HALO), :]
    ext[pl.ds(0, HALO), :] = jnp.where(fresh, 0.0, halo)
    ext[pl.ds(HALO, STRETCH), :] = xin[...]
    dtp = dtp_in[...]
    pre = convolved(ext, taps)
    act = pre * sigmoid(pre)
    values = act[:, :lanes_v]
    written = act[:, lanes_v : lanes_v + N].astype(BF)
    readout = act[:, lanes_v + N :].astype(BF)
    step = softplus(dtp)
    rows, cols = lower_ones()
    causal = rows >= cols
    decay = split_sum(causal, step * heads[1:2, :], lanes_v // P_SIZE)
    decay_t = decay.T
    before = jnp.where(fresh, 0.0, state[...])
    sin_out[half] = before
    scores[...] = mm_nt(readout, written)
    columns[...] = mm(three_parts(decay, lanes_v // P_SIZE), to_lanes[...])
    steps[...] = mm(three_parts(step, lanes_v // P_SIZE), to_pairs[...])
    read_rest = (act[:, lanes_v + N :] - readout.astype(F32)).astype(BF)
    before_high = before.astype(BF)
    before_rest = (before - before_high.astype(F32)).astype(BF)
    carried = mm(
        jnp.concatenate([readout, read_rest], axis=1),
        jnp.concatenate([before_high, before_high], axis=0),
    ) + mm(readout, before_rest)
    written_t = act[:, lanes_v : lanes_v + N].T.astype(BF)
    left = half_mask(STRETCH)
    for pair in range(lanes_v // LANES):
        lo = pair * LANES
        v = values[:, lo : lo + LANES]
        step_pair = steps[:, lo : lo + LANES]
        decay_pair = jnp.where(
            left, columns[:, 2 * lo : 2 * lo + LANES], columns[:, 2 * lo + LANES : 2 * (lo + LANES)]
        )
        last_pair = decay_pair[STRETCH - 1 :, :]
        sv_wide = v * step_pair
        sv = sv_wide.astype(BF)
        out = jnp.exp(decay_pair) * carried[:, lo : lo + LANES] + skip[:, lo : lo + LANES] * v
        top, bottom = out[:HALF], out[HALF:]
        for j in range(2):
            h = 2 * pair + j
            for r in range(0, STRETCH, ROWS):
                column = columns[r : r + ROWS, h * HALF : (h + 1) * HALF]
                for t in range(0, HALF if r < HALF else STRETCH, HALF):
                    gap = column - decay_t[h : h + 1, t : t + HALF]
                    if t + HALF > r:
                        gap = jnp.where(block_mask(r, t), gap, NEGATIVE)
                    block = scores[r : r + ROWS, t : t + HALF] * jnp.exp(gap)
                    mixing[j, r : r + ROWS, t : t + HALF] = block.astype(BF)
            mine = left if j == 0 else jnp.logical_not(left)
            sv_mine = jnp.where(mine, sv, jnp.zeros_like(sv))
            top = top + mm(mixing[j, :HALF, :HALF], sv_mine[:HALF])
            bottom = bottom + mm(mixing[j, HALF:, :], sv_mine)
        mixed_out[:HALF, lo : lo + LANES] = top
        mixed_out[HALF:, lo : lo + LANES] = bottom
        tv = (sv_wide * jnp.exp(last_pair - decay_pair)).astype(BF)
        state[:, lo : lo + LANES] = jnp.exp(last_pair) * before[:, lo : lo + LANES] + mm(
            written_t, tv
        )


def block_mask(r, t):
    rows = lax.broadcasted_iota(jnp.int32, (ROWS, HALF), 0) + r
    cols = lax.broadcasted_iota(jnp.int32, (ROWS, HALF), 1) + t
    return rows >= cols


def block_mask_t(r, t):
    rows = lax.broadcasted_iota(jnp.int32, (ROWS, HALF), 0) + r
    cols = lax.broadcasted_iota(jnp.int32, (ROWS, HALF), 1) + t
    return rows <= cols


def live_rows(block, lengths, c):
    row = lax.broadcasted_iota(jnp.int32, (WIDE, 1), 0)
    limit = jnp.where(row < STRETCH, lengths[2 * c], STRETCH + lengths[2 * c + 1])
    return jnp.where(row < limit, block, jnp.zeros_like(block))


def column_rows(column):
    wide = jnp.broadcast_to(column, (column.shape[0], LANES))
    return wide.T[0:8, :]


def gate_kernel(u, wg, ow, mixed, gain, branch_out, gate_out, squares_out):
    gate = mm(u[...], wg[...])
    gate_out[...] = gate
    gated = mixed[...] * gate * sigmoid(gate)
    branch_out[...] = mm((gated * gain[...]).astype(BF), ow[...]).astype(BF)
    squares_out[...] = column_rows(jnp.sum(gated * gated, axis=1, keepdims=True))


def pull_kernel(lengths, cot, ow, gate, mixed, gain, gg_out, along_out):
    c = pl.program_id(0)
    cotangent = live_rows(cot[...], lengths, c)
    gg = mm_nt(cotangent, ow[...])
    gg_out[...] = gg
    gated = mixed[...] * gate[...] * sigmoid(gate[...])
    along_out[...] = column_rows(jnp.sum(gg * gain[...] * gated, axis=1, keepdims=True))


def gate_back_kernel(
    outer,
    lengths,
    hid,
    cot,
    gate,
    gg,
    mixed,
    stats,
    gain,
    dmix_out,
    dgate_out,
    ggg_out,
    *rest,
):
    c = pl.program_id(0)
    outs, (owg, iwg) = rest[:-2], rest[-2:]
    count = pl.num_programs(0)
    r = stats[:, 0:1]
    m = stats[:, 1:2]
    v = gate[...]
    s = sigmoid(v)
    silu = v * s
    mix = mixed[...]
    normed = mix * silu * r
    back = gg[...]
    dgated = r * (back * gain[...] - normed * m)
    dmix_out[...] = dgated * silu
    dgate = dgated * mix * (s * (1.0 + v * (1.0 - s)))
    dgate_low = dgate.astype(BF)
    dgate_out[...] = dgate_low
    cotangent = live_rows(cot[...], lengths, c)
    owg_part = mm_tn((normed * gain[...]).astype(BF), cotangent)
    iwg_part = mm_tn(hid[...], dgate_low)
    ggg_part = jnp.sum(back * normed, axis=0, keepdims=True)

    @pl.when(c == 0)
    def _():
        owg[...] = owg_part
        iwg[...] = iwg_part
        ggg_out[...] = ggg_part

    @pl.when(c > 0)
    def _():
        owg[...] += owg_part
        iwg[...] += iwg_part
        ggg_out[...] += ggg_part

    @pl.when(c == pl.num_programs(0) - 1)
    def _():
        rows, cols = iwg.shape[0] // outer, iwg.shape[1]
        for k in range(outer):
            spot = lax.rem(lengths[2 * count] + k, outer)
            low = pl.multiple_of(spot * rows, 16)
            outs[k][:rows, :] = iwg[pl.ds(low, rows), :].astype(BF)
            if len(outs) == outer:
                high = owg.shape[0] // outer
                low = pl.multiple_of(spot * high, 16)
                for q in range(owg.shape[1] // cols):
                    part = owg[pl.ds(low, high), q * cols : (q + 1) * cols]
                    outs[k][rows + q * high : rows + (q + 1) * high, :] = part.astype(BF)
        if len(outs) > outer:
            outs[outer][...] = owg[...].astype(BF)


def backward_kernel(
    starts,
    xin,
    xprev,
    dtp_in,
    dmix,
    dgate,
    sin,
    wv,
    ws,
    wg,
    taps,
    heads,
    skip,
    to_pairs,
    to_lanes,
    f_out,
    gpv_out,
    gps_out,
    conv_out,
    head_out,
    skip_out,
    dstate,
    ext,
    gext,
    gbuf,
    scores,
    dscores,
    dmixing,
    mixing,
    row_sums,
    col_sums,
    columns,
    steps,
):
    step_id = pl.program_id(0)
    count = pl.num_programs(0)
    c = count - 1 - step_id
    fresh = starts[c] > 0
    lanes_v = skip.shape[1]
    lanes_x = taps.shape[1]
    first = step_id == 0
    next_fresh = jnp.logical_or(first, starts[jnp.minimum(c + 1, count - 1)] > 0)

    ext[pl.ds(0, HALO), :] = jnp.where(fresh, 0.0, xprev[...])
    ext[pl.ds(HALO, STRETCH), :] = xin[...]
    pre = convolved(ext, taps)
    sig = sigmoid(pre)
    act = pre * sig
    values = act[:, :lanes_v]
    written_f = act[:, lanes_v : lanes_v + N]
    readout_f = act[:, lanes_v + N :]
    written = written_f.astype(BF)
    readout = readout_f.astype(BF)
    dtp = dtp_in[...]
    step = softplus(dtp)
    rate = heads[1:2, :]
    rows, cols = lower_ones()
    causal = rows >= cols
    anti = rows <= cols
    decay = split_sum(causal, step * rate, lanes_v // P_SIZE)
    decay_t = decay.T
    last = decay[STRETCH - 1 : STRETCH, :]
    grow_last = jnp.exp(last)
    before = sin[0]
    before_low = before.astype(BF)
    after = jnp.where(next_fresh, 0.0, dstate[...])
    after_low = after.astype(BF)
    scores[...] = mm_nt(written, readout)
    columns[...] = mm(three_parts(decay, lanes_v // P_SIZE), to_lanes[...])
    steps[...] = mm(three_parts(step, lanes_v // P_SIZE), to_pairs[...])
    carried = mm(readout, before_low)
    spread = mm(written, after_low)
    readout_t = readout_f.T.astype(BF)
    left = half_mask(STRETCH)
    left_row = half_mask(1)
    lane = lax.broadcasted_iota(jnp.int32, (STRETCH, LANES), 1)
    lane_row = lax.broadcasted_iota(jnp.int32, (1, LANES), 1)
    row_sums[...] = jnp.zeros_like(row_sums)
    lane_rows = lax.broadcasted_iota(jnp.int32, (ROWS, LANES), 1)
    within = jnp.zeros((STRETCH, LANES), F32)
    inner = jnp.zeros((STRETCH, LANES), F32)
    direct = jnp.zeros((STRETCH, LANES), F32)
    through = jnp.zeros((1, LANES), F32)
    dwritten = jnp.zeros((STRETCH, N), F32)
    dreadout = jnp.zeros((STRETCH, N), F32)
    for pair in range(lanes_v // LANES):
        lo = pair * LANES
        v = values[:, lo : lo + LANES]
        dy = dmix[:, lo : lo + LANES]
        step_pair = steps[:, lo : lo + LANES]
        decay_pair = jnp.where(
            left, columns[:, 2 * lo : 2 * lo + LANES], columns[:, 2 * lo + LANES : 2 * (lo + LANES)]
        )
        last_pair = decay_pair[STRETCH - 1 :, :]
        fall_pair = jnp.exp(last_pair - decay_pair)
        sv = v * step_pair
        sv_low = sv.astype(BF)
        dy_low = dy.astype(BF)
        q = fall_pair * spread[:, lo : lo + LANES]
        flow = sv * q
        grown = dy * jnp.exp(decay_pair)
        enter = grown * carried[:, lo : lo + LANES]
        top, bottom = q[:HALF], q[HALF:]
        for j in range(2):
            h = 2 * pair + j
            mine = left if j == 0 else jnp.logical_not(left)
            low_mine = jnp.where(mine, dy_low, jnp.zeros_like(dy_low))
            dmixing[j, :HALF, :] = mm_nt(sv_low[:HALF], low_mine)
            dmixing[j, HALF:, HALF:] = mm_nt(sv_low[HALF:], low_mine[HALF:])
            sums = [jnp.zeros((8, HALF), F32), jnp.zeros((8, HALF), F32)]
            for r in range(0, STRETCH, ROWS):
                column = columns[r : r + ROWS, h * HALF : (h + 1) * HALF]
                across = jnp.zeros((ROWS, HALF), F32)
                for t in range(0 if r < HALF else HALF, STRETCH, HALF):
                    gap = decay_t[h : h + 1, t : t + HALF] - column
                    if t < r + ROWS:
                        gap = jnp.where(block_mask_t(r, t), gap, NEGATIVE)
                    kernel = jnp.exp(gap)
                    block = scores[r : r + ROWS, t : t + HALF] * kernel
                    back = dmixing[j, r : r + ROWS, t : t + HALF]
                    mixing[j, r : r + ROWS, t : t + HALF] = block.astype(BF)
                    turned = kernel * back
                    if h:
                        turned = turned + dscores[r : r + ROWS, t : t + HALF]
                    dscores[r : r + ROWS, t : t + HALF] = turned
                    edges = block * back
                    across = across + edges
                    for k in range(0, ROWS, 8):
                        sums[t // HALF] = sums[t // HALF] + edges[k : k + 8]
                total = jnp.sum(across, axis=1, keepdims=True)
                old = col_sums[r : r + ROWS, :] if h else jnp.zeros((ROWS, LANES), F32)
                col_sums[r : r + ROWS, :] = jnp.where(lane_rows == h, total, old)
            row_sums[h : h + 1, :HALF] = jnp.sum(sums[0], axis=0, keepdims=True)
            row_sums[h : h + 1, HALF:] = jnp.sum(sums[1], axis=0, keepdims=True)
            top = top + mm(mixing[j, :HALF, :], low_mine)
            bottom = bottom + mm(mixing[j, HALF:, HALF:], low_mine[HALF:])
            zero = jnp.zeros_like(flow)
            within = jnp.where(
                lane == h, jnp.sum(jnp.where(mine, flow, zero), axis=1, keepdims=True), within
            )
            inner = jnp.where(
                lane == h, jnp.sum(jnp.where(mine, enter, zero), axis=1, keepdims=True), inner
            )
        q = jnp.concatenate([top, bottom], axis=0)
        vq = v * q
        cross = jnp.sum(
            before[:, lo : lo + LANES] * after[:, lo : lo + LANES], axis=0, keepdims=True
        )
        for j in range(2):
            h = 2 * pair + j
            mine = left if j == 0 else jnp.logical_not(left)
            mine_row = left_row if j == 0 else jnp.logical_not(left_row)
            direct = jnp.where(
                lane == h, jnp.sum(jnp.where(mine, vq, 0.0), axis=1, keepdims=True), direct
            )
            through = jnp.where(
                lane_row == h,
                jnp.sum(jnp.where(mine_row, cross, 0.0), axis=1, keepdims=True),
                through,
            )
        gbuf[:, lo : lo + LANES] = step_pair * q + skip[:, lo : lo + LANES] * dy
        skip_part = jnp.sum(dy * v, axis=0, keepdims=True)
        skip_out[0:1, lo : lo + LANES] = skip_part + jnp.where(
            first, 0.0, skip_out[0:1, lo : lo + LANES]
        )
        tv = (sv * fall_pair).astype(BF)
        grown_low = grown.astype(BF)
        dwritten = dwritten + mm_nt(tv, after_low[:, lo : lo + LANES])
        dreadout = dreadout + mm_nt_exact(grown, before[:, lo : lo + LANES])
        dstate[:, lo : lo + LANES] = jnp.exp(last_pair) * after[
            :, lo : lo + LANES
        ] + mm(readout_t, grown_low)
    low_top = dscores[:HALF, :].astype(BF)
    low_bottom = dscores[HALF:, HALF:].astype(BF)
    gbuf[:HALF, lanes_v : lanes_v + N] = dwritten[:HALF] + mm(low_top, readout)
    gbuf[HALF:, lanes_v : lanes_v + N] = dwritten[HALF:] + mm(low_bottom, readout[HALF:])
    turned_left = dscores[:HALF, :HALF].T.astype(BF)
    turned_right = dscores[:HALF, HALF:].T.astype(BF)
    turned_low = dscores[HALF:, HALF:].T.astype(BF)
    gbuf[:HALF, lanes_v + N :] = dreadout[:HALF] + mm(turned_left, written[:HALF])
    gbuf[HALF:, lanes_v + N :] = (
        dreadout[HALF:] + mm(turned_right, written[:HALF]) + mm(turned_low, written[HALF:])
    )

    suffix = row_sums[...].T - col_sums[...] + inner
    grad_a = (
        split_sum(anti, suffix, lanes_v // P_SIZE)
        + split_sum(rows > cols, within, lanes_v // P_SIZE)
        + grow_last * through
    )
    grad_step = direct + rate * grad_a
    grad_raw = grad_step * sigmoid(dtp)
    decay_part = jnp.sum(grad_a * step, axis=0, keepdims=True) * rate
    bias_part = jnp.sum(grad_raw, axis=0, keepdims=True)
    head_row = lax.broadcasted_iota(jnp.int32, (8, LANES), 0)
    head_part = jnp.where(head_row == 0, bias_part, jnp.where(head_row == 1, decay_part, 0.0))

    grad_pre = gbuf[...] * (sig * (1.0 + pre * (1.0 - sig)))
    gext[pl.ds(STRETCH, HALO), :] = jnp.where(next_fresh, 0.0, gext[pl.ds(0, HALO), :])
    gext[pl.ds(0, STRETCH), :] = grad_pre
    grad_in = grad_pre * taps[TAPS - 1 : TAPS, :]
    for j in range(TAPS - 1):
        up = TAPS - 1 - j
        grad_in = grad_in + gext[pl.ds(up, STRETCH), :] * taps[j : j + 1, :]
    conv_row = lax.broadcasted_iota(jnp.int32, (8, lanes_x), 0)
    conv_part = jnp.where(conv_row == TAPS, jnp.sum(grad_pre, axis=0, keepdims=True), 0.0)
    for j in range(TAPS):
        low = HALO - (TAPS - 1) + j
        conv_part = jnp.where(
            conv_row == j,
            jnp.sum(grad_pre * ext[pl.ds(low, STRETCH), :], axis=0, keepdims=True),
            conv_part,
        )
    conv_out[...] = conv_part + jnp.where(first, 0.0, conv_out[...])
    head_out[...] = head_part + jnp.where(first, 0.0, head_out[...])

    grad_in_low = grad_in.astype(BF)
    grad_raw_low = grad_raw.astype(BF)
    f = mm_nt(dgate[...], wg[...])
    f = f + mm_nt(grad_in_low[:, :lanes_v], wv[...])
    f = f + mm_nt(grad_in_low[:, lanes_v:], ws[:, : 2 * N])
    f = f + mm_nt(grad_raw_low, ws[:, 2 * N :])
    f_out[...] = f.astype(BF)
    gpv_out[...] = grad_in_low[:, :lanes_v]
    gps_out[:, : 2 * N] = grad_in_low[:, lanes_v:]
    gps_out[:, 2 * N :] = grad_raw_low


def full(shape):
    return pl.BlockSpec(shape, lambda c, *_: (0,) * len(shape))


def blocks_of(width):
    return pl.BlockSpec((WIDE, width), lambda c, *_: (c, 0))


def tokens(width):
    return pl.BlockSpec((STRETCH, width), lambda c, *_: (c, 0))


def cost(total, depth, lanes, passes):
    return pl.CostEstimate(
        flops=int(2 * total * depth * lanes * passes), bytes_accessed=0, transcendentals=0
    )


def params(name_limit=VMEM_BYTES):
    return pltpu.CompilerParams(
        dimension_semantics=("arbitrary",), vmem_limit_bytes=name_limit
    )


def spreaders(lanes_v):
    heads_here = lanes_v // P_SIZE
    return spreader(heads_here, P_SIZE), spreader(heads_here, LANES)


def run_forward(starts, hid, gain, wv, ws, taps, heads, skip):
    count, depth = starts.shape[0], hid.shape[1]
    lanes_v, lanes_x = skip.shape[1], taps.shape[1]
    total = hid.shape[0]
    return pl.pallas_call(
        forward_kernel,
        grid_spec=pltpu.PrefetchScalarGridSpec(
            num_scalar_prefetch=1,
            grid=(count // 2,),
            in_specs=[
                blocks_of(depth),
                full(gain.shape),
                full((depth, wv.shape[1])),
                full((depth, ws.shape[1])),
                full(taps.shape),
                full(heads.shape),
                full(skip.shape),
                full((LANES, lanes_v)),
                full((LANES, 2 * lanes_v)),
            ],
            out_specs=[
                blocks_of(depth),
                blocks_of(lanes_x),
                blocks_of(LANES),
                blocks_of(lanes_v),
                pl.BlockSpec((2, N, lanes_v), lambda c, *_: (c, 0, 0)),
            ],
            scratch_shapes=[
                pltpu.VMEM((N, lanes_v), F32),
                pltpu.VMEM((STRETCH + HALO, lanes_x), F32),
                pltpu.VMEM((STRETCH, STRETCH), F32),
                pltpu.VMEM((2, STRETCH, STRETCH), BF),
                pltpu.VMEM((STRETCH, 2 * lanes_v), F32),
                pltpu.VMEM((STRETCH, lanes_v), F32),
            ],
        ),
        out_shape=[
            jax.ShapeDtypeStruct((total, depth), BF),
            jax.ShapeDtypeStruct((total, lanes_x), F32),
            jax.ShapeDtypeStruct((total, LANES), F32),
            jax.ShapeDtypeStruct((total, lanes_v), F32),
            jax.ShapeDtypeStruct((count, N, lanes_v), F32),
        ],
        compiler_params=params(),
        cost_estimate=cost(total, depth, lanes_v, 6),
    )(starts, hid, gain, wv, ws, taps, heads, skip, *spreaders(lanes_v))


def run_gate(u, wg, ow, mixed, gain):
    depth = u.shape[1]
    total, lanes_v = mixed.shape
    return pl.pallas_call(
        gate_kernel,
        grid=(total // WIDE,),
        in_specs=[
            blocks_of(depth),
            full((depth, lanes_v)),
            full((lanes_v, depth)),
            blocks_of(lanes_v),
            full(gain.shape),
        ],
        out_specs=[
            blocks_of(depth),
            blocks_of(lanes_v),
            pl.BlockSpec((8, WIDE), lambda c, *_: (0, c)),
        ],
        out_shape=[
            jax.ShapeDtypeStruct((total, depth), BF),
            jax.ShapeDtypeStruct((total, lanes_v), F32),
            jax.ShapeDtypeStruct((8, total), F32),
        ],
        compiler_params=params(),
        cost_estimate=cost(total, depth, lanes_v, 1),
    )(u, wg, ow, mixed, gain)


def run_pull(lengths, cot, ow, gate, mixed, gain):
    count, depth = lengths.shape[0], cot.shape[1]
    total, lanes_v = mixed.shape
    return pl.pallas_call(
        pull_kernel,
        grid_spec=pltpu.PrefetchScalarGridSpec(
            num_scalar_prefetch=1,
            grid=(count // 2,),
            in_specs=[
                blocks_of(depth),
                full((lanes_v, depth)),
                blocks_of(lanes_v),
                blocks_of(lanes_v),
                full(gain.shape),
            ],
            out_specs=[blocks_of(lanes_v), pl.BlockSpec((8, WIDE), lambda c, *_: (0, c))],
        ),
        out_shape=[
            jax.ShapeDtypeStruct((total, lanes_v), F32),
            jax.ShapeDtypeStruct((8, total), F32),
        ],
        compiler_params=params(),
        cost_estimate=cost(total, depth, lanes_v, 0.01),
    )(lengths, cot, ow, gate, mixed, gain)


def run_gate_back(lengths, place, outer, strided, hid, cot, gate, gg, mixed, stats, gain):
    count, depth = lengths.shape[0], hid.shape[1]
    total, lanes_v = mixed.shape
    lengths = jnp.concatenate([lengths, place[None]])
    if strided:
        blocks = [(2 * depth // outer, lanes_v)] * outer
    else:
        blocks = [(depth // outer, lanes_v)] * outer + [(lanes_v, depth)]
    return pl.pallas_call(
        functools.partial(gate_back_kernel, outer),
        grid_spec=pltpu.PrefetchScalarGridSpec(
            num_scalar_prefetch=1,
            grid=(count // 2,),
            in_specs=[
                blocks_of(depth),
                blocks_of(depth),
                blocks_of(lanes_v),
                blocks_of(lanes_v),
                blocks_of(lanes_v),
                blocks_of(LANES),
                full(gain.shape),
            ],
            out_specs=[
                blocks_of(lanes_v),
                blocks_of(lanes_v),
                full((1, lanes_v)),
                *[full(shape) for shape in blocks],
            ],
            scratch_shapes=[
                pltpu.VMEM((lanes_v, depth), F32),
                pltpu.VMEM((depth, lanes_v), F32),
            ],
        ),
        out_shape=[
            jax.ShapeDtypeStruct((total, lanes_v), F32),
            jax.ShapeDtypeStruct((total, lanes_v), BF),
            jax.ShapeDtypeStruct((1, lanes_v), F32),
            *[jax.ShapeDtypeStruct(shape, BF) for shape in blocks],
        ],
        compiler_params=params(),
        cost_estimate=cost(total, depth, lanes_v, 0.01),
    )(lengths, hid, cot, gate, gg, mixed, stats, gain)


def run_backward(starts, depth, xin, dtp, dmix, dgate, sin, wv, ws, wg, taps, heads, skip):
    count = starts.shape[0]
    lanes_v, lanes_x = skip.shape[1], taps.shape[1]
    total = xin.shape[0]
    per = STRETCH // HALO

    def back(width):
        return pl.BlockSpec((STRETCH, width), lambda i, *_: (count - 1 - i, 0))

    return pl.pallas_call(
        backward_kernel,
        grid_spec=pltpu.PrefetchScalarGridSpec(
            num_scalar_prefetch=1,
            grid=(count,),
            in_specs=[
                back(lanes_x),
                pl.BlockSpec(
                    (HALO, lanes_x), lambda i, *_: (jnp.maximum((count - 1 - i) * per - 1, 0), 0)
                ),
                back(LANES),
                back(lanes_v),
                back(lanes_v),
                pl.BlockSpec((1, N, lanes_v), lambda i, *_: (count - 1 - i, 0, 0)),
                full((depth, wv.shape[1])),
                full((depth, ws.shape[1])),
                full((depth, lanes_v)),
                full(taps.shape),
                full(heads.shape),
                full(skip.shape),
                full((LANES, lanes_v)),
                full((LANES, 2 * lanes_v)),
            ],
            out_specs=[
                back(depth),
                back(lanes_v),
                back(2 * N + LANES),
                full((8, lanes_x)),
                full((8, LANES)),
                full((1, lanes_v)),
            ],
            scratch_shapes=[
                pltpu.VMEM((N, lanes_v), F32),
                pltpu.VMEM((STRETCH + HALO, lanes_x), F32),
                pltpu.VMEM((STRETCH + HALO, lanes_x), F32),
                pltpu.VMEM((STRETCH, lanes_x), F32),
                pltpu.VMEM((STRETCH, STRETCH), F32),
                pltpu.VMEM((STRETCH, STRETCH), F32),
                pltpu.VMEM((2, STRETCH, STRETCH), F32),
                pltpu.VMEM((2, STRETCH, STRETCH), BF),
                pltpu.VMEM((LANES, STRETCH), F32),
                pltpu.VMEM((STRETCH, LANES), F32),
                pltpu.VMEM((STRETCH, 2 * lanes_v), F32),
                pltpu.VMEM((STRETCH, lanes_v), F32),
            ],
        ),
        out_shape=[
            jax.ShapeDtypeStruct((total, depth), BF),
            jax.ShapeDtypeStruct((total, lanes_v), BF),
            jax.ShapeDtypeStruct((total, 2 * N + LANES), BF),
            jax.ShapeDtypeStruct((8, lanes_x), F32),
            jax.ShapeDtypeStruct((8, LANES), F32),
            jax.ShapeDtypeStruct((1, lanes_v), F32),
        ],
        compiler_params=params(),
        cost_estimate=cost(total, depth, lanes_v, 0.01),
    )(starts, xin, xin, dtp, dmix, dgate, sin, wv, ws, wg, taps, heads, skip, *spreaders(lanes_v))


def relay_blocks(part, axis):
    count, place = lax.axis_size(axis), lax.axis_index(axis)
    got = []
    right, left = part, part
    for k in range(1, count):
        right = lax.ppermute(right, axis, [(i, i + 1) for i in range(count - 1)])
        left = lax.ppermute(left, axis, [(i + 1, i) for i in range(count - 1)])
        got.append((right, jnp.where(place >= k, place - k, count)))
        got.append((left, jnp.where(place + k < count, place + k, count)))
    return got


def rotation(block, axis, k):
    count = lax.axis_size(axis)
    return lax.ppermute(block, axis, [(i, (i + k) % count) for i in range(count)])


def direct_blocks(part, axis):
    count, place = lax.axis_size(axis), lax.axis_index(axis)
    return [(rotation(part, axis, k), lax.rem(place + count - k, count)) for k in range(1, count)]


def exchanged_sum(blocks, axis):
    total = blocks[0].astype(F32)
    for k in range(1, len(blocks)):
        total = total + rotation(blocks[k], axis, k).astype(F32)
    return total


def assembled(part, got, axis, after=None):
    count, place = lax.axis_size(axis), lax.axis_index(axis)
    rows = part.shape[0]
    start = (0,) * (part.ndim - 1)
    blocks = [part] + [block for block, _ in got]
    places = [place] + [at for _, at in got]
    if after is not None:
        blocks, _ = lax.optimization_barrier((blocks, after))
    whole = jnp.zeros(((count + 1) * rows, *part.shape[1:]), part.dtype)
    for block, at in zip(blocks, places):
        whole = lax.dynamic_update_slice(whole, block, (at * rows, *start))
    return whole


def rows_kernel(outer_h, gate, values, shared, weight, gain, grad_out, norm_out):
    inner, rows, lanes_v = gate.shape
    width = lanes_v // outer_h
    per = lanes_v // P_SIZE // outer_h
    total = jnp.zeros((rows, 1), F32)

    def put(low, part):
        grad_out[:, low : low + part.shape[1]] = part
        old = weight[:, low : low + part.shape[1]].astype(F32)
        return jnp.sum(old * part, axis=1, keepdims=True)

    for base, got in ((0, gate), (DI, values)):
        for f in range(inner):
            for z in range(outer_h):
                part = got[f, :, z * width : (z + 1) * width].astype(F32)
                total = total + put(base + (z * inner + f) * width, part)
    common = jnp.zeros((rows, 2 * N), F32)
    steps = jnp.zeros((rows, H), F32)
    source = lax.broadcasted_iota(jnp.int32, (LANES, H), 0)
    target = lax.broadcasted_iota(jnp.int32, (LANES, H), 1)
    for f in range(inner):
        common = common + shared[f, :, : 2 * N].astype(F32)
        spot = ((source // per) * inner + f) * per + source % per
        chosen = jnp.logical_and(spot == target, source < per * outer_h)
        steps = steps + mm(shared[f, :, 2 * N :], chosen.astype(F32).astype(BF))
    total = total + put(2 * DI, common) + put(2 * DI + 2 * N, steps)
    norm_out[...] = jnp.broadcast_to(total / gain[...], norm_out.shape)


def run_rows(outer_h, gate, values, shared, weight, gain):
    rows, width = weight.shape
    return pl.pallas_call(
        functools.partial(rows_kernel, outer_h),
        out_shape=[
            jax.ShapeDtypeStruct((rows, width), F32),
            jax.ShapeDtypeStruct((rows, LANES), F32),
        ],
        compiler_params=pltpu.CompilerParams(vmem_limit_bytes=VMEM_BYTES),
    )(gate, values, shared, weight, gain)


def body(
    hidden,
    out_cotangent,
    norm_gain,
    in_weight,
    conv_weight,
    conv_bias,
    step_bias,
    decay_log,
    skip_gain,
    gate_gain,
    out_weight,
    stretch_len,
    stretch_start,
):
    outer, inner = lax.axis_size("dp"), lax.axis_size("fsdp")
    place = lax.axis_index("fsdp")
    local_heads = H // inner
    lanes_v = local_heads * P_SIZE
    lanes_x = lanes_v + 2 * N
    rows_w = in_weight.shape[0]
    rows_o = out_weight.shape[0]
    depth = hidden.shape[1]
    strided = rows_o % P_SIZE == 0
    outer_h = outer if strided else 1

    def by_place(whole, axis, unit):
        shape = whole.shape
        cut = (*shape[:axis], outer_h, inner, local_heads // outer_h * unit, *shape[axis + 1 :])
        parts = jnp.moveaxis(whole.reshape(cut), axis + 1, 0)
        return parts.reshape(inner, *shape[:axis], local_heads * unit, *shape[axis + 1 :])

    def from_places(parts, axis, unit):
        shape = parts.shape[1:]
        cut = (inner, *shape[:axis], outer_h, local_heads // outer_h * unit, *shape[axis + 1 :])
        whole = jnp.moveaxis(parts.reshape(cut), 0, axis + 1)
        return whole.reshape(*shape[:axis], H * unit, *shape[axis + 1 :])

    def own(whole, axis, unit):
        return lax.dynamic_index_in_dim(by_place(whole, axis, unit), place, 0, False)

    wide = CONV - 2 * N
    hid = lax.all_gather(hidden, "fsdp", axis=0, tiled=True)

    shared_width = 2 * N + H
    gains = (norm_gain, gate_gain)
    small = (
        conv_weight,
        conv_bias,
        step_bias,
        decay_log,
        skip_gain,
        stretch_len.astype(BF),
        stretch_start.astype(BF),
    )

    def in_rows(arrays):
        flat = jnp.concatenate([a.reshape(-1) for a in arrays])
        rows = -(-flat.shape[0] // shared_width)
        return jnp.pad(flat, (0, rows * shared_width - flat.shape[0])).reshape(rows, shared_width)

    gain_rows, small_rows = in_rows(gains), in_rows(small)
    block = jnp.concatenate([in_weight[:, DI + wide :], gain_rows, small_rows], axis=0)
    height = -(-block.shape[0] // 16) * 16
    block = jnp.pad(block, ((0, height - block.shape[0]), (0, 0)))
    along = assembled(block, direct_blocks(block, "dp"), "dp")[: outer * height]
    along = jnp.broadcast_to(along[None], (inner, *along.shape))
    common = lax.all_to_all(along, "fsdp", 0, 0, tiled=True)
    common = common.reshape(inner, outer, height, shared_width)

    wv = lax.all_to_all(by_place(in_weight[:, DI : DI + wide], 1, P_SIZE), "fsdp", 0, 0, tiled=True)
    wv = wv.reshape(inner * rows_w, lanes_v)
    wg = lax.all_to_all(by_place(in_weight[:, :DI], 1, P_SIZE), "fsdp", 0, 0, tiled=True)
    wg = wg.reshape(inner * rows_w, lanes_v)
    cot, _ = lax.optimization_barrier((out_cotangent, wv))
    cot = lax.all_gather(cot, "fsdp", axis=0, tiled=True)
    if strided:
        ow_got = direct_blocks(out_weight, "dp")
        wv, ow_got = lax.optimization_barrier((wv, ow_got))
    wv_got = relay_blocks(wv, "dp")
    late = max(len(wv_got) - 2, 0)
    wg, _ = lax.optimization_barrier((wg, wv_got[late : late + 2]))
    wg_got = direct_blocks(wg, "dp")
    wv = assembled(wv, wv_got, "dp")

    rows_all = jnp.swapaxes(common[:, :, :rows_w], 0, 1).reshape(depth, shared_width)
    head_of = np.arange(H).reshape(outer_h, inner, local_heads // outer_h)
    order = jnp.asarray(np.swapaxes(head_of, 0, 1).reshape(inner, local_heads))
    mine = lax.dynamic_index_in_dim(order, place, 0, False)
    pick = (jnp.arange(H)[:, None] == mine[None, :]).astype(BF)
    pick = jnp.pad(pick, ((0, 0), (0, LANES - local_heads)))
    ws = jnp.concatenate([rows_all[:, : 2 * N], mm(rows_all[:, 2 * N :], pick).astype(BF)], axis=1)

    def out_of_rows(rows, arrays):
        flat = rows.reshape(*rows.shape[:-2], -1).astype(F32)
        parts, low = [], 0
        for a in arrays:
            size = math.prod(a.shape)
            parts.append(flat[..., low : low + size])
            low += size
        return parts

    at = rows_w + gain_rows.shape[0]
    norm_part, gate_part = out_of_rows(common[:, :, rows_w:at], gains)
    norm_full = jnp.swapaxes(norm_part, 0, 1).reshape(-1)
    gate_full = jnp.swapaxes(gate_part, 0, 1).reshape(-1)
    same = lax.dynamic_index_in_dim(common, lax.axis_index("dp"), 1, False)
    pieces = out_of_rows(same[:, at : at + small_rows.shape[0]], small)
    conv_full = pieces[0].reshape(CONV, TAPS)
    bias_full = pieces[1].reshape(CONV)
    per_head = [own(a.reshape(H), 0, 1) for a in pieces[2:5]]
    lengths = pieces[5].reshape(-1).astype(jnp.int32)
    starts = pieces[6].reshape(-1).astype(jnp.int32)

    gain_own = own(gate_full, 0, P_SIZE)[None, :]
    taps_all = jnp.concatenate([conv_full.T, bias_full[None, :]], axis=0)
    taps = jnp.concatenate([own(taps_all[:, :wide], 1, P_SIZE), taps_all[:, wide:]], axis=1)
    taps = jnp.pad(taps, ((0, 8 - (TAPS + 1)), (0, 0)))
    heads = jnp.stack([per_head[0], -jnp.exp(per_head[1])])
    heads = jnp.pad(heads, ((0, 6), (0, LANES - local_heads)))
    skip = jnp.repeat(per_head[2], P_SIZE)[None, :]

    u, xin, dtp, mixed, sin = run_forward(
        starts, hid, norm_full[None, :], wv, ws, taps, heads, skip
    )
    wg = assembled(wg, wg_got, "dp", mixed)
    if strided:
        ow = assembled(out_weight, ow_got, "dp")
    else:
        ow = own(lax.all_gather(out_weight, ("dp", "fsdp"), axis=0, tiled=True), 0, P_SIZE)

    branch, gate, squares = run_gate(u, wg, ow, mixed, gain_own)
    gg, along = run_pull(lengths, cot, ow, gate, mixed, gain_own)
    stats = lax.psum(jnp.concatenate([squares[0:1], along[0:1]], axis=0), "fsdp")
    r = lax.rsqrt(stats[0] / DI + EPSILON)
    m = r * stats[1] / DI
    table = jnp.pad(jnp.stack([r, m], axis=1), ((0, 0), (0, LANES - 2)))
    branch = lax.psum_scatter(branch, "fsdp", scatter_dimension=0, tiled=True)

    dmix, dgate, ggg, *blocks = run_gate_back(
        lengths, lax.axis_index("dp"), outer, strided, u, cot, gate, gg, mixed, table, gain_own
    )
    weight_sum = exchanged_sum(blocks[:outer], "dp")
    iwg_gate = weight_sum[: depth // outer].astype(BF)
    if strided:
        out_weight_grad = weight_sum[depth // outer :].reshape(-1, rows_o, lanes_v)
        out_weight_grad = jnp.swapaxes(out_weight_grad, 0, 1).reshape(rows_o, depth)
    else:
        rows = lax.dynamic_update_slice_in_dim(
            jnp.zeros((DI, depth), BF), blocks[outer], place * lanes_v, 0
        )
        out_weight_grad = lax.psum_scatter(rows, ("dp", "fsdp"), scatter_dimension=0, tiled=True)
        out_weight_grad = out_weight_grad.astype(F32)

    def to_rows(mine):
        mine = mine.reshape(inner, rows_w, mine.shape[1])
        return lax.all_to_all(mine, "fsdp", 0, 0, tiled=True)


    f, gpv, gps, conv_sums, head_sums, skip_sums = run_backward(
        starts, depth, xin, dtp, dmix, dgate, sin, wv, ws, wg, taps, heads, skip
    )
    skip_part = jnp.sum(skip_sums.reshape(local_heads, P_SIZE), axis=1)
    parts = (
        conv_sums[: TAPS + 1, :lanes_v].reshape(-1),
        conv_sums[: TAPS + 1, lanes_v:].reshape(-1),
        head_sums[0:2, :local_heads].reshape(-1),
        skip_part,
        ggg.reshape(-1),
    )
    counts = [a.shape[0] for a in parts]
    bundle = jnp.concatenate(parts)
    bundle = jnp.pad(bundle, (0, -bundle.shape[0] % (8 * LANES))).reshape(-1, LANES)
    f, branch, out_weight_grad, iwg_gate, bundle = lax.optimization_barrier(
        (f, branch, out_weight_grad, iwg_gate, bundle)
    )
    f = lax.psum_scatter(f, "fsdp", scatter_dimension=0, tiled=True)
    def by_rows(grad):
        rows = depth // outer
        place_z = lax.axis_index("dp")
        blocks = [
            lax.dynamic_slice_in_dim(grad, lax.rem(place_z + k, outer) * rows, rows, 0)
            for k in range(outer)
        ]
        return blocks

    def passed_on(blocks):
        return blocks[:1] + [rotation(blocks[k], "dp", k) for k in range(1, outer)]

    def row_sum(got):
        return sum(a.astype(F32) for a in got).astype(BF)

    iwg_values = by_rows(mm_tn(u, gpv).astype(BF))
    gate_rows = to_rows(iwg_gate)
    iwg_values = passed_on(iwg_values)
    if outer > 1:
        gps, gate_rows, iwg_values[1] = lax.optimization_barrier((gps, gate_rows, iwg_values[1]))
    iwg_shared = passed_on(by_rows(mm_tn(u, gps).astype(BF)))
    value_rows, shared_rows = to_rows(row_sum(iwg_values)), to_rows(row_sum(iwg_shared))
    in_weight_grad, norm_rows = run_rows(
        outer_h, gate_rows, value_rows, shared_rows, in_weight, norm_gain.astype(F32)[:, None]
    )
    norm_gain_grad = norm_rows[:, 0]

    total = hidden.shape[0]
    r_own = lax.dynamic_slice_in_dim(r, place * total, total, 0)
    len_here = jnp.repeat(stretch_len, STRETCH)
    alive = (jnp.arange(total) % STRETCH < len_here).astype(F32)
    rows_float = hidden.astype(F32)
    rs_own = lax.rsqrt(jnp.mean(rows_float * rows_float, axis=1, keepdims=True) + EPSILON)
    block_out = (rows_float + (alive * r_own)[:, None] * branch.astype(F32)).astype(BF)
    unit = rows_float * rs_own
    scaled = f.astype(F32) * norm_full[None, :]
    hidden_grad = out_cotangent.astype(F32) + rs_own * (
        scaled - unit * jnp.mean(scaled * unit, axis=1, keepdims=True)
    )

    bundle = exchanged_sum([bundle] * outer, "dp")
    bundle = jnp.broadcast_to(bundle[None], (inner, *bundle.shape))
    bundle = lax.all_to_all(bundle, "fsdp", 0, 0, tiled=True).reshape(inner, -1)
    stops = [sum(counts[: i + 1]) for i in range(len(counts))]
    cuts = [bundle[:, stop - size : stop] for stop, size in zip(stops, counts)]
    conv_values = from_places(cuts[0].reshape(inner, TAPS + 1, lanes_v), 1, P_SIZE)
    conv_shared = jnp.sum(cuts[1].reshape(inner, TAPS + 1, 2 * N), axis=0)
    conv_all = jnp.concatenate([conv_values, conv_shared], axis=1)
    conv_mine = lax.dynamic_slice_in_dim(
        conv_all, place * conv_weight.shape[0], conv_weight.shape[0], 1
    )
    conv_weight_grad = conv_mine[:TAPS].T
    conv_bias_grad = conv_mine[TAPS]

    def heads_mine(parts_h, size):
        whole = from_places(parts_h, 0, 1)
        return lax.dynamic_slice_in_dim(whole, place * size, size, 0)

    pair_sums = cuts[2].reshape(inner, 2, local_heads)
    step_bias_grad = heads_mine(pair_sums[:, 0], step_bias.shape[0])
    decay_log_grad = heads_mine(pair_sums[:, 1], decay_log.shape[0])
    skip_gain_grad = heads_mine(cuts[3], skip_gain.shape[0])
    gate_all = from_places(cuts[4], 0, P_SIZE)
    flat = lax.axis_index("dp") * inner + place
    gate_gain_grad = lax.dynamic_slice_in_dim(
        gate_all, flat * gate_gain.shape[0], gate_gain.shape[0], 0
    )
    return (
        block_out,
        hidden_grad,
        norm_gain_grad,
        in_weight_grad,
        conv_weight_grad,
        conv_bias_grad,
        step_bias_grad,
        decay_log_grad,
        skip_gain_grad,
        gate_gain_grad,
        out_weight_grad,
    )


def solution(mesh):
    both = P(("dp", "fsdp"))
    rows = P(("dp", "fsdp"), None)
    one = P("fsdp")
    return jax.shard_map(
        body,
        mesh=mesh,
        in_specs=(rows, rows, both, rows, P("fsdp", None), one, one, one, one, both, rows, both, both),
        out_specs=(rows, rows, both, rows, P("fsdp", None), one, one, one, one, both, rows),
        check_vma=False,
    )
```

```python
import functools
import math

import jax
import jax.numpy as jnp
import numpy as np
from jax import lax
from jax.experimental import pallas as pl
from jax.experimental.pallas import tpu as pltpu
from jax.sharding import PartitionSpec as P

H = 64
P_SIZE = 64
N = 128
TAPS = 4
STRETCH = 256
DI = 4096
CONV = 4352
LANES = 128
HALO = 8

EPSILON = 1e-05
BF = jnp.bfloat16
F32 = jnp.float32
VMEM_BYTES = 58 * 1024 * 1024
NEGATIVE = -1e30
PACK = 32
WIDE = 2 * STRETCH
ROWS = 32
HALF = 128


def mm(a, b):
    return lax.dot_general(a, b, (((1,), (0,)), ((), ())), preferred_element_type=F32)


def mm_nt(a, b):
    return lax.dot_general(a, b, (((1,), (1,)), ((), ())), preferred_element_type=F32)


def mm_tn(a, b):
    return lax.dot_general(a, b, (((0,), (0,)), ((), ())), preferred_element_type=F32)


def mm_exact(a, b):
    return lax.dot_general(
        a, b, (((1,), (0,)), ((), ())), precision=lax.Precision.HIGHEST, preferred_element_type=F32
    )


def mm_nt_exact(a, b):
    return lax.dot_general(
        a, b, (((1,), (1,)), ((), ())), precision=lax.Precision.HIGHEST, preferred_element_type=F32
    )


def sigmoid(v):
    return 1.0 / (1.0 + jnp.exp(-v))


def softplus(v):
    return jnp.maximum(v, 0.0) + jnp.log1p(jnp.exp(-jnp.abs(v)))


def half_mask(rows):
    return lax.broadcasted_iota(jnp.int32, (rows, LANES), 1) < P_SIZE


def convolved(ext, taps):
    out = taps[TAPS : TAPS + 1, :]
    for j in range(TAPS):
        low = HALO - (TAPS - 1) + j
        out = out + ext[low : low + STRETCH, :] * taps[j : j + 1, :]
    return out


def three_parts(table, heads_here):
    lane = lax.broadcasted_iota(jnp.int32, table.shape, 1)
    table = jnp.where(lane < heads_here, table, 0.0)
    high = table.astype(BF).astype(F32)
    rest = table - high
    middle = rest.astype(BF).astype(F32)
    low = rest - middle
    packed = high + pltpu.roll(middle, PACK, 1) + pltpu.roll(low, 2 * PACK, 1)
    return packed.astype(BF)


def spreader(heads_here, width):
    source = np.arange(LANES)
    head = np.where(source < 3 * PACK, source % PACK, heads_here)
    return jnp.asarray(head[:, None] == np.arange(heads_here * width)[None, :] // width, BF)


def split_sum(ones, table, heads_here):
    lane = lax.broadcasted_iota(jnp.int32, table.shape, 1)
    got = mm(ones.astype(F32).astype(BF), three_parts(table, heads_here))
    got = got + pltpu.roll(got, LANES - PACK, 1) + pltpu.roll(got, LANES - 2 * PACK, 1)
    return jnp.where(lane < heads_here, got, 0.0)


def lower_ones():
    rows = lax.broadcasted_iota(jnp.int32, (STRETCH, STRETCH), 0)
    cols = lax.broadcasted_iota(jnp.int32, (STRETCH, STRETCH), 1)
    return rows, cols


def forward_kernel(
    starts, hid, gain, wv, ws, taps, heads, skip, to_pairs, to_lanes, u_out, xin_out, dtp_out, mixed_out, sin_out, state, ext,
    scores, mixing, columns, steps,
):
    step_id = pl.program_id(0)
    lanes_v = skip.shape[1]
    rows_in = hid[...]
    wide = rows_in.astype(F32)
    square = jnp.sum(wide * wide, axis=1, keepdims=True)
    rs = lax.rsqrt(square / rows_in.shape[1] + EPSILON)
    u = (wide * rs * gain[...]).astype(BF)
    u_out[...] = u
    from_values = mm(u, wv[...])
    from_shared = mm(u, ws[...])
    xin_out[:, :lanes_v] = from_values
    xin_out[:, lanes_v:] = from_shared[:, : 2 * N]
    dtp_out[...] = from_shared[:, 2 * N :] + heads[0:1, :]
    for half in range(2):
        part = pl.ds(half * STRETCH, STRETCH)
        forward_stretch(
            starts[2 * step_id + half] > 0,
            half,
            taps,
            heads,
            skip,
            to_pairs,
            to_lanes,
            xin_out.at[part, :],
            dtp_out.at[part, :],
            mixed_out.at[part, :],
            sin_out,
            state,
            ext,
            scores,
            mixing,
            columns,
            steps,
        )


def forward_stretch(
    fresh,
    half,
    taps,
    heads,
    skip,
    to_pairs,
    to_lanes,
    xin,
    dtp_in,
    mixed_out,
    sin_out,
    state,
    ext,
    scores,
    mixing,
    columns,
    steps,
):
    lanes_v = skip.shape[1]
    halo = ext[pl.ds(STRETCH, HALO), :]
    ext[pl.ds(0, HALO), :] = jnp.where(fresh, 0.0, halo)
    ext[pl.ds(HALO, STRETCH), :] = xin[...]
    dtp = dtp_in[...]
    pre = convolved(ext, taps)
    act = pre * sigmoid(pre)
    values = act[:, :lanes_v]
    written = act[:, lanes_v : lanes_v + N].astype(BF)
    readout = act[:, lanes_v + N :].astype(BF)
    step = softplus(dtp)
    rows, cols = lower_ones()
    causal = rows >= cols
    decay = split_sum(causal, step * heads[1:2, :], lanes_v // P_SIZE)
    decay_t = decay.T
    before = jnp.where(fresh, 0.0, state[...])
    sin_out[half] = before
    scores[...] = mm_nt(readout, written)
    columns[...] = mm(three_parts(decay, lanes_v // P_SIZE), to_lanes[...])
    steps[...] = mm(three_parts(step, lanes_v // P_SIZE), to_pairs[...])
    read_rest = (act[:, lanes_v + N :] - readout.astype(F32)).astype(BF)
    before_high = before.astype(BF)
    before_rest = (before - before_high.astype(F32)).astype(BF)
    carried = mm(
        jnp.concatenate([readout, read_rest], axis=1),
        jnp.concatenate([before_high, before_high], axis=0),
    ) + mm(readout, before_rest)
    written_t = act[:, lanes_v : lanes_v + N].T.astype(BF)
    left = half_mask(STRETCH)
    for pair in range(lanes_v // LANES):
        lo = pair * LANES
        v = values[:, lo : lo + LANES]
        step_pair = steps[:, lo : lo + LANES]
        decay_pair = jnp.where(
            left, columns[:, 2 * lo : 2 * lo + LANES], columns[:, 2 * lo + LANES : 2 * (lo + LANES)]
        )
        last_pair = decay_pair[STRETCH - 1 :, :]
        sv_wide = v * step_pair
        sv = sv_wide.astype(BF)
        out = jnp.exp(decay_pair) * carried[:, lo : lo + LANES] + skip[:, lo : lo + LANES] * v
        top, bottom = out[:HALF], out[HALF:]
        for j in range(2):
            h = 2 * pair + j
            for r in range(0, STRETCH, ROWS):
                column = columns[r : r + ROWS, h * HALF : (h + 1) * HALF]
                for t in range(0, HALF if r < HALF else STRETCH, HALF):
                    gap = column - decay_t[h : h + 1, t : t + HALF]
                    if t + HALF > r:
                        gap = jnp.where(block_mask(r, t), gap, NEGATIVE)
                    block = scores[r : r + ROWS, t : t + HALF] * jnp.exp(gap)
                    mixing[j, r : r + ROWS, t : t + HALF] = block.astype(BF)
            mine = left if j == 0 else jnp.logical_not(left)
            sv_mine = jnp.where(mine, sv, jnp.zeros_like(sv))
            top = top + mm(mixing[j, :HALF, :HALF], sv_mine[:HALF])
            bottom = bottom + mm(mixing[j, HALF:, :], sv_mine)
        mixed_out[:HALF, lo : lo + LANES] = top
        mixed_out[HALF:, lo : lo + LANES] = bottom
        tv = (sv_wide * jnp.exp(last_pair - decay_pair)).astype(BF)
        state[:, lo : lo + LANES] = jnp.exp(last_pair) * before[:, lo : lo + LANES] + mm(
            written_t, tv
        )


def block_mask(r, t):
    rows = lax.broadcasted_iota(jnp.int32, (ROWS, HALF), 0) + r
    cols = lax.broadcasted_iota(jnp.int32, (ROWS, HALF), 1) + t
    return rows >= cols


def block_mask_t(r, t):
    rows = lax.broadcasted_iota(jnp.int32, (ROWS, HALF), 0) + r
    cols = lax.broadcasted_iota(jnp.int32, (ROWS, HALF), 1) + t
    return rows <= cols


def live_rows(block, lengths, c):
    row = lax.broadcasted_iota(jnp.int32, (WIDE, 1), 0)
    limit = jnp.where(row < STRETCH, lengths[2 * c], STRETCH + lengths[2 * c + 1])
    return jnp.where(row < limit, block, jnp.zeros_like(block))


def column_rows(column):
    wide = jnp.broadcast_to(column, (column.shape[0], LANES))
    return wide.T[0:8, :]


def gate_kernel(u, wg, ow, mixed, gain, branch_out, gate_out, squares_out):
    gate = mm(u[...], wg[...])
    gate_out[...] = gate
    gated = mixed[...] * gate * sigmoid(gate)
    branch_out[...] = mm((gated * gain[...]).astype(BF), ow[...]).astype(BF)
    squares_out[...] = column_rows(jnp.sum(gated * gated, axis=1, keepdims=True))


def pull_kernel(lengths, cot, ow, gate, mixed, gain, gg_out, along_out):
    c = pl.program_id(0)
    cotangent = live_rows(cot[...], lengths, c)
    gg = mm_nt(cotangent, ow[...])
    gg_out[...] = gg
    gated = mixed[...] * gate[...] * sigmoid(gate[...])
    along_out[...] = column_rows(jnp.sum(gg * gain[...] * gated, axis=1, keepdims=True))


def gate_back_kernel(
    outer,
    lengths,
    hid,
    cot,
    gate,
    gg,
    mixed,
    stats,
    gain,
    dmix_out,
    dgate_out,
    ggg_out,
    *rest,
):
    c = pl.program_id(0)
    outs, (owg, iwg) = rest[:-2], rest[-2:]
    count = pl.num_programs(0)
    r = stats[:, 0:1]
    m = stats[:, 1:2]
    v = gate[...]
    s = sigmoid(v)
    silu = v * s
    mix = mixed[...]
    normed = mix * silu * r
    back = gg[...]
    dgated = r * (back * gain[...] - normed * m)
    dmix_out[...] = dgated * silu
    dgate = dgated * mix * (s * (1.0 + v * (1.0 - s)))
    dgate_low = dgate.astype(BF)
    dgate_out[...] = dgate_low
    cotangent = live_rows(cot[...], lengths, c)
    owg_part = mm_tn((normed * gain[...]).astype(BF), cotangent)
    iwg_part = mm_tn(hid[...], dgate_low)
    ggg_part = jnp.sum(back * normed, axis=0, keepdims=True)

    @pl.when(c == 0)
    def _():
        owg[...] = owg_part
        iwg[...] = iwg_part
        ggg_out[...] = ggg_part

    @pl.when(c > 0)
    def _():
        owg[...] += owg_part
        iwg[...] += iwg_part
        ggg_out[...] += ggg_part

    @pl.when(c == pl.num_programs(0) - 1)
    def _():
        rows, cols = iwg.shape[0] // outer, iwg.shape[1]
        for k in range(outer):
            spot = lax.rem(lengths[2 * count] + k, outer)
            low = pl.multiple_of(spot * rows, 16)
            outs[k][:rows, :] = iwg[pl.ds(low, rows), :].astype(BF)
            if len(outs) == outer:
                high = owg.shape[0] // outer
                low = pl.multiple_of(spot * high, 16)
                for q in range(owg.shape[1] // cols):
                    part = owg[pl.ds(low, high), q * cols : (q + 1) * cols]
                    outs[k][rows + q * high : rows + (q + 1) * high, :] = part.astype(BF)
        if len(outs) > outer:
            outs[outer][...] = owg[...].astype(BF)


def backward_kernel(
    starts,
    xin,
    xprev,
    dtp_in,
    dmix,
    dgate,
    sin,
    wv,
    ws,
    wg,
    taps,
    heads,
    skip,
    to_pairs,
    to_lanes,
    f_out,
    gpv_out,
    gps_out,
    conv_out,
    head_out,
    skip_out,
    dstate,
    ext,
    gext,
    gbuf,
    scores,
    dscores,
    dmixing,
    mixing,
    row_sums,
    col_sums,
    columns,
    steps,
):
    step_id = pl.program_id(0)
    count = pl.num_programs(0)
    c = count - 1 - step_id
    fresh = starts[c] > 0
    lanes_v = skip.shape[1]
    lanes_x = taps.shape[1]
    first = step_id == 0
    next_fresh = jnp.logical_or(first, starts[jnp.minimum(c + 1, count - 1)] > 0)

    ext[pl.ds(0, HALO), :] = jnp.where(fresh, 0.0, xprev[...])
    ext[pl.ds(HALO, STRETCH), :] = xin[...]
    pre = convolved(ext, taps)
    sig = sigmoid(pre)
    act = pre * sig
    values = act[:, :lanes_v]
    written_f = act[:, lanes_v : lanes_v + N]
    readout_f = act[:, lanes_v + N :]
    written = written_f.astype(BF)
    readout = readout_f.astype(BF)
    dtp = dtp_in[...]
    step = softplus(dtp)
    rate = heads[1:2, :]
    rows, cols = lower_ones()
    causal = rows >= cols
    anti = rows <= cols
    decay = split_sum(causal, step * rate, lanes_v // P_SIZE)
    decay_t = decay.T
    last = decay[STRETCH - 1 : STRETCH, :]
    grow_last = jnp.exp(last)
    before = sin[0]
    before_low = before.astype(BF)
    after = jnp.where(next_fresh, 0.0, dstate[...])
    after_low = after.astype(BF)
    scores[...] = mm_nt(written, readout)
    columns[...] = mm(three_parts(decay, lanes_v // P_SIZE), to_lanes[...])
    steps[...] = mm(three_parts(step, lanes_v // P_SIZE), to_pairs[...])
    carried = mm(readout, before_low)
    spread = mm(written, after_low)
    readout_t = readout_f.T.astype(BF)
    left = half_mask(STRETCH)
    left_row = half_mask(1)
    lane = lax.broadcasted_iota(jnp.int32, (STRETCH, LANES), 1)
    lane_row = lax.broadcasted_iota(jnp.int32, (1, LANES), 1)
    row_sums[...] = jnp.zeros_like(row_sums)
    lane_rows = lax.broadcasted_iota(jnp.int32, (ROWS, LANES), 1)
    within = jnp.zeros((STRETCH, LANES), F32)
    inner = jnp.zeros((STRETCH, LANES), F32)
    direct = jnp.zeros((STRETCH, LANES), F32)
    through = jnp.zeros((1, LANES), F32)
    dwritten = jnp.zeros((STRETCH, N), F32)
    dreadout = jnp.zeros((STRETCH, N), F32)
    for pair in range(lanes_v // LANES):
        lo = pair * LANES
        v = values[:, lo : lo + LANES]
        dy = dmix[:, lo : lo + LANES]
        step_pair = steps[:, lo : lo + LANES]
        decay_pair = jnp.where(
            left, columns[:, 2 * lo : 2 * lo + LANES], columns[:, 2 * lo + LANES : 2 * (lo + LANES)]
        )
        last_pair = decay_pair[STRETCH - 1 :, :]
        fall_pair = jnp.exp(last_pair - decay_pair)
        sv = v * step_pair
        sv_low = sv.astype(BF)
        dy_low = dy.astype(BF)
        q = fall_pair * spread[:, lo : lo + LANES]
        flow = sv * q
        grown = dy * jnp.exp(decay_pair)
        enter = grown * carried[:, lo : lo + LANES]
        top, bottom = q[:HALF], q[HALF:]
        for j in range(2):
            h = 2 * pair + j
            mine = left if j == 0 else jnp.logical_not(left)
            low_mine = jnp.where(mine, dy_low, jnp.zeros_like(dy_low))
            dmixing[j, :HALF, :] = mm_nt(sv_low[:HALF], low_mine)
            dmixing[j, HALF:, HALF:] = mm_nt(sv_low[HALF:], low_mine[HALF:])
            sums = [jnp.zeros((8, HALF), F32), jnp.zeros((8, HALF), F32)]
            for r in range(0, STRETCH, ROWS):
                column = columns[r : r + ROWS, h * HALF : (h + 1) * HALF]
                across = jnp.zeros((ROWS, HALF), F32)
                for t in range(0 if r < HALF else HALF, STRETCH, HALF):
                    gap = decay_t[h : h + 1, t : t + HALF] - column
                    if t < r + ROWS:
                        gap = jnp.where(block_mask_t(r, t), gap, NEGATIVE)
                    kernel = jnp.exp(gap)
                    block = scores[r : r + ROWS, t : t + HALF] * kernel
                    back = dmixing[j, r : r + ROWS, t : t + HALF]
                    mixing[j, r : r + ROWS, t : t + HALF] = block.astype(BF)
                    turned = kernel * back
                    if h:
                        turned = turned + dscores[r : r + ROWS, t : t + HALF]
                    dscores[r : r + ROWS, t : t + HALF] = turned
                    edges = block * back
                    across = across + edges
                    for k in range(0, ROWS, 8):
                        sums[t // HALF] = sums[t // HALF] + edges[k : k + 8]
                total = jnp.sum(across, axis=1, keepdims=True)
                old = col_sums[r : r + ROWS, :] if h else jnp.zeros((ROWS, LANES), F32)
                col_sums[r : r + ROWS, :] = jnp.where(lane_rows == h, total, old)
            row_sums[h : h + 1, :HALF] = jnp.sum(sums[0], axis=0, keepdims=True)
            row_sums[h : h + 1, HALF:] = jnp.sum(sums[1], axis=0, keepdims=True)
            top = top + mm(mixing[j, :HALF, :], low_mine)
            bottom = bottom + mm(mixing[j, HALF:, HALF:], low_mine[HALF:])
            zero = jnp.zeros_like(flow)
            within = jnp.where(
                lane == h, jnp.sum(jnp.where(mine, flow, zero), axis=1, keepdims=True), within
            )
            inner = jnp.where(
                lane == h, jnp.sum(jnp.where(mine, enter, zero), axis=1, keepdims=True), inner
            )
        q = jnp.concatenate([top, bottom], axis=0)
        vq = v * q
        cross = jnp.sum(
            before[:, lo : lo + LANES] * after[:, lo : lo + LANES], axis=0, keepdims=True
        )
        for j in range(2):
            h = 2 * pair + j
            mine = left if j == 0 else jnp.logical_not(left)
            mine_row = left_row if j == 0 else jnp.logical_not(left_row)
            direct = jnp.where(
                lane == h, jnp.sum(jnp.where(mine, vq, 0.0), axis=1, keepdims=True), direct
            )
            through = jnp.where(
                lane_row == h,
                jnp.sum(jnp.where(mine_row, cross, 0.0), axis=1, keepdims=True),
                through,
            )
        gbuf[:, lo : lo + LANES] = step_pair * q + skip[:, lo : lo + LANES] * dy
        skip_part = jnp.sum(dy * v, axis=0, keepdims=True)
        skip_out[0:1, lo : lo + LANES] = skip_part + jnp.where(
            first, 0.0, skip_out[0:1, lo : lo + LANES]
        )
        tv = (sv * fall_pair).astype(BF)
        grown_low = grown.astype(BF)
        dwritten = dwritten + mm_nt(tv, after_low[:, lo : lo + LANES])
        dreadout = dreadout + mm_nt_exact(grown, before[:, lo : lo + LANES])
        dstate[:, lo : lo + LANES] = jnp.exp(last_pair) * after[
            :, lo : lo + LANES
        ] + mm(readout_t, grown_low)
    low_top = dscores[:HALF, :].astype(BF)
    low_bottom = dscores[HALF:, HALF:].astype(BF)
    gbuf[:HALF, lanes_v : lanes_v + N] = dwritten[:HALF] + mm(low_top, readout)
    gbuf[HALF:, lanes_v : lanes_v + N] = dwritten[HALF:] + mm(low_bottom, readout[HALF:])
    turned_left = dscores[:HALF, :HALF].T.astype(BF)
    turned_right = dscores[:HALF, HALF:].T.astype(BF)
    turned_low = dscores[HALF:, HALF:].T.astype(BF)
    gbuf[:HALF, lanes_v + N :] = dreadout[:HALF] + mm(turned_left, written[:HALF])
    gbuf[HALF:, lanes_v + N :] = (
        dreadout[HALF:] + mm(turned_right, written[:HALF]) + mm(turned_low, written[HALF:])
    )

    suffix = row_sums[...].T - col_sums[...] + inner
    grad_a = (
        split_sum(anti, suffix, lanes_v // P_SIZE)
        + split_sum(rows > cols, within, lanes_v // P_SIZE)
        + grow_last * through
    )
    grad_step = direct + rate * grad_a
    grad_raw = grad_step * sigmoid(dtp)
    decay_part = jnp.sum(grad_a * step, axis=0, keepdims=True) * rate
    bias_part = jnp.sum(grad_raw, axis=0, keepdims=True)
    head_row = lax.broadcasted_iota(jnp.int32, (8, LANES), 0)
    head_part = jnp.where(head_row == 0, bias_part, jnp.where(head_row == 1, decay_part, 0.0))

    grad_pre = gbuf[...] * (sig * (1.0 + pre * (1.0 - sig)))
    gext[pl.ds(STRETCH, HALO), :] = jnp.where(next_fresh, 0.0, gext[pl.ds(0, HALO), :])
    gext[pl.ds(0, STRETCH), :] = grad_pre
    grad_in = grad_pre * taps[TAPS - 1 : TAPS, :]
    for j in range(TAPS - 1):
        up = TAPS - 1 - j
        grad_in = grad_in + gext[pl.ds(up, STRETCH), :] * taps[j : j + 1, :]
    conv_row = lax.broadcasted_iota(jnp.int32, (8, lanes_x), 0)
    conv_part = jnp.where(conv_row == TAPS, jnp.sum(grad_pre, axis=0, keepdims=True), 0.0)
    for j in range(TAPS):
        low = HALO - (TAPS - 1) + j
        conv_part = jnp.where(
            conv_row == j,
            jnp.sum(grad_pre * ext[pl.ds(low, STRETCH), :], axis=0, keepdims=True),
            conv_part,
        )
    conv_out[...] = conv_part + jnp.where(first, 0.0, conv_out[...])
    head_out[...] = head_part + jnp.where(first, 0.0, head_out[...])

    grad_in_low = grad_in.astype(BF)
    grad_raw_low = grad_raw.astype(BF)
    f = mm_nt(dgate[...], wg[...])
    f = f + mm_nt(grad_in_low[:, :lanes_v], wv[...])
    f = f + mm_nt(grad_in_low[:, lanes_v:], ws[:, : 2 * N])
    f = f + mm_nt(grad_raw_low, ws[:, 2 * N :])
    f_out[...] = f.astype(BF)
    gpv_out[...] = grad_in_low[:, :lanes_v]
    gps_out[:, : 2 * N] = grad_in_low[:, lanes_v:]
    gps_out[:, 2 * N :] = grad_raw_low


def full(shape):
    return pl.BlockSpec(shape, lambda c, *_: (0,) * len(shape))


def blocks_of(width):
    return pl.BlockSpec((WIDE, width), lambda c, *_: (c, 0))


def tokens(width):
    return pl.BlockSpec((STRETCH, width), lambda c, *_: (c, 0))


def cost(total, depth, lanes, passes):
    return pl.CostEstimate(
        flops=int(2 * total * depth * lanes * passes), bytes_accessed=0, transcendentals=0
    )


def params(name_limit=VMEM_BYTES):
    return pltpu.CompilerParams(
        dimension_semantics=("arbitrary",), vmem_limit_bytes=name_limit
    )


def spreaders(lanes_v):
    heads_here = lanes_v // P_SIZE
    return spreader(heads_here, P_SIZE), spreader(heads_here, LANES)


def run_forward(starts, hid, gain, wv, ws, taps, heads, skip):
    count, depth = starts.shape[0], hid.shape[1]
    lanes_v, lanes_x = skip.shape[1], taps.shape[1]
    total = hid.shape[0]
    return pl.pallas_call(
        forward_kernel,
        grid_spec=pltpu.PrefetchScalarGridSpec(
            num_scalar_prefetch=1,
            grid=(count // 2,),
            in_specs=[
                blocks_of(depth),
                full(gain.shape),
                full((depth, wv.shape[1])),
                full((depth, ws.shape[1])),
                full(taps.shape),
                full(heads.shape),
                full(skip.shape),
                full((LANES, lanes_v)),
                full((LANES, 2 * lanes_v)),
            ],
            out_specs=[
                blocks_of(depth),
                blocks_of(lanes_x),
                blocks_of(LANES),
                blocks_of(lanes_v),
                pl.BlockSpec((2, N, lanes_v), lambda c, *_: (c, 0, 0)),
            ],
            scratch_shapes=[
                pltpu.VMEM((N, lanes_v), F32),
                pltpu.VMEM((STRETCH + HALO, lanes_x), F32),
                pltpu.VMEM((STRETCH, STRETCH), F32),
                pltpu.VMEM((2, STRETCH, STRETCH), BF),
                pltpu.VMEM((STRETCH, 2 * lanes_v), F32),
                pltpu.VMEM((STRETCH, lanes_v), F32),
            ],
        ),
        out_shape=[
            jax.ShapeDtypeStruct((total, depth), BF),
            jax.ShapeDtypeStruct((total, lanes_x), F32),
            jax.ShapeDtypeStruct((total, LANES), F32),
            jax.ShapeDtypeStruct((total, lanes_v), F32),
            jax.ShapeDtypeStruct((count, N, lanes_v), F32),
        ],
        compiler_params=params(),
        cost_estimate=cost(total, depth, lanes_v, 6),
    )(starts, hid, gain, wv, ws, taps, heads, skip, *spreaders(lanes_v))


def run_gate(u, wg, ow, mixed, gain):
    depth = u.shape[1]
    total, lanes_v = mixed.shape
    return pl.pallas_call(
        gate_kernel,
        grid=(total // WIDE,),
        in_specs=[
            blocks_of(depth),
            full((depth, lanes_v)),
            full((lanes_v, depth)),
            blocks_of(lanes_v),
            full(gain.shape),
        ],
        out_specs=[
            blocks_of(depth),
            blocks_of(lanes_v),
            pl.BlockSpec((8, WIDE), lambda c, *_: (0, c)),
        ],
        out_shape=[
            jax.ShapeDtypeStruct((total, depth), BF),
            jax.ShapeDtypeStruct((total, lanes_v), F32),
            jax.ShapeDtypeStruct((8, total), F32),
        ],
        compiler_params=params(),
        cost_estimate=cost(total, depth, lanes_v, 1),
    )(u, wg, ow, mixed, gain)


def run_pull(lengths, cot, ow, gate, mixed, gain):
    count, depth = lengths.shape[0], cot.shape[1]
    total, lanes_v = mixed.shape
    return pl.pallas_call(
        pull_kernel,
        grid_spec=pltpu.PrefetchScalarGridSpec(
            num_scalar_prefetch=1,
            grid=(count // 2,),
            in_specs=[
                blocks_of(depth),
                full((lanes_v, depth)),
                blocks_of(lanes_v),
                blocks_of(lanes_v),
                full(gain.shape),
            ],
            out_specs=[blocks_of(lanes_v), pl.BlockSpec((8, WIDE), lambda c, *_: (0, c))],
        ),
        out_shape=[
            jax.ShapeDtypeStruct((total, lanes_v), F32),
            jax.ShapeDtypeStruct((8, total), F32),
        ],
        compiler_params=params(),
        cost_estimate=cost(total, depth, lanes_v, 0.01),
    )(lengths, cot, ow, gate, mixed, gain)


def run_gate_back(lengths, place, outer, strided, hid, cot, gate, gg, mixed, stats, gain):
    count, depth = lengths.shape[0], hid.shape[1]
    total, lanes_v = mixed.shape
    lengths = jnp.concatenate([lengths, place[None]])
    if strided:
        blocks = [(2 * depth // outer, lanes_v)] * outer
    else:
        blocks = [(depth // outer, lanes_v)] * outer + [(lanes_v, depth)]
    return pl.pallas_call(
        functools.partial(gate_back_kernel, outer),
        grid_spec=pltpu.PrefetchScalarGridSpec(
            num_scalar_prefetch=1,
            grid=(count // 2,),
            in_specs=[
                blocks_of(depth),
                blocks_of(depth),
                blocks_of(lanes_v),
                blocks_of(lanes_v),
                blocks_of(lanes_v),
                blocks_of(LANES),
                full(gain.shape),
            ],
            out_specs=[
                blocks_of(lanes_v),
                blocks_of(lanes_v),
                full((1, lanes_v)),
                *[full(shape) for shape in blocks],
            ],
            scratch_shapes=[
                pltpu.VMEM((lanes_v, depth), F32),
                pltpu.VMEM((depth, lanes_v), F32),
            ],
        ),
        out_shape=[
            jax.ShapeDtypeStruct((total, lanes_v), F32),
            jax.ShapeDtypeStruct((total, lanes_v), BF),
            jax.ShapeDtypeStruct((1, lanes_v), F32),
            *[jax.ShapeDtypeStruct(shape, BF) for shape in blocks],
        ],
        compiler_params=params(),
        cost_estimate=cost(total, depth, lanes_v, 0.01),
    )(lengths, hid, cot, gate, gg, mixed, stats, gain)


def run_backward(starts, depth, xin, dtp, dmix, dgate, sin, wv, ws, wg, taps, heads, skip):
    count = starts.shape[0]
    lanes_v, lanes_x = skip.shape[1], taps.shape[1]
    total = xin.shape[0]
    per = STRETCH // HALO

    def back(width):
        return pl.BlockSpec((STRETCH, width), lambda i, *_: (count - 1 - i, 0))

    return pl.pallas_call(
        backward_kernel,
        grid_spec=pltpu.PrefetchScalarGridSpec(
            num_scalar_prefetch=1,
            grid=(count,),
            in_specs=[
                back(lanes_x),
                pl.BlockSpec(
                    (HALO, lanes_x), lambda i, *_: (jnp.maximum((count - 1 - i) * per - 1, 0), 0)
                ),
                back(LANES),
                back(lanes_v),
                back(lanes_v),
                pl.BlockSpec((1, N, lanes_v), lambda i, *_: (count - 1 - i, 0, 0)),
                full((depth, wv.shape[1])),
                full((depth, ws.shape[1])),
                full((depth, lanes_v)),
                full(taps.shape),
                full(heads.shape),
                full(skip.shape),
                full((LANES, lanes_v)),
                full((LANES, 2 * lanes_v)),
            ],
            out_specs=[
                back(depth),
                back(lanes_v),
                back(2 * N + LANES),
                full((8, lanes_x)),
                full((8, LANES)),
                full((1, lanes_v)),
            ],
            scratch_shapes=[
                pltpu.VMEM((N, lanes_v), F32),
                pltpu.VMEM((STRETCH + HALO, lanes_x), F32),
                pltpu.VMEM((STRETCH + HALO, lanes_x), F32),
                pltpu.VMEM((STRETCH, lanes_x), F32),
                pltpu.VMEM((STRETCH, STRETCH), F32),
                pltpu.VMEM((STRETCH, STRETCH), F32),
                pltpu.VMEM((2, STRETCH, STRETCH), F32),
                pltpu.VMEM((2, STRETCH, STRETCH), BF),
                pltpu.VMEM((LANES, STRETCH), F32),
                pltpu.VMEM((STRETCH, LANES), F32),
                pltpu.VMEM((STRETCH, 2 * lanes_v), F32),
                pltpu.VMEM((STRETCH, lanes_v), F32),
            ],
        ),
        out_shape=[
            jax.ShapeDtypeStruct((total, depth), BF),
            jax.ShapeDtypeStruct((total, lanes_v), BF),
            jax.ShapeDtypeStruct((total, 2 * N + LANES), BF),
            jax.ShapeDtypeStruct((8, lanes_x), F32),
            jax.ShapeDtypeStruct((8, LANES), F32),
            jax.ShapeDtypeStruct((1, lanes_v), F32),
        ],
        compiler_params=params(),
        cost_estimate=cost(total, depth, lanes_v, 0.01),
    )(starts, xin, xin, dtp, dmix, dgate, sin, wv, ws, wg, taps, heads, skip, *spreaders(lanes_v))


def relay_blocks(part, axis):
    count, place = lax.axis_size(axis), lax.axis_index(axis)
    got = []
    right, left = part, part
    for k in range(1, count):
        right = lax.ppermute(right, axis, [(i, i + 1) for i in range(count - 1)])
        left = lax.ppermute(left, axis, [(i + 1, i) for i in range(count - 1)])
        got.append((right, jnp.where(place >= k, place - k, count)))
        got.append((left, jnp.where(place + k < count, place + k, count)))
    return got


def rotation(block, axis, k):
    count = lax.axis_size(axis)
    return lax.ppermute(block, axis, [(i, (i + k) % count) for i in range(count)])


def direct_blocks(part, axis):
    count, place = lax.axis_size(axis), lax.axis_index(axis)
    return [(rotation(part, axis, k), lax.rem(place + count - k, count)) for k in range(1, count)]


def exchanged_sum(blocks, axis):
    total = blocks[0].astype(F32)
    for k in range(1, len(blocks)):
        total = total + rotation(blocks[k], axis, k).astype(F32)
    return total


def assembled(part, got, axis, after=None):
    count, place = lax.axis_size(axis), lax.axis_index(axis)
    rows = part.shape[0]
    start = (0,) * (part.ndim - 1)
    blocks = [part] + [block for block, _ in got]
    places = [place] + [at for _, at in got]
    if after is not None:
        blocks, _ = lax.optimization_barrier((blocks, after))
    whole = jnp.zeros(((count + 1) * rows, *part.shape[1:]), part.dtype)
    for block, at in zip(blocks, places):
        whole = lax.dynamic_update_slice(whole, block, (at * rows, *start))
    return whole


def rows_kernel(outer_h, gate, values, shared, weight, gain, grad_out, norm_out):
    inner, rows, lanes_v = gate.shape
    width = lanes_v // outer_h
    per = lanes_v // P_SIZE // outer_h
    total = jnp.zeros((rows, 1), F32)

    def put(low, part):
        grad_out[:, low : low + part.shape[1]] = part
        old = weight[:, low : low + part.shape[1]].astype(F32)
        return jnp.sum(old * part, axis=1, keepdims=True)

    for base, got in ((0, gate), (DI, values)):
        for f in range(inner):
            for z in range(outer_h):
                part = got[f, :, z * width : (z + 1) * width].astype(F32)
                total = total + put(base + (z * inner + f) * width, part)
    common = jnp.zeros((rows, 2 * N), F32)
    steps = jnp.zeros((rows, H), F32)
    source = lax.broadcasted_iota(jnp.int32, (LANES, H), 0)
    target = lax.broadcasted_iota(jnp.int32, (LANES, H), 1)
    for f in range(inner):
        common = common + shared[f, :, : 2 * N].astype(F32)
        spot = ((source // per) * inner + f) * per + source % per
        chosen = jnp.logical_and(spot == target, source < per * outer_h)
        steps = steps + mm(shared[f, :, 2 * N :], chosen.astype(F32).astype(BF))
    total = total + put(2 * DI, common) + put(2 * DI + 2 * N, steps)
    norm_out[...] = jnp.broadcast_to(total / gain[...], norm_out.shape)


def run_rows(outer_h, gate, values, shared, weight, gain):
    rows, width = weight.shape
    return pl.pallas_call(
        functools.partial(rows_kernel, outer_h),
        out_shape=[
            jax.ShapeDtypeStruct((rows, width), F32),
            jax.ShapeDtypeStruct((rows, LANES), F32),
        ],
        compiler_params=pltpu.CompilerParams(vmem_limit_bytes=VMEM_BYTES),
    )(gate, values, shared, weight, gain)


def body(
    hidden,
    out_cotangent,
    norm_gain,
    in_weight,
    conv_weight,
    conv_bias,
    step_bias,
    decay_log,
    skip_gain,
    gate_gain,
    out_weight,
    stretch_len,
    stretch_start,
):
    outer, inner = lax.axis_size("dp"), lax.axis_size("fsdp")
    place = lax.axis_index("fsdp")
    local_heads = H // inner
    lanes_v = local_heads * P_SIZE
    lanes_x = lanes_v + 2 * N
    rows_w = in_weight.shape[0]
    rows_o = out_weight.shape[0]
    depth = hidden.shape[1]
    strided = rows_o % P_SIZE == 0
    outer_h = outer if strided else 1

    def by_place(whole, axis, unit):
        shape = whole.shape
        cut = (*shape[:axis], outer_h, inner, local_heads // outer_h * unit, *shape[axis + 1 :])
        parts = jnp.moveaxis(whole.reshape(cut), axis + 1, 0)
        return parts.reshape(inner, *shape[:axis], local_heads * unit, *shape[axis + 1 :])

    def from_places(parts, axis, unit):
        shape = parts.shape[1:]
        cut = (inner, *shape[:axis], outer_h, local_heads // outer_h * unit, *shape[axis + 1 :])
        whole = jnp.moveaxis(parts.reshape(cut), 0, axis + 1)
        return whole.reshape(*shape[:axis], H * unit, *shape[axis + 1 :])

    def own(whole, axis, unit):
        return lax.dynamic_index_in_dim(by_place(whole, axis, unit), place, 0, False)

    wide = CONV - 2 * N
    hid = lax.all_gather(hidden, "fsdp", axis=0, tiled=True)

    shared_width = 2 * N + H
    gains = (norm_gain, gate_gain)
    small = (
        conv_weight,
        conv_bias,
        step_bias,
        decay_log,
        skip_gain,
        stretch_len.astype(BF),
        stretch_start.astype(BF),
    )

    def in_rows(arrays):
        flat = jnp.concatenate([a.reshape(-1) for a in arrays])
        rows = -(-flat.shape[0] // shared_width)
        return jnp.pad(flat, (0, rows * shared_width - flat.shape[0])).reshape(rows, shared_width)

    gain_rows, small_rows = in_rows(gains), in_rows(small)
    block = jnp.concatenate([in_weight[:, DI + wide :], gain_rows, small_rows], axis=0)
    height = -(-block.shape[0] // 16) * 16
    block = jnp.pad(block, ((0, height - block.shape[0]), (0, 0)))
    along = assembled(block, direct_blocks(block, "dp"), "dp")[: outer * height]
    along = jnp.broadcast_to(along[None], (inner, *along.shape))
    common = lax.all_to_all(along, "fsdp", 0, 0, tiled=True)
    common = common.reshape(inner, outer, height, shared_width)

    wv = lax.all_to_all(by_place(in_weight[:, DI : DI + wide], 1, P_SIZE), "fsdp", 0, 0, tiled=True)
    wv = wv.reshape(inner * rows_w, lanes_v)
    wg = lax.all_to_all(by_place(in_weight[:, :DI], 1, P_SIZE), "fsdp", 0, 0, tiled=True)
    wg = wg.reshape(inner * rows_w, lanes_v)
    cot, _ = lax.optimization_barrier((out_cotangent, wv))
    cot = lax.all_gather(cot, "fsdp", axis=0, tiled=True)
    if strided:
        ow_got = direct_blocks(out_weight, "dp")
        wv, ow_got = lax.optimization_barrier((wv, ow_got))
    wv_got = relay_blocks(wv, "dp")
    late = max(len(wv_got) - 2, 0)
    wg, _ = lax.optimization_barrier((wg, wv_got[late : late + 2]))
    wg_got = direct_blocks(wg, "dp")
    wv = assembled(wv, wv_got, "dp")

    rows_all = jnp.swapaxes(common[:, :, :rows_w], 0, 1).reshape(depth, shared_width)
    head_of = np.arange(H).reshape(outer_h, inner, local_heads // outer_h)
    order = jnp.asarray(np.swapaxes(head_of, 0, 1).reshape(inner, local_heads))
    mine = lax.dynamic_index_in_dim(order, place, 0, False)
    pick = (jnp.arange(H)[:, None] == mine[None, :]).astype(BF)
    pick = jnp.pad(pick, ((0, 0), (0, LANES - local_heads)))
    ws = jnp.concatenate([rows_all[:, : 2 * N], mm(rows_all[:, 2 * N :], pick).astype(BF)], axis=1)

    def out_of_rows(rows, arrays):
        flat = rows.reshape(*rows.shape[:-2], -1).astype(F32)
        parts, low = [], 0
        for a in arrays:
            size = math.prod(a.shape)
            parts.append(flat[..., low : low + size])
            low += size
        return parts

    at = rows_w + gain_rows.shape[0]
    norm_part, gate_part = out_of_rows(common[:, :, rows_w:at], gains)
    norm_full = jnp.swapaxes(norm_part, 0, 1).reshape(-1)
    gate_full = jnp.swapaxes(gate_part, 0, 1).reshape(-1)
    same = lax.dynamic_index_in_dim(common, lax.axis_index("dp"), 1, False)
    pieces = out_of_rows(same[:, at : at + small_rows.shape[0]], small)
    conv_full = pieces[0].reshape(CONV, TAPS)
    bias_full = pieces[1].reshape(CONV)
    per_head = [own(a.reshape(H), 0, 1) for a in pieces[2:5]]
    lengths = pieces[5].reshape(-1).astype(jnp.int32)
    starts = pieces[6].reshape(-1).astype(jnp.int32)

    gain_own = own(gate_full, 0, P_SIZE)[None, :]
    taps_all = jnp.concatenate([conv_full.T, bias_full[None, :]], axis=0)
    taps = jnp.concatenate([own(taps_all[:, :wide], 1, P_SIZE), taps_all[:, wide:]], axis=1)
    taps = jnp.pad(taps, ((0, 8 - (TAPS + 1)), (0, 0)))
    heads = jnp.stack([per_head[0], -jnp.exp(per_head[1])])
    heads = jnp.pad(heads, ((0, 6), (0, LANES - local_heads)))
    skip = jnp.repeat(per_head[2], P_SIZE)[None, :]

    u, xin, dtp, mixed, sin = run_forward(
        starts, hid, norm_full[None, :], wv, ws, taps, heads, skip
    )
    wg = assembled(wg, wg_got, "dp", mixed)
    if strided:
        ow = assembled(out_weight, ow_got, "dp")
    else:
        ow = own(lax.all_gather(out_weight, ("dp", "fsdp"), axis=0, tiled=True), 0, P_SIZE)

    branch, gate, squares = run_gate(u, wg, ow, mixed, gain_own)
    gg, along = run_pull(lengths, cot, ow, gate, mixed, gain_own)
    stats = lax.psum(jnp.concatenate([squares[0:1], along[0:1]], axis=0), "fsdp")
    r = lax.rsqrt(stats[0] / DI + EPSILON)
    m = r * stats[1] / DI
    table = jnp.pad(jnp.stack([r, m], axis=1), ((0, 0), (0, LANES - 2)))
    branch = lax.psum_scatter(branch, "fsdp", scatter_dimension=0, tiled=True)

    dmix, dgate, ggg, *blocks = run_gate_back(
        lengths, lax.axis_index("dp"), outer, strided, u, cot, gate, gg, mixed, table, gain_own
    )
    weight_got = [blocks[0]] + [rotation(blocks[k], "dp", k) for k in range(1, outer)]

    def to_rows(mine):
        mine = mine.reshape(inner, rows_w, mine.shape[1])
        return lax.all_to_all(mine, "fsdp", 0, 0, tiled=True)


    f, gpv, gps, conv_sums, head_sums, skip_sums = run_backward(
        starts, depth, xin, dtp, dmix, dgate, sin, wv, ws, wg, taps, heads, skip
    )
    f, branch, weight_got = lax.optimization_barrier((f, branch, weight_got))
    f = lax.psum_scatter(f, "fsdp", scatter_dimension=0, tiled=True)
    def by_rows(grad):
        rows = depth // outer
        place_z = lax.axis_index("dp")
        blocks = [
            lax.dynamic_slice_in_dim(grad, lax.rem(place_z + k, outer) * rows, rows, 0)
            for k in range(outer)
        ]
        return blocks

    def passed_on(blocks):
        return blocks[:1] + [rotation(blocks[k], "dp", k) for k in range(1, outer)]

    def row_sum(got):
        return sum(a.astype(F32) for a in got).astype(BF)

    weight_sum = sum(a.astype(F32) for a in weight_got)
    iwg_gate = weight_sum[: depth // outer].astype(BF)
    if strided:
        out_weight_grad = weight_sum[depth // outer :].reshape(-1, rows_o, lanes_v)
        out_weight_grad = jnp.swapaxes(out_weight_grad, 0, 1).reshape(rows_o, depth)
    else:
        rows = lax.dynamic_update_slice_in_dim(
            jnp.zeros((DI, depth), BF), blocks[outer], place * lanes_v, 0
        )
        out_weight_grad = lax.psum_scatter(rows, ("dp", "fsdp"), scatter_dimension=0, tiled=True)
        out_weight_grad = out_weight_grad.astype(F32)
    iwg_values = by_rows(mm_tn(u, gpv).astype(BF))
    gate_rows = to_rows(iwg_gate)
    iwg_values = passed_on(iwg_values)
    conv_sums, head_sums, skip_sums, iwg_values[0] = lax.optimization_barrier(
        (conv_sums, head_sums, skip_sums, iwg_values[0])
    )
    skip_part = jnp.sum(skip_sums.reshape(local_heads, P_SIZE), axis=1)
    parts = (
        conv_sums[: TAPS + 1, :lanes_v].reshape(-1),
        conv_sums[: TAPS + 1, lanes_v:].reshape(-1),
        head_sums[0:2, :local_heads].reshape(-1),
        skip_part,
        ggg.reshape(-1),
    )
    counts = [a.shape[0] for a in parts]
    bundle = jnp.concatenate(parts)
    bundle = jnp.pad(bundle, (0, -bundle.shape[0] % (8 * LANES))).reshape(-1, LANES)
    if outer > 1:
        gps, gate_rows, iwg_values[1] = lax.optimization_barrier((gps, gate_rows, iwg_values[1]))
    iwg_shared = passed_on(by_rows(mm_tn(u, gps).astype(BF)))
    value_rows, shared_rows = to_rows(row_sum(iwg_values)), to_rows(row_sum(iwg_shared))
    in_weight_grad, norm_rows = run_rows(
        outer_h, gate_rows, value_rows, shared_rows, in_weight, norm_gain.astype(F32)[:, None]
    )
    norm_gain_grad = norm_rows[:, 0]

    total = hidden.shape[0]
    r_own = lax.dynamic_slice_in_dim(r, place * total, total, 0)
    len_here = jnp.repeat(stretch_len, STRETCH)
    alive = (jnp.arange(total) % STRETCH < len_here).astype(F32)
    rows_float = hidden.astype(F32)
    rs_own = lax.rsqrt(jnp.mean(rows_float * rows_float, axis=1, keepdims=True) + EPSILON)
    block_out = (rows_float + (alive * r_own)[:, None] * branch.astype(F32)).astype(BF)
    unit = rows_float * rs_own
    scaled = f.astype(F32) * norm_full[None, :]
    hidden_grad = out_cotangent.astype(F32) + rs_own * (
        scaled - unit * jnp.mean(scaled * unit, axis=1, keepdims=True)
    )

    bundle = exchanged_sum([bundle] * outer, "dp")
    bundle = jnp.broadcast_to(bundle[None], (inner, *bundle.shape))
    bundle = lax.all_to_all(bundle, "fsdp", 0, 0, tiled=True).reshape(inner, -1)
    stops = [sum(counts[: i + 1]) for i in range(len(counts))]
    cuts = [bundle[:, stop - size : stop] for stop, size in zip(stops, counts)]
    conv_values = from_places(cuts[0].reshape(inner, TAPS + 1, lanes_v), 1, P_SIZE)
    conv_shared = jnp.sum(cuts[1].reshape(inner, TAPS + 1, 2 * N), axis=0)
    conv_all = jnp.concatenate([conv_values, conv_shared], axis=1)
    conv_mine = lax.dynamic_slice_in_dim(
        conv_all, place * conv_weight.shape[0], conv_weight.shape[0], 1
    )
    conv_weight_grad = conv_mine[:TAPS].T
    conv_bias_grad = conv_mine[TAPS]

    def heads_mine(parts_h, size):
        whole = from_places(parts_h, 0, 1)
        return lax.dynamic_slice_in_dim(whole, place * size, size, 0)

    pair_sums = cuts[2].reshape(inner, 2, local_heads)
    step_bias_grad = heads_mine(pair_sums[:, 0], step_bias.shape[0])
    decay_log_grad = heads_mine(pair_sums[:, 1], decay_log.shape[0])
    skip_gain_grad = heads_mine(cuts[3], skip_gain.shape[0])
    gate_all = from_places(cuts[4], 0, P_SIZE)
    flat = lax.axis_index("dp") * inner + place
    gate_gain_grad = lax.dynamic_slice_in_dim(
        gate_all, flat * gate_gain.shape[0], gate_gain.shape[0], 0
    )
    return (
        block_out,
        hidden_grad,
        norm_gain_grad,
        in_weight_grad,
        conv_weight_grad,
        conv_bias_grad,
        step_bias_grad,
        decay_log_grad,
        skip_gain_grad,
        gate_gain_grad,
        out_weight_grad,
    )


def solution(mesh):
    both = P(("dp", "fsdp"))
    rows = P(("dp", "fsdp"), None)
    one = P("fsdp")
    return jax.shard_map(
        body,
        mesh=mesh,
        in_specs=(rows, rows, both, rows, P("fsdp", None), one, one, one, one, both, rows, both, both),
        out_specs=(rows, rows, both, rows, P("fsdp", None), one, one, one, one, both, rows),
        check_vma=False,
    )
```
